512 devices in a mesh: req: 64 (over z, x), tp: 8 (over y, core).
Axes of the slice: x: 4, y: 4, z: 16, core: 2. Of those that a mesh axis runs over, the one named last changes fastest.
Arguments:
- tokens: bfloat16 [32768, 1024], P('req', 'tp'), may hold values from -24 to 24
- qkv_weight: bfloat16 [1024, 3, 1024], P(None, None, 'tp'), may hold values from -0.1875 to 0.1875
- out_weight: bfloat16 [1024, 1024], P('tp'), may hold values from -0.1875 to 0.1875
- attn_gain: float32 [1024], replicated, may hold values from 0.1 to 1.9
- attn_shift: float32 [1024], replicated, may hold values from -3 to 3
- up_weight: bfloat16 [1024, 4096], P(None, 'tp'), may hold values from -0.1875 to 0.1875
- down_weight: bfloat16 [4096, 1024], P('tp'), may hold values from -0.09375 to 0.09375
- mlp_gain: float32 [1024], replicated, may hold values from 0.1 to 1.9
- mlp_shift: float32 [1024], replicated, may hold values from -3 to 3
- prefix_cache: bfloat16 [128, 256, 2, 1024], P('req', None, None, 'tp'), may hold values from -6 to 6
- earlier_cache: bfloat16 [2048, 16, 2, 1024], P('req', None, None, 'tp'), may hold values from -6 to 6
- suffix_len: int32 [4096], P('req'), may hold values from 1 to 15, as said below
- prefix_id: int32 [4096], P('req'), may hold values from 0 to 127, as said below
- earlier_slot: int32 [4096], P('req'), may hold values from -1 to 2047, as said below
Outputs:
- encoded: bfloat16 [32768, 1024], P('req', 'tp')
The draws below stay inside these ranges and needn't reach their ends.
Inputs may be any that keep to these rules, and one draw needn't show every extreme that they name: `suffix_len`: requests 2g and 2g+1 of a device together fill its tokens g * 16 to (g + 1) * 16 - 1. `prefix_id`: both requests of a pair read prefix caches held by the same index of req, and the 32 pairs of a device read caches held by 32 different indices. `earlier_slot`: exactly one request of each pair continues an earlier cache, every row of earlier_cache is continued by exactly one request, and the 32 pairs of a device continue caches held by 32 different indices of req.
All inputs are finite; a program needn't handle non-finite values.
Results may differ from the reference program's by a relative error of at most 0.0049.
The reference program's roundings to bfloat16 on the way count: a program that leaves them out, or rounds other values in their place, can miss the bound.
Values may be sent and summed in bfloat16 or wider, within the bound.
No kernel may reach another device: no remote copies, remote signals or barrier semaphores. Data moves between devices by JAX's collectives and lax.ppermute only.
A program may use at most 64 MiB of HBM per device.

```python
import jax
import jax.numpy as jnp
from jax import lax

D = 1024
H = 16
HD = 64
FF = 4096
TOK_DEV = 512
P_LEN = 256
PRE_DEV = 2
E_LEN = 16
GROUPS = 32
REQ_DEV = 64
QCAP = 16
ERL_DEV = 32
TOKENS = 32768
PREFIXES = 128
EARLIER = 2048
N_REQ = 64


def draw_tokens(key, part):
    base_key = jax.random.fold_in(key, 11)
    drawn = jnp.clip(jax.random.normal(base_key, (TOKENS, D), jnp.float32), -4.0, 4.0)
    return drawn.astype(jnp.bfloat16)


def permute_rest(sub_key):
    return jax.random.permutation(sub_key, REQ_DEV - 1)


def permute_groups(sub_key):
    return jax.random.permutation(sub_key, GROUPS)


def plan_requests(key):
    base_key = jax.random.fold_in(key, 5)
    devices = REQ_DEV
    cut_points = jax.random.randint(jax.random.fold_in(base_key, 0), (devices, GROUPS), 1, QCAP)
    cut_points = cut_points.at[:, -1].set(QCAP - 1)
    cut_points = cut_points.at[:, 0].set(1)
    lengths = jnp.stack([cut_points, QCAP - cut_points], axis=-1).reshape(devices * REQ_DEV)
    hot_owner = jax.random.randint(jax.random.fold_in(base_key, 1), (), 0, devices)
    others = jax.vmap(permute_rest)(jax.random.split(jax.random.fold_in(base_key, 2), devices))
    chosen = jnp.concatenate([jnp.zeros((devices, 1), jnp.int32), others[:, :GROUPS - 1].astype(jnp.int32) + 1], axis=1)
    group_order = jax.vmap(permute_groups)(jax.random.split(jax.random.fold_in(base_key, 3), devices))
    chosen = jnp.take_along_axis(chosen, group_order.astype(jnp.int32), axis=1)
    owners = (hot_owner + chosen) % devices
    within = jax.random.randint(jax.random.fold_in(base_key, 4), (devices, GROUPS, 2), 0, PRE_DEV)
    prefix = (owners[:, :, None] * PRE_DEV + within).reshape(devices * REQ_DEV)
    shifts = jax.random.permutation(jax.random.fold_in(base_key, 5), devices)[:GROUPS].astype(jnp.int32)
    slot_index = jax.vmap(permute_groups)(jax.random.split(jax.random.fold_in(base_key, 6), devices))
    slot_index = slot_index.astype(jnp.int32)
    erl_owner = (jnp.arange(devices, dtype=jnp.int32)[:, None] + shifts[slot_index]) % devices
    slot_value = erl_owner * ERL_DEV + slot_index
    side_pick = jax.random.randint(jax.random.fold_in(base_key, 7), (devices, GROUPS), 0, 2)
    earlier = jnp.where(side_pick[:, :, None] == jnp.arange(2), slot_value[:, :, None], -1)
    earlier = earlier.reshape(devices * REQ_DEV)
    return (lengths.astype(jnp.int32), prefix.astype(jnp.int32), earlier.astype(jnp.int32))


def draw_suffix_len(key, part):
    return plan_requests(key)[0]


def draw_prefix_id(key, part):
    return plan_requests(key)[1]


def draw_earlier_slot(key, part):
    return plan_requests(key)[2]


def level_of(key, shape, cuts, least, top_value):
    gain, own = 1.0, jax.random.fold_in(key, 6)
    for position, parts in cuts:
        steps = jnp.exp(jax.random.uniform(jax.random.fold_in(own, position), (parts,), jnp.float32, least / len(cuts), top_value / len(cuts)))
        gain = gain * jnp.repeat(steps, shape[position] // parts).reshape([-1 if axis == position else 1 for axis in range(len(shape))])
    return gain


def scatter_about(stream_key, dims, spread, bound, shards=(), kind=jnp.bfloat16):
    factor_of = level_of(stream_key, dims, shards, -0.22, 0.18) if shards else 1.0
    array = jax.random.normal(stream_key, dims, jnp.float32) * spread * factor_of
    return jnp.minimum(jnp.maximum(array, -bound), bound).astype(kind)


def setup_inputs(seed: int = 0) -> dict:
    arg_keys = jax.random.split(jax.random.key(seed), 15)
    return {
        "tokens": draw_tokens(jax.random.fold_in(arg_keys[14], 71), 0),
        "qkv_weight": scatter_about(arg_keys[1], (D, 3, D), D ** -0.5, 0.1875, ((2, 8),)),
        "out_weight": scatter_about(arg_keys[2], (D, D), D ** -0.5, 0.1875, ((0, 8),)),
        "attn_gain": jnp.clip(1.0 + 0.18 * jax.random.normal(arg_keys[3], (D,), jnp.float32), 0.1, 1.9),
        "attn_shift": scatter_about(arg_keys[4], (D,), 0.5, 3.0, (), jnp.float32),
        "up_weight": scatter_about(arg_keys[5], (D, FF), D ** -0.5, 0.1875, ((1, 8),)),
        "down_weight": scatter_about(arg_keys[6], (FF, D), FF ** -0.5, 0.09375, ((0, 8),)),
        "mlp_gain": jnp.clip(1.0 + 0.18 * jax.random.normal(arg_keys[7], (D,), jnp.float32), 0.1, 1.9),
        "mlp_shift": scatter_about(arg_keys[8], (D,), 0.5, 3.0, (), jnp.float32),
        "prefix_cache": scatter_about(arg_keys[9], (PREFIXES, P_LEN, 2, D), 1.0, 6.0, ((0, 64), (3, 8))),
        "earlier_cache": scatter_about(arg_keys[10], (EARLIER, E_LEN, 2, D), 1.0, 6.0, ((0, 64), (3, 8))),
        "suffix_len": draw_suffix_len(jax.random.fold_in(arg_keys[14], 71), 0),
        "prefix_id": draw_prefix_id(jax.random.fold_in(arg_keys[14], 71), 0),
        "earlier_slot": draw_earlier_slot(jax.random.fold_in(arg_keys[14], 71), 0),
    }


scale_qk = 0.125
neg_fill = -1e+30
epsilon = 1e-05

def partial_attend(scores, allowed):
    masked = jnp.where(allowed, scores, jnp.float32(neg_fill))
    row_max = lax.optimization_barrier(jnp.max(masked, axis=-1, keepdims=True))
    weights = jnp.exp(masked - row_max)
    return (row_max[..., 0], lax.optimization_barrier(jnp.sum(weights, axis=-1)), weights.astype(jnp.bfloat16))

def norm_rows(hidden, scale_vec, shift_vec):
    row_mean = lax.optimization_barrier(jnp.mean(hidden, axis=-1, keepdims=True))
    centred = hidden - row_mean
    row_var = lax.optimization_barrier(jnp.mean(centred * centred, axis=-1, keepdims=True))
    return centred * lax.rsqrt(row_var + epsilon) * scale_vec + shift_vec

def device_attention(device_item, prefix_cache, earlier_cache):
    qkv_rows, lengths, prefix, earlier = device_item
    qkv_rows = qkv_rows.reshape(GROUPS, QCAP, 3, H, HD).astype(jnp.float32)
    query_heads = qkv_rows[:, :, 0]
    key_heads = qkv_rows[:, :, 1]
    value_heads = qkv_rows[:, :, 2]
    length_pairs = lengths.reshape(GROUPS, 2)
    in_first = jnp.arange(QCAP)[None, :] < length_pairs[:, :1]
    causal = (jnp.arange(QCAP)[:, None] >= jnp.arange(QCAP)[None, :])[None, :, None, :]
    same_req = (in_first[:, :, None] == in_first[:, None, :])[:, :, None, :] & causal
    scores = jnp.einsum('gqhd,gkhd->gqhk', query_heads, key_heads) * scale_qk
    own_max, own_total, own_weights = partial_attend(scores, same_req)
    own_out = jnp.einsum('gqhk,gkhd->gqhd', own_weights.astype(jnp.float32), value_heads)
    pair_cache = prefix_cache[prefix].astype(jnp.float32).reshape(GROUPS, 2, P_LEN, 2, H, HD)
    pre_keys = pair_cache[:, :, :, 0]
    pre_values = pair_cache[:, :, :, 1]
    scores = jnp.einsum('gqhd,grkhd->gqhrk', query_heads, pre_keys) * scale_qk
    which_req = jnp.where(in_first, 0, 1)
    allowed = jnp.broadcast_to(which_req[:, :, None, None, None] == jnp.arange(2)[:, None], scores.shape)
    pre_max, pre_total, pre_weights = partial_attend(scores.reshape(GROUPS, QCAP, H, 2 * P_LEN), allowed.reshape(GROUPS, QCAP, H, 2 * P_LEN))
    pre_weights = pre_weights.astype(jnp.float32).reshape(GROUPS, QCAP, H, 2, P_LEN)
    pre_out = jnp.einsum('gqhrk,grkhd->gqhd', pre_weights, pre_values)
    slot_pairs = earlier.reshape(GROUPS, 2)
    slot_group = jnp.maximum(slot_pairs[:, 0], slot_pairs[:, 1])
    block_rows = earlier_cache[slot_group].astype(jnp.float32).reshape(GROUPS, E_LEN, 2, H, HD)
    carry_on = jnp.where(in_first, slot_pairs[:, :1] >= 0, slot_pairs[:, 1:] >= 0)
    scores = jnp.einsum('gqhd,gkhd->gqhk', query_heads, block_rows[:, :, 0]) * scale_qk
    erl_max, erl_total, erl_weights = partial_attend(scores, carry_on[:, :, None, None])
    erl_out = jnp.einsum('gqhk,gkhd->gqhd', erl_weights.astype(jnp.float32), block_rows[:, :, 1])
    on_rows = carry_on[:, :, None]
    erl_max = jnp.where(on_rows, erl_max, jnp.float32(neg_fill))
    erl_total = jnp.where(on_rows, erl_total, jnp.float32(0.0))
    erl_out = jnp.where(on_rows[..., None], erl_out, jnp.float32(0.0))
    merged_max = jnp.maximum(jnp.maximum(own_max, pre_max), erl_max)
    own_scale = jnp.exp(own_max - merged_max)
    pre_scale = jnp.exp(pre_max - merged_max)
    erl_scale = jnp.exp(erl_max - merged_max)
    merged_total = own_total * own_scale + pre_total * pre_scale + erl_total * erl_scale
    mixed = (own_out * own_scale[..., None] + pre_out * pre_scale[..., None] + erl_out * erl_scale[..., None]) / merged_total[..., None]
    return mixed.reshape(TOK_DEV, D).astype(jnp.bfloat16)

def reference(tokens, qkv_weight, out_weight, attn_gain, attn_shift, up_weight, down_weight, mlp_gain, mlp_shift, prefix_cache, earlier_cache, suffix_len, prefix_id, earlier_slot):
    qkv_rows = jnp.dot(tokens, qkv_weight.reshape(D, 3 * D), preferred_element_type=jnp.float32).astype(jnp.bfloat16)
    device_items = (qkv_rows.reshape(N_REQ, TOK_DEV, 3 * D), suffix_len.reshape(N_REQ, REQ_DEV), prefix_id.reshape(N_REQ, REQ_DEV), earlier_slot.reshape(N_REQ, REQ_DEV))

    def per_device(device_item):
        return device_attention(device_item, prefix_cache, earlier_cache)
    attended = lax.map(per_device, device_items).reshape(TOKENS, D)
    projected = jnp.dot(attended, out_weight, preferred_element_type=jnp.float32)
    normed = norm_rows(tokens.astype(jnp.float32) + projected, attn_gain, attn_shift).astype(jnp.bfloat16)
    inner = jax.nn.gelu(jnp.dot(normed, up_weight, preferred_element_type=jnp.float32), approximate=False).astype(jnp.bfloat16)
    lowered = jnp.dot(inner, down_weight, preferred_element_type=jnp.float32)
    return norm_rows(normed.astype(jnp.float32) + lowered, mlp_gain, mlp_shift).astype(jnp.bfloat16)
```

```python
import jax
import jax.numpy as jnp
from jax import lax
from jax.experimental import pallas as pl
from jax.experimental.pallas import tpu as pltpu
from jax.sharding import Mesh, PartitionSpec as P

HD = 64
REQ = ("z", "x")
TP = ("y", "c")
SCALE = 0.125
NEG = -1e30
EPS = 1e-05
bf16 = jnp.bfloat16
f32 = jnp.float32

VM = pl.BlockSpec(memory_space=pltpu.VMEM)
SM = pl.BlockSpec(memory_space=pltpu.SMEM)


def iota(shape, axis):
    return lax.broadcasted_iota(jnp.int32, shape, axis)


def head_mask(x, h):
    lane = iota(x.shape, len(x.shape) - 1)
    return jnp.where((lane >= HD) == (h == 1), x, jnp.zeros_like(x))


def dot_t(a, b):
    return lax.dot_general(a, b, (((1,), (1,)), ((), ())), preferred_element_type=f32)


def dot(a, b):
    return jnp.dot(a, b, preferred_element_type=f32)


def softmax_parts(scores, allowed):
    masked = scores if allowed is None else jnp.where(allowed, scores, NEG)
    top = jnp.max(masked, axis=-1, keepdims=True)
    weights = jnp.exp(masked - top)
    total = jnp.sum(weights, axis=-1, keepdims=True)
    return weights.astype(bf16), 1.0 / total, top + jnp.log(total)


def qkv_kernel(pairs, own_ref, far_ref, w_ref, info_ref, send_ref, qkv_ref):
    slots = send_ref.shape[0]
    row = iota((16, 128), 0)
    for b in range(slots // 8):
        rows = pl.ds(8 * b, 8)
        send_ref[rows, 0:16, :] = jnp.zeros((8, 16, 128), bf16)
        base = jnp.broadcast_to(info_ref[rows, :][:, None, :], (8, 16, 128))
        send_ref[rows, 16:32, :] = jnp.where(row[None] == 15, base, 0.0).astype(bf16)

    def block(b, carry):
        r0 = pl.multiple_of(b * 128, 128)
        rows = pl.ds(r0, 128)
        parts = [own_ref[i, rows, :] for i in range(4)] + [far_ref[i, rows, :] for i in range(4)]
        out = dot(jnp.concatenate(parts, axis=1), w_ref[...])
        qkv_ref[rows, :] = out.astype(bf16)
        q = out[:, :128].astype(bf16)
        for p in range(8):
            g = b * 8 + p
            qp = q[16 * p : 16 * p + 16]
            send_ref[pairs[0, g], 0:16, :] = qp
            qf = qp.astype(f32)
            moved = jnp.where(pairs[2, g] == 1, pltpu.roll(qf, 15, 0), qf)
            slot = pairs[1, g]
            held = send_ref[slot, 16:32, :].astype(f32)
            send_ref[slot, 16:32, :] = jnp.where(row == 15, held, moved).astype(bf16)
        return carry

    lax.fori_loop(0, 4, block, 0)


def own_kernel(qkv_ref, len_ref, out_ref, lse_ref):
    r = iota((128, 128), 0)
    c = iota((128, 128), 1)

    def block(b, carry):
        rows = pl.ds(pl.multiple_of(b * 128, 128), 128)
        q = qkv_ref[rows, 0:128]
        k = qkv_ref[rows, 128:256]
        v = qkv_ref[rows, 256:384]
        span = len_ref[rows, :]
        same = ((r // 16) == (c // 16)) & (c <= r) & (((r % 16) < span) == ((c % 16) < span))
        res = []
        for h in range(2):
            w, inv, lse = softmax_parts(dot_t(head_mask(q, h), k) * SCALE, same)
            res.append((dot(w, v) * inv, jnp.broadcast_to(lse, (128, 128))))
        out_ref[rows, :] = head_mask(res[0][0], 0) + head_mask(res[1][0], 1)
        lse_ref[rows, :] = head_mask(res[0][1], 0) + head_mask(res[1][1], 1)
        return carry

    lax.fori_loop(0, 4, block, 0)


def owner_kernel(got_ref, pk_ref, pv_ref, ek_ref, ev_ref, ret_ref):
    sub = iota((8, 16, 128), 1)
    lane = iota((8, 16, 128), 2)
    key_row = iota((128, 512), 1) // 16

    def block(b, carry):
        slots = pl.ds(b * 8, 8)
        q_pre = got_ref[slots, 0:16, :].reshape(128, 128)
        erl_in = got_ref[slots, 16:32, :]
        q_erl = erl_in.reshape(128, 128)
        info = jnp.broadcast_to(erl_in.astype(f32)[:, 15:16, :], (8, 16, 128))
        pick = jnp.sum(jnp.where(lane == sub, info, 0.0), axis=-1, keepdims=True)
        pick = pick.reshape(128, 1) > 0.5
        row_j = jnp.sum(jnp.where(lane == 16, info, 0.0), axis=-1, keepdims=True)
        row_j = row_j.reshape(128, 1).astype(jnp.int32) - 1
        mine = key_row == row_j
        pre, erl, stats = [], [], []
        for h in range(2):
            q = head_mask(q_pre, h)
            s = jnp.where(pick, dot_t(q, pk_ref[1]), dot_t(q, pk_ref[0])) * SCALE
            w, inv, lse = softmax_parts(s, None)
            none = jnp.zeros_like(w)
            o = dot(jnp.where(pick, none, w), pv_ref[0]) + dot(jnp.where(pick, w, none), pv_ref[1])
            pre.append(o * inv)
            stats.append(lse)
        for h in range(2):
            w, inv, lse = softmax_parts(dot_t(head_mask(q_erl, h), ek_ref[...]) * SCALE, mine)
            erl.append(dot(w, ev_ref[...]) * inv)
            stats.append(lse)
        ret_ref[slots, 0:16, :] = (
            (head_mask(pre[0], 0) + head_mask(pre[1], 1)).astype(bf16).reshape(8, 16, 128)
        )
        erl_out = (head_mask(erl[0], 0) + head_mask(erl[1], 1)).reshape(8, 16, 128)
        group = lane // 16
        spread = jnp.zeros((8, 16, 128), f32)
        for n in range(4):
            want = ((group // 4) * 2 + group % 2) == n
            spread = jnp.where(want, stats[n].reshape(8, 16, 1), spread)
        line = jnp.sum(jnp.where(lane % 16 == sub, spread, 0.0), axis=1, keepdims=True)
        high = line.astype(bf16).astype(f32)
        line = jnp.where((group[:, 0:1] // 2) % 2 == 1, line - high, high)
        ret_ref[slots, 16:32, :] = jnp.where(
            sub == 15, jnp.broadcast_to(line, (8, 16, 128)), erl_out
        ).astype(bf16)
        return carry

    lax.fori_loop(0, 8, block, 0)


def merge_kernel(
    pairs, ret_ref, own_ref, lse_ref, out_ref, pre_o, pre_s, erl_o, erl_s, erl_on
):
    row = iota((16, 128), 0)
    lane = iota((16, 128), 1)
    diag = (lane % 16) == row

    def block(b, carry):
        for p in range(8):
            g = b * 8 + p
            rows = pl.ds(pl.multiple_of(b * 128, 128) + 16 * p, 16)
            slot, slot_e, second, span = pairs[0, g], pairs[1, g], pairs[2, g], pairs[3, g]
            pre_o[rows, :] = ret_ref[slot, 0:16, :].astype(f32)
            line = jnp.broadcast_to(ret_ref[slot, 16:32, :].astype(f32)[15:16, :], (16, 128))
            pre_s[rows, :] = jnp.where(diag & (lane < 64), line, 0.0)
            part = ret_ref[slot_e, 16:32, :].astype(f32)
            line = jnp.broadcast_to(part[15:16, :], (16, 128))
            stat = jnp.where(diag & (lane >= 64), line, 0.0)
            late = second == 1
            erl_o[rows, :] = jnp.where(late, pltpu.roll(part, 1, 0), part)
            erl_s[rows, :] = jnp.where(late, pltpu.roll(stat, 1, 0), stat)
            erl_on[rows, :] = ((row < span) == jnp.logical_not(late)).astype(f32)
        rows = pl.ds(pl.multiple_of(b * 128, 128), 128)
        a = iota((128, 128), 0)
        c = iota((128, 128), 1)
        pick = (((a // 16) % 2) == (c // 64)).astype(bf16)
        l_pre = dot(pre_s[rows, :].astype(bf16), pick)
        l_erl = dot(erl_s[rows, :].astype(bf16), pick)
        on = erl_on[rows, :] > 0.5
        l_erl = jnp.where(on, l_erl, NEG)
        l_own = lse_ref[rows, :]
        top = jnp.maximum(jnp.maximum(l_own, l_pre), l_erl)
        w_own = jnp.exp(l_own - top)
        w_pre = jnp.exp(l_pre - top)
        w_erl = jnp.exp(l_erl - top)
        mixed = w_own * own_ref[rows, :] + w_pre * pre_o[rows, :]
        mixed = mixed + w_erl * jnp.where(on, erl_o[rows, :], 0.0)
        out_ref[rows, :] = (mixed / (w_own + w_pre + w_erl)).astype(bf16)
        return carry

    lax.fori_loop(0, 4, block, 0)


def norm_rows(hidden, gain, shift):
    mean = jnp.mean(hidden, axis=-1, keepdims=True)
    centred = hidden - mean
    var = jnp.mean(centred * centred, axis=-1, keepdims=True)
    return centred * lax.rsqrt(var + EPS) * gain + shift


def tail_kernel(
    att_ref, tok_ref, w_out, ag_ref, as_ref, mg_ref, ms_ref, up_ref, down_ref, out_ref, normed, acc
):
    t = pl.program_id(0)

    @pl.when(t == 0)
    def _():
        att = jnp.concatenate([att_ref[i] for i in range(8)], axis=1)
        proj = [
            dot(att, w_out[:, 128 * n : 128 * n + 128, :].reshape(1024, 512)) for n in range(2)
        ]
        hidden = tok_ref[...].astype(f32) + jnp.concatenate(proj, axis=1)
        normed[...] = norm_rows(hidden, ag_ref[...], as_ref[...]).astype(bf16)
        acc[...] = jnp.zeros_like(acc)

    h = dot(normed[...], up_ref[0])
    inner = (0.5 * h * (1.0 + lax.erf(h * 0.7071067811865476))).astype(bf16)
    for n in range(2):
        cols = pl.ds(512 * n, 512)
        acc[:, cols] += dot(inner, down_ref[0, 512 * n : 512 * n + 512, :])

    @pl.when(t == 7)
    def _():
        hidden = normed[...].astype(f32) + acc[...]
        done = norm_rows(hidden, mg_ref[...], ms_ref[...]).astype(bf16)
        for i in range(8):
            out_ref[i] = done[:, 128 * i : 128 * i + 128]


def swap_all(value, axis):
    return lax.all_to_all(value, axis, split_axis=0, concat_axis=0, tiled=True)


def cost(flops, size, trans=0):
    return pl.CostEstimate(flops=flops, bytes_accessed=size, transcendentals=trans)


def local(
    tokens,
    qkv_weight,
    out_weight,
    attn_gain,
    attn_shift,
    up_weight,
    down_weight,
    mlp_gain,
    mlp_shift,
    prefix_cache,
    earlier_cache,
    suffix_len,
    prefix_id,
    earlier_slot,
):
    n_req = lax.axis_size(REQ)
    core = lax.axis_index("c")
    rank = lax.axis_index(TP)

    own_half = swap_all(jnp.broadcast_to(tokens[None], (4, 512, 128)), "y")
    far_half = lax.ppermute(own_half, "c", [(0, 1), (1, 0)])

    shards = jnp.concatenate(
        [
            up_weight,
            down_weight[:, :512],
            down_weight[:, 512:],
            out_weight[:, :512],
            out_weight[:, 512:],
        ],
        axis=0,
    )
    shards = lax.all_gather(shards, TP, axis=0, tiled=False)

    lengths = suffix_len.reshape(32, 2)[:, 0]
    prefix = prefix_id.reshape(32, 2)
    slots = earlier_slot.reshape(32, 2)
    own_pre = prefix[:, 0] // 2
    slot = jnp.maximum(slots[:, 0], slots[:, 1])
    own_erl = slot // 32
    second = (slots[:, 1] >= 0).astype(jnp.int32)
    pairs = jnp.stack([own_pre, own_erl, second, lengths])
    idx = jnp.arange(16)
    picks = jnp.where(idx[None] < lengths[:, None], prefix[:, :1] % 2, prefix[:, 1:] % 2)
    owners = jnp.arange(n_req)[:, None]
    info_pre = jnp.sum(
        jnp.where((owners == own_pre[None])[:, :, None], picks[None], 0), axis=1
    )
    info_erl = jnp.sum(jnp.where(owners == own_erl[None], slot[None] % 32 + 1, 0), axis=1)
    info = jnp.concatenate(
        [info_pre, info_erl[:, None], jnp.zeros((n_req, 111), jnp.int32)], axis=1
    ).astype(f32)

    w_split = qkv_weight.reshape(4, 2, 128, 384)
    w_own = jnp.where(core == 0, w_split[:, 0], w_split[:, 1]).reshape(512, 384)
    w_far = jnp.where(core == 0, w_split[:, 1], w_split[:, 0]).reshape(512, 384)
    w_qkv = jnp.concatenate([w_own, w_far], axis=0)

    send, qkv = pl.pallas_call(
        qkv_kernel,
        in_specs=[SM, VM, VM, VM, VM],
        out_specs=[VM, VM],
        out_shape=[
            jax.ShapeDtypeStruct((n_req, 32, 128), bf16),
            jax.ShapeDtypeStruct((512, 384), bf16),
        ],
        cost_estimate=cost(2 * 512 * 1024 * 384, 3 << 20),
        name="qkv_place",
    )(pairs, own_half, far_half, w_qkv, info)

    got = swap_all(send, REQ)

    len_rows = jnp.broadcast_to(lengths[:, None, None], (32, 16, 1)).reshape(512, 1)
    own_out, own_lse = pl.pallas_call(
        own_kernel,
        in_specs=[VM, VM],
        out_specs=[VM, VM],
        out_shape=[jax.ShapeDtypeStruct((512, 128), f32)] * 2,
        cost_estimate=cost(2 * 512 * 128 * 128 * 4, 1 << 20, 2 * 512 * 128),
        name="own_attention",
    )(qkv, len_rows)

    ret = pl.pallas_call(
        owner_kernel,
        in_specs=[VM] * 5,
        out_specs=VM,
        out_shape=jax.ShapeDtypeStruct((n_req, 32, 128), bf16),
        cost_estimate=cost(2 * 1024 * 128 * 4096, 2 << 20, 2 * 1024 * 768),
        name="owner_attention",
    )(
        got,
        prefix_cache[:, :, 0],
        prefix_cache[:, :, 1],
        earlier_cache[:, :, 0].reshape(512, 128),
        earlier_cache[:, :, 1].reshape(512, 128),
    )

    back = swap_all(ret, REQ)

    attended = pl.pallas_call(
        merge_kernel,
        in_specs=[SM, VM, VM, VM],
        out_specs=VM,
        out_shape=jax.ShapeDtypeStruct((512, 128), bf16),
        scratch_shapes=[pltpu.VMEM((512, 128), f32)] * 5,
        cost_estimate=cost(2 * 512 * 128 * 256, 1 << 20, 3 * 512 * 128),
        name="merge",
    )(pairs, back, own_out, own_lse)

    att = swap_all(attended.reshape(8, 64, 128), TP)

    own_rows = lax.dynamic_slice_in_dim(own_half, rank * 64, 64, 1)
    far_rows = lax.dynamic_slice_in_dim(far_half, rank * 64, 64, 1)
    even = jnp.where(core == 0, own_rows, far_rows)
    odd = jnp.where(core == 0, far_rows, own_rows)
    tok_rows = jnp.stack([even, odd], axis=1).transpose(2, 0, 1, 3).reshape(64, 1024)

    whole = lambda *shape: pl.BlockSpec(shape, lambda t: (0,) * len(shape))
    encoded = pl.pallas_call(
        tail_kernel,
        grid=(8,),
        in_specs=[
            whole(8, 64, 128),
            whole(64, 1024),
            pl.BlockSpec((8, 256, 512), lambda t: (0, 8, 0)),
            whole(1, 1024),
            whole(1, 1024),
            whole(1, 1024),
            whole(1, 1024),
            pl.BlockSpec((1, 1024, 512), lambda t: (t, 0, 0)),
            pl.BlockSpec((1, 1024, 512), lambda t: (t, 1, 0)),
        ],
        out_specs=whole(8, 64, 128),
        out_shape=jax.ShapeDtypeStruct((8, 64, 128), bf16),
        scratch_shapes=[pltpu.VMEM((64, 1024), bf16), pltpu.VMEM((64, 1024), f32)],
        compiler_params=pltpu.CompilerParams(vmem_limit_bytes=32 << 20),
        cost_estimate=cost(2 * 64 * 9 * 1024 * 1024, 19 << 20, 64 * 4096),
        name="project_norm_ffn",
    )(
        att,
        tok_rows,
        shards,
        attn_gain.reshape(1, 1024),
        attn_shift.reshape(1, 1024),
        mlp_gain.reshape(1, 1024),
        mlp_shift.reshape(1, 1024),
        shards,
        shards,
    )
    return swap_all(encoded, TP).reshape(512, 128)


def solution(mesh):
    split = Mesh(mesh.devices.reshape(16, 4, 4, 2), ("z", "x", "y", "c"))
    placed = (
        P(REQ, TP),
        P(None, None, TP),
        P(TP, None),
        P(),
        P(),
        P(None, TP),
        P(TP, None),
        P(),
        P(),
        P(REQ, None, None, TP),
        P(REQ, None, None, TP),
        P(REQ),
        P(REQ),
        P(REQ),
    )
    return jax.shard_map(
        local, mesh=split, in_specs=placed, out_specs=P(REQ, TP), check_vma=False
    )
```

```python
import jax
import jax.numpy as jnp
from jax import lax
from jax.experimental import pallas as pl
from jax.experimental.pallas import tpu as pltpu
from jax.sharding import Mesh, PartitionSpec as P

HD = 64
REQ = ("z", "x")
TP = ("y", "c")
SCALE = 0.125
NEG = -1e30
EPS = 1e-05
bf16 = jnp.bfloat16
f32 = jnp.float32

VM = pl.BlockSpec(memory_space=pltpu.VMEM)
SM = pl.BlockSpec(memory_space=pltpu.SMEM)
SMALL = pltpu.CompilerParams(vmem_limit_bytes=16 << 20)


def iota(shape, axis):
    return lax.broadcasted_iota(jnp.int32, shape, axis)


def head_mask(x, h):
    lane = iota(x.shape, len(x.shape) - 1)
    return jnp.where((lane >= HD) == (h == 1), x, jnp.zeros_like(x))


def dot_t(a, b):
    return lax.dot_general(a, b, (((1,), (1,)), ((), ())), preferred_element_type=f32)


def dot(a, b):
    return jnp.dot(a, b, preferred_element_type=f32)


def softmax_parts(scores, allowed):
    masked = scores if allowed is None else jnp.where(allowed, scores, NEG)
    top = jnp.max(masked, axis=-1, keepdims=True)
    weights = jnp.exp(masked - top)
    total = jnp.sum(weights, axis=-1, keepdims=True)
    return weights.astype(bf16), 1.0 / total, top + jnp.log(total)


def half_weight(w_ref, core, buf):
    for y in range(4):
        rows = pl.ds(pl.multiple_of((2 * y + core) * 128, 128), 128)
        for n in range(3):
            buf[128 * y : 128 * y + 128, 128 * n : 128 * n + 128] = w_ref[n, rows, :]


def half_rows(half_ref, rows):
    return jnp.concatenate([half_ref[i, rows, :] for i in range(4)], axis=1)


def part_kernel(core, half_ref, w_ref, part_ref, buf):
    half_weight(w_ref, core[0], buf)

    def block(b, carry):
        rows = pl.ds(pl.multiple_of(b * 256, 256), 256)
        part_ref[rows, :] = dot(half_rows(half_ref, rows), buf[...])
        return carry

    lax.fori_loop(0, 2, block, 0)


def pair_of(lens, pre, erl, g):
    first, later = erl[2 * g], erl[2 * g + 1]
    slot = jnp.maximum(first, later)
    return pre[2 * g] // 2, slot // 32, slot % 32, later >= 0, lens[2 * g]


def place_kernel(core, lens, pre, erl, part_ref, half_ref, w_ref, send_ref, qkv_ref, buf):
    row = iota((16, 128), 0)
    lane = iota((16, 128), 1)
    half_weight(w_ref, 1 - core[0], buf)
    send_ref[...] = jnp.zeros(send_ref.shape, bf16)

    def block(b, carry):
        rows = pl.ds(pl.multiple_of(b * 128, 128), 128)
        out = part_ref[rows, :] + dot(half_rows(half_ref, rows), buf[...])
        qkv_ref[rows, :] = out.astype(bf16)
        q = out[:, :128].astype(bf16)
        for p in range(8):
            g = b * 8 + p
            slot, slot_e, row_e, late, span = pair_of(lens, pre, erl, g)
            qp = q[16 * p : 16 * p + 16]
            send_ref[slot, 0:16, :] = qp
            pick = jnp.where(lane < span, pre[2 * g] % 2, pre[2 * g + 1] % 2)
            pick = jnp.where((row == 15) & (lane < 16), pick, 0).astype(f32)
            held = send_ref[slot, 16:32, :].astype(f32)
            send_ref[slot, 16:32, :] = (held + pick).astype(bf16)
            qf = qp.astype(f32)
            moved = jnp.where(late, pltpu.roll(qf, 15, 0), qf)
            held = send_ref[slot_e, 16:32, :].astype(f32)
            held = jnp.where(lane == 16, (row_e + 1).astype(f32), held)
            send_ref[slot_e, 16:32, :] = jnp.where(row == 15, held, moved).astype(bf16)
        return carry

    lax.fori_loop(0, 4, block, 0)


def own_kernel(lens, qkv_ref, out_ref, lse_ref):
    r = iota((128, 128), 0)
    c = iota((128, 128), 1)

    def block(b, carry):
        rows = pl.ds(pl.multiple_of(b * 128, 128), 128)
        q = qkv_ref[rows, 0:128]
        k = qkv_ref[rows, 128:256]
        v = qkv_ref[rows, 256:384]
        span = jnp.concatenate(
            [jnp.full((16, 128), lens[2 * (b * 8 + p)], jnp.int32) for p in range(8)], axis=0
        )
        same = ((r // 16) == (c // 16)) & (c <= r) & (((r % 16) < span) == ((c % 16) < span))
        res = []
        for h in range(2):
            w, inv, lse = softmax_parts(dot_t(head_mask(q, h), k) * SCALE, same)
            res.append((dot(w, v) * inv, jnp.broadcast_to(lse, (128, 128))))
        out_ref[rows, :] = head_mask(res[0][0], 0) + head_mask(res[1][0], 1)
        lse_ref[rows, :] = head_mask(res[0][1], 0) + head_mask(res[1][1], 1)
        return carry

    lax.fori_loop(0, 4, block, 0)


def stack_heads(q):
    q = q * jnp.asarray(SCALE, q.dtype)
    return jnp.concatenate([head_mask(q, 0), head_mask(q, 1)], axis=0)


def join_heads(x):
    n = x.shape[0] // 2
    return head_mask(x[:n], 0) + head_mask(x[n:], 1)


def owner_kernel(got_ref, pk_ref, pv_ref, ek_ref, ev_ref, ret_ref, row_v, row_s, sem):
    sub = iota((8, 16, 128), 1)
    lane = iota((8, 16, 128), 2)
    group = lane // 16
    r = iota((256, 128), 0)
    c = iota((256, 128), 1)
    near = ((r % 128) // 16) == (c // 16)

    def rows_of(b, carry):
        slots = pl.ds(pl.multiple_of(b * 8, 8), 8)
        line = got_ref[slots, 16:32, :].astype(f32)[:, 15:16, :]
        row_v[slots, :] = jnp.maximum(line.reshape(8, 128) - 1.0, 0.0).astype(jnp.int32)
        return carry

    lax.fori_loop(0, 8, rows_of, 0)
    copy = pltpu.make_async_copy(row_v, row_s, sem)
    copy.start()
    copy.wait()

    def prefix_part(b):
        slots = pl.ds(b * 8, 8)
        q = stack_heads(got_ref[slots, 0:16, :].reshape(128, 128))
        line = got_ref[slots, 16:32, :].astype(f32)[:, 15:16, :]
        info = jnp.broadcast_to(line, (8, 16, 128))
        pick = jnp.sum(jnp.where(lane == sub, info, 0.0), axis=-1, keepdims=True)
        pick = pick.reshape(128, 1) > 0.5
        pick = jnp.broadcast_to(pick, (128, 256))
        pick = jnp.concatenate([pick, pick], axis=0)
        s = jnp.where(pick, dot_t(q, pk_ref[1]), dot_t(q, pk_ref[0]))
        w, inv, lse = softmax_parts(s, None)
        none = jnp.zeros_like(w)
        o = dot(jnp.where(pick, none, w), pv_ref[0]) + dot(jnp.where(pick, w, none), pv_ref[1])
        return join_heads(o * inv), lse

    def earlier_part(b):
        slots = pl.ds(b * 8, 8)
        q = stack_heads(got_ref[slots, 16:32, :].reshape(128, 128))
        at = [pl.ds(pl.multiple_of(row_s[b * 8 + i, 16] * 16, 16), 16) for i in range(8)]
        keys = jnp.concatenate([ek_ref[x, :] for x in at], axis=0)
        values = jnp.concatenate([ev_ref[x, :] for x in at], axis=0)
        w, inv, lse = softmax_parts(dot_t(q, keys), near)
        return join_heads(dot(w, values) * inv), lse

    def block(b, carry):
        slots = pl.ds(b * 8, 8)
        pre, pre_lse = prefix_part(b)
        erl, erl_lse = earlier_part(b)
        ret_ref[slots, 0:16, :] = pre.astype(bf16).reshape(8, 16, 128)
        stats = (pre_lse[:128], pre_lse[128:], erl_lse[:128], erl_lse[128:])
        spread = jnp.zeros((8, 16, 128), f32)
        for n in range(4):
            want = ((group // 4) * 2 + group % 2) == n
            spread = jnp.where(want, stats[n].reshape(8, 16, 1), spread)
        line = jnp.sum(jnp.where(lane % 16 == sub, spread, 0.0), axis=1, keepdims=True)
        high = line.astype(bf16).astype(f32)
        line = jnp.where((group[:, 0:1] // 2) % 2 == 1, line - high, high)
        ret_ref[slots, 16:32, :] = jnp.where(
            sub == 15, jnp.broadcast_to(line, (8, 16, 128)), erl.reshape(8, 16, 128)
        ).astype(bf16)
        return carry

    lax.fori_loop(0, 8, block, 0, unroll=2)


def merge_kernel(
    lens, pre, erl, ret_ref, own_ref, lse_ref, out_ref, pre_o, pre_s, erl_o, erl_s, erl_on
):
    row = iota((16, 128), 0)
    lane = iota((16, 128), 1)
    diag = (lane % 16) == row

    def block(b, carry):
        for p in range(8):
            g = b * 8 + p
            rows = pl.ds(pl.multiple_of(b * 128, 128) + 16 * p, 16)
            slot, slot_e, _, late, span = pair_of(lens, pre, erl, g)
            pre_o[rows, :] = ret_ref[slot, 0:16, :].astype(f32)
            line = jnp.broadcast_to(ret_ref[slot, 16:32, :].astype(f32)[15:16, :], (16, 128))
            pre_s[rows, :] = jnp.where(diag & (lane < 64), line, 0.0)
            part = ret_ref[slot_e, 16:32, :].astype(f32)
            line = jnp.broadcast_to(part[15:16, :], (16, 128))
            stat = jnp.where(diag & (lane >= 64), line, 0.0)
            erl_o[rows, :] = jnp.where(late, pltpu.roll(part, 1, 0), part)
            erl_s[rows, :] = jnp.where(late, pltpu.roll(stat, 1, 0), stat)
            turn = jnp.where(late, 1, 0)
            erl_on[rows, :] = jnp.where((row < span).astype(jnp.int32) + turn == 1, 1.0, 0.0)
        rows = pl.ds(pl.multiple_of(b * 128, 128), 128)
        a = iota((128, 128), 0)
        c = iota((128, 128), 1)
        pick = (((a // 16) % 2) == (c // 64)).astype(bf16)
        l_pre = dot(pre_s[rows, :].astype(bf16), pick)
        l_erl = dot(erl_s[rows, :].astype(bf16), pick)
        on = erl_on[rows, :] > 0.5
        l_erl = jnp.where(on, l_erl, NEG)
        l_own = lse_ref[rows, :]
        top = jnp.maximum(jnp.maximum(l_own, l_pre), l_erl)
        w_own = jnp.exp(l_own - top)
        w_pre = jnp.exp(l_pre - top)
        w_erl = jnp.exp(l_erl - top)
        mixed = w_own * own_ref[rows, :] + w_pre * pre_o[rows, :]
        mixed = mixed + w_erl * jnp.where(on, erl_o[rows, :], 0.0)
        out_ref[rows, :] = (mixed / (w_own + w_pre + w_erl)).astype(bf16)
        return carry

    lax.fori_loop(0, 4, block, 0)


def norm_rows(hidden, gain, shift):
    mean = jnp.mean(hidden, axis=-1, keepdims=True)
    centred = hidden - mean
    var = jnp.mean(centred * centred, axis=-1, keepdims=True)
    return centred * lax.rsqrt(var + EPS) * gain + shift


def tail_kernel(
    att_ref, tok_ref, ag_ref, as_ref, mg_ref, ms_ref, up_hbm, rest_hbm, out_ref, w_out, up, down, sem
):
    def fetch(t):
        return (
            pltpu.make_async_copy(up_hbm.at[t], up.at[t], sem.at[2 * t + 1]),
            pltpu.make_async_copy(rest_hbm.at[t, 0:512, :], down.at[t], sem.at[2 * t + 2]),
        )

    first = pltpu.make_async_copy(rest_hbm.at[:, 512:640, :], w_out, sem.at[0])
    first.start()
    for t in range(8):
        for copy in fetch(t):
            copy.start()
    att = jnp.concatenate([att_ref[i] for i in range(8)], axis=1)
    first.wait()
    hidden = tok_ref[...].astype(f32) + dot(att, w_out[...].reshape(1024, 1024))
    normed = norm_rows(hidden, ag_ref[...], as_ref[...]).astype(bf16)

    def block(t, acc):
        up_copy, down_copy = fetch(t)
        up_copy.wait()
        h = dot(normed, up[t])
        inner = (0.5 * h * (1.0 + lax.erf(h * 0.7071067811865476))).astype(bf16)
        down_copy.wait()
        return acc + dot(inner, down[t])

    acc = lax.fori_loop(0, 8, block, jnp.zeros((64, 1024), f32))
    hidden = normed.astype(f32) + acc
    done = norm_rows(hidden, mg_ref[...], ms_ref[...]).astype(bf16)
    for i in range(8):
        out_ref[i] = done[:, 128 * i : 128 * i + 128]


def swap_all(value, axis):
    return lax.all_to_all(value, axis, split_axis=0, concat_axis=0, tiled=True)


def cost(flops, size, trans=0):
    return pl.CostEstimate(flops=flops, bytes_accessed=size, transcendentals=trans)


def local(
    tokens,
    qkv_weight,
    out_weight,
    attn_gain,
    attn_shift,
    up_weight,
    down_weight,
    mlp_gain,
    mlp_shift,
    prefix_cache,
    earlier_cache,
    suffix_len,
    prefix_id,
    earlier_slot,
):
    n_req = lax.axis_size(REQ)
    core = lax.axis_index("c")
    rank = lax.axis_index(TP)

    ups = lax.all_gather(up_weight, TP, axis=0, tiled=False)

    own_half = swap_all(jnp.broadcast_to(tokens[None], (4, 512, 128)), "y")
    far_half = lax.ppermute(own_half, "c", [(0, 1), (1, 0)])

    far_half, down_weight, out_weight = lax.optimization_barrier(
        (far_half, down_weight, out_weight)
    )
    rest = jnp.concatenate([down_weight, out_weight], axis=0)
    rest = lax.all_gather(rest, TP, axis=0, tiled=False)

    core1 = core.reshape(1)
    w_qkv = qkv_weight.transpose(1, 0, 2)
    part = pl.pallas_call(
        part_kernel,
        in_specs=[SM, VM, VM],
        out_specs=VM,
        out_shape=jax.ShapeDtypeStruct((512, 384), f32),
        scratch_shapes=[pltpu.VMEM((512, 384), bf16)],
        compiler_params=SMALL,
        cost_estimate=cost(2 * 512 * 512 * 384, 2 << 20),
        name="qkv_own_half",
    )(core1, own_half, w_qkv)
    send, qkv = pl.pallas_call(
        place_kernel,
        in_specs=[SM] * 4 + [VM] * 3,
        out_specs=[VM, VM],
        out_shape=[
            jax.ShapeDtypeStruct((n_req, 32, 128), bf16),
            jax.ShapeDtypeStruct((512, 384), bf16),
        ],
        scratch_shapes=[pltpu.VMEM((512, 384), bf16)],
        compiler_params=SMALL,
        cost_estimate=cost(2 * 512 * 512 * 384, 3 << 20),
        name="qkv_place",
    )(core1, suffix_len, prefix_id, earlier_slot, part, far_half, w_qkv)

    got = swap_all(send, REQ)

    own_out, own_lse = pl.pallas_call(
        own_kernel,
        in_specs=[SM, VM],
        out_specs=[VM, VM],
        out_shape=[jax.ShapeDtypeStruct((512, 128), f32)] * 2,
        compiler_params=SMALL,
        cost_estimate=cost(2 * 512 * 128 * 128 * 4, 1 << 20, 2 * 512 * 128),
        name="own_attention",
    )(suffix_len, qkv)

    ret = pl.pallas_call(
        owner_kernel,
        in_specs=[VM] * 5,
        out_specs=VM,
        out_shape=jax.ShapeDtypeStruct((n_req, 32, 128), bf16),
        scratch_shapes=[
            pltpu.VMEM((n_req, 128), jnp.int32),
            pltpu.SMEM((n_req, 128), jnp.int32),
            pltpu.SemaphoreType.DMA,
        ],
        compiler_params=SMALL,
        cost_estimate=cost(2 * 1024 * 128 * 2048, 2 << 20, 2 * 1024 * 384),
        name="owner_attention",
    )(
        got,
        prefix_cache[:, :, 0],
        prefix_cache[:, :, 1],
        earlier_cache[:, :, 0].reshape(512, 128),
        earlier_cache[:, :, 1].reshape(512, 128),
    )

    back = swap_all(ret, REQ)

    attended = pl.pallas_call(
        merge_kernel,
        in_specs=[SM, SM, SM, VM, VM, VM],
        out_specs=VM,
        out_shape=jax.ShapeDtypeStruct((512, 128), bf16),
        scratch_shapes=[pltpu.VMEM((512, 128), f32)] * 5,
        cost_estimate=cost(2 * 512 * 128 * 256, 1 << 20, 3 * 512 * 128),
        compiler_params=SMALL,
        name="merge",
    )(suffix_len, prefix_id, earlier_slot, back, own_out, own_lse)

    att = swap_all(attended.reshape(8, 64, 128), TP)

    own_rows = lax.dynamic_slice_in_dim(own_half, rank * 64, 64, 1)
    far_rows = lax.dynamic_slice_in_dim(far_half, rank * 64, 64, 1)
    even = jnp.where(core == 0, own_rows, far_rows)
    odd = jnp.where(core == 0, far_rows, own_rows)
    tok_rows = jnp.stack([even, odd], axis=1).transpose(2, 0, 1, 3).reshape(64, 1024)

    hbm = pl.BlockSpec(memory_space=pl.ANY)
    encoded = pl.pallas_call(
        tail_kernel,
        in_specs=[VM] * 6 + [hbm] * 2,
        out_specs=VM,
        out_shape=jax.ShapeDtypeStruct((8, 64, 128), bf16),
        scratch_shapes=[
            pltpu.VMEM((8, 128, 1024), bf16),
            pltpu.VMEM((8, 1024, 512), bf16),
            pltpu.VMEM((8, 512, 1024), bf16),
            pltpu.SemaphoreType.DMA((17,)),
        ],
        compiler_params=pltpu.CompilerParams(vmem_limit_bytes=52 << 20),
        cost_estimate=cost(2 * 64 * 9 * 1024 * 1024, 19 << 20, 64 * 4096),
        name="project_norm_ffn",
    )(
        att,
        tok_rows,
        attn_gain.reshape(1, 1024),
        attn_shift.reshape(1, 1024),
        mlp_gain.reshape(1, 1024),
        mlp_shift.reshape(1, 1024),
        ups,
        rest,
    )
    return swap_all(encoded, TP).reshape(512, 128)


def solution(mesh):
    split = Mesh(mesh.devices.reshape(16, 4, 4, 2), ("z", "x", "y", "c"))
    placed = (
        P(REQ, TP),
        P(None, None, TP),
        P(TP, None),
        P(),
        P(),
        P(None, TP),
        P(TP, None),
        P(),
        P(),
        P(REQ, None, None, TP),
        P(REQ, None, None, TP),
        P(REQ),
        P(REQ),
        P(REQ),
    )
    return jax.shard_map(
        local, mesh=split, in_specs=placed, out_specs=P(REQ, TP), check_vma=False
    )
```

```python
import jax
import jax.numpy as jnp
from jax import lax
from jax.experimental import pallas as pl
from jax.experimental.pallas import tpu as pltpu
from jax.sharding import Mesh, PartitionSpec as P

HD = 64
REQ = ("z", "x")
TP = ("y", "c")
SCALE = 0.125
NEG = -1e30
EPS = 1e-05
bf16 = jnp.bfloat16
f32 = jnp.float32

VM = pl.BlockSpec(memory_space=pltpu.VMEM)
SM = pl.BlockSpec(memory_space=pltpu.SMEM)
SMALL = pltpu.CompilerParams(vmem_limit_bytes=16 << 20)


def iota(shape, axis):
    return lax.broadcasted_iota(jnp.int32, shape, axis)


def head_mask(x, h):
    lane = iota(x.shape, len(x.shape) - 1)
    return jnp.where((lane >= HD) == (h == 1), x, jnp.zeros_like(x))


def dot_t(a, b):
    return lax.dot_general(a, b, (((1,), (1,)), ((), ())), preferred_element_type=f32)


def dot(a, b):
    return jnp.dot(a, b, preferred_element_type=f32)


def softmax_parts(scores, allowed):
    masked = scores if allowed is None else jnp.where(allowed, scores, NEG)
    top = jnp.max(masked, axis=-1, keepdims=True)
    weights = jnp.exp(masked - top)
    total = jnp.sum(weights, axis=-1, keepdims=True)
    return weights.astype(bf16), 1.0 / total, top + jnp.log(total)


def half_weight(w_ref, core, buf):
    for y in range(4):
        rows = pl.ds(pl.multiple_of((2 * y + core) * 128, 128), 128)
        for n in range(3):
            buf[128 * y : 128 * y + 128, 128 * n : 128 * n + 128] = w_ref[n, rows, :]


def half_rows(half_ref, rows):
    return jnp.concatenate([half_ref[i, rows, :] for i in range(4)], axis=1)


def part_kernel(core, half_ref, w_ref, part_ref, buf):
    half_weight(w_ref, core[0], buf)

    def block(b, carry):
        rows = pl.ds(pl.multiple_of(b * 256, 256), 256)
        part_ref[rows, :] = dot(half_rows(half_ref, rows), buf[...])
        return carry

    lax.fori_loop(0, 2, block, 0)


def pair_of(lens, pre, erl, g):
    first, later = erl[2 * g], erl[2 * g + 1]
    slot = jnp.maximum(first, later)
    return pre[2 * g] // 2, slot // 32, slot % 32, later >= 0, lens[2 * g]


def place_kernel(core, lens, pre, erl, part_ref, half_ref, w_ref, send_ref, qkv_ref, buf):
    row = iota((16, 128), 0)
    lane = iota((16, 128), 1)
    half_weight(w_ref, 1 - core[0], buf)
    send_ref[...] = jnp.zeros(send_ref.shape, bf16)

    def block(b, carry):
        rows = pl.ds(pl.multiple_of(b * 128, 128), 128)
        out = part_ref[rows, :] + dot(half_rows(half_ref, rows), buf[...])
        qkv_ref[rows, :] = out.astype(bf16)
        q = out[:, :128].astype(bf16)
        for p in range(8):
            g = b * 8 + p
            slot, slot_e, row_e, late, span = pair_of(lens, pre, erl, g)
            qp = q[16 * p : 16 * p + 16]
            send_ref[slot, 0:16, :] = qp
            pick = jnp.where(lane < span, pre[2 * g] % 2, pre[2 * g + 1] % 2)
            pick = jnp.where((row == 15) & (lane < 16), pick, 0).astype(f32)
            held = send_ref[slot, 16:32, :].astype(f32)
            send_ref[slot, 16:32, :] = (held + pick).astype(bf16)
            qf = qp.astype(f32)
            moved = jnp.where(late, pltpu.roll(qf, 15, 0), qf)
            held = send_ref[slot_e, 16:32, :].astype(f32)
            held = jnp.where(lane == 16, (row_e + 1).astype(f32), held)
            send_ref[slot_e, 16:32, :] = jnp.where(row == 15, held, moved).astype(bf16)
        return carry

    lax.fori_loop(0, 4, block, 0)


def own_kernel(lens, qkv_ref, out_ref, lse_ref):
    r = iota((128, 128), 0)
    c = iota((128, 128), 1)

    def block(b, carry):
        rows = pl.ds(pl.multiple_of(b * 128, 128), 128)
        q = qkv_ref[rows, 0:128]
        k = qkv_ref[rows, 128:256]
        v = qkv_ref[rows, 256:384]
        span = jnp.concatenate(
            [jnp.full((16, 128), lens[2 * (b * 8 + p)], jnp.int32) for p in range(8)], axis=0
        )
        same = ((r // 16) == (c // 16)) & (c <= r) & (((r % 16) < span) == ((c % 16) < span))
        res = []
        for h in range(2):
            w, inv, lse = softmax_parts(dot_t(head_mask(q, h), k) * SCALE, same)
            res.append((dot(w, v) * inv, jnp.broadcast_to(lse, (128, 128))))
        out_ref[rows, :] = head_mask(res[0][0], 0) + head_mask(res[1][0], 1)
        lse_ref[rows, :] = head_mask(res[0][1], 0) + head_mask(res[1][1], 1)
        return carry

    lax.fori_loop(0, 4, block, 0)


def stack_heads(q):
    q = q * jnp.asarray(SCALE, q.dtype)
    return jnp.concatenate([head_mask(q, 0), head_mask(q, 1)], axis=0)


def join_heads(x):
    n = x.shape[0] // 2
    return head_mask(x[:n], 0) + head_mask(x[n:], 1)


def owner_kernel(got_ref, pk_ref, pv_ref, ek_ref, ev_ref, ret_ref, row_v, row_s, sem):
    sub = iota((8, 16, 128), 1)
    lane = iota((8, 16, 128), 2)
    group = lane // 16
    r = iota((256, 128), 0)
    c = iota((256, 128), 1)
    near = ((r % 128) // 16) == (c // 16)

    def rows_of(b, carry):
        slots = pl.ds(pl.multiple_of(b * 8, 8), 8)
        line = got_ref[slots, 16:32, :].astype(f32)[:, 15:16, :]
        row_v[slots, :] = jnp.maximum(line.reshape(8, 128) - 1.0, 0.0).astype(jnp.int32)
        return carry

    lax.fori_loop(0, 8, rows_of, 0)
    copy = pltpu.make_async_copy(row_v, row_s, sem)
    copy.start()
    copy.wait()

    def prefix_part(b):
        slots = pl.ds(b * 8, 8)
        q = stack_heads(got_ref[slots, 0:16, :].reshape(128, 128))
        line = got_ref[slots, 16:32, :].astype(f32)[:, 15:16, :]
        info = jnp.broadcast_to(line, (8, 16, 128))
        pick = jnp.sum(jnp.where(lane == sub, info, 0.0), axis=-1, keepdims=True)
        pick = pick.reshape(128, 1) > 0.5
        pick = jnp.broadcast_to(pick, (128, 256))
        pick = jnp.concatenate([pick, pick], axis=0)
        s = jnp.where(pick, dot_t(q, pk_ref[1]), dot_t(q, pk_ref[0]))
        w, inv, lse = softmax_parts(s, None)
        none = jnp.zeros_like(w)
        o = dot(jnp.where(pick, none, w), pv_ref[0]) + dot(jnp.where(pick, w, none), pv_ref[1])
        return join_heads(o * inv), lse

    def earlier_part(b):
        slots = pl.ds(b * 8, 8)
        q = stack_heads(got_ref[slots, 16:32, :].reshape(128, 128))
        at = [pl.ds(pl.multiple_of(row_s[b * 8 + i, 16] * 16, 16), 16) for i in range(8)]
        keys = jnp.concatenate([ek_ref[x, :] for x in at], axis=0)
        values = jnp.concatenate([ev_ref[x, :] for x in at], axis=0)
        w, inv, lse = softmax_parts(dot_t(q, keys), near)
        return join_heads(dot(w, values) * inv), lse

    def block(b, carry):
        slots = pl.ds(b * 8, 8)
        pre, pre_lse = prefix_part(b)
        erl, erl_lse = earlier_part(b)
        ret_ref[slots, 0:16, :] = pre.astype(bf16).reshape(8, 16, 128)
        stats = (pre_lse[:128], pre_lse[128:], erl_lse[:128], erl_lse[128:])
        spread = jnp.zeros((8, 16, 128), f32)
        for n in range(4):
            want = ((group // 4) * 2 + group % 2) == n
            spread = jnp.where(want, stats[n].reshape(8, 16, 1), spread)
        line = jnp.sum(jnp.where(lane % 16 == sub, spread, 0.0), axis=1, keepdims=True)
        high = line.astype(bf16).astype(f32)
        line = jnp.where((group[:, 0:1] // 2) % 2 == 1, line - high, high)
        ret_ref[slots, 16:32, :] = jnp.where(
            sub == 15, jnp.broadcast_to(line, (8, 16, 128)), erl.reshape(8, 16, 128)
        ).astype(bf16)
        return carry

    lax.fori_loop(0, 8, block, 0, unroll=2)


def merge_kernel(
    lens, pre, erl, ret_ref, own_ref, lse_ref, out_ref, pre_o, pre_s, erl_o, erl_s, erl_on
):
    row = iota((16, 128), 0)
    lane = iota((16, 128), 1)
    diag = (lane % 16) == row

    def block(b, carry):
        for p in range(8):
            g = b * 8 + p
            rows = pl.ds(pl.multiple_of(b * 128, 128) + 16 * p, 16)
            slot, slot_e, _, late, span = pair_of(lens, pre, erl, g)
            pre_o[rows, :] = ret_ref[slot, 0:16, :].astype(f32)
            line = jnp.broadcast_to(ret_ref[slot, 16:32, :].astype(f32)[15:16, :], (16, 128))
            pre_s[rows, :] = jnp.where(diag & (lane < 64), line, 0.0)
            part = ret_ref[slot_e, 16:32, :].astype(f32)
            line = jnp.broadcast_to(part[15:16, :], (16, 128))
            stat = jnp.where(diag & (lane >= 64), line, 0.0)
            erl_o[rows, :] = jnp.where(late, pltpu.roll(part, 1, 0), part)
            erl_s[rows, :] = jnp.where(late, pltpu.roll(stat, 1, 0), stat)
            turn = jnp.where(late, 1, 0)
            erl_on[rows, :] = jnp.where((row < span).astype(jnp.int32) + turn == 1, 1.0, 0.0)
        rows = pl.ds(pl.multiple_of(b * 128, 128), 128)
        a = iota((128, 128), 0)
        c = iota((128, 128), 1)
        pick = (((a // 16) % 2) == (c // 64)).astype(bf16)
        l_pre = dot(pre_s[rows, :].astype(bf16), pick)
        l_erl = dot(erl_s[rows, :].astype(bf16), pick)
        on = erl_on[rows, :] > 0.5
        l_erl = jnp.where(on, l_erl, NEG)
        l_own = lse_ref[rows, :]
        top = jnp.maximum(jnp.maximum(l_own, l_pre), l_erl)
        w_own = jnp.exp(l_own - top)
        w_pre = jnp.exp(l_pre - top)
        w_erl = jnp.exp(l_erl - top)
        mixed = w_own * own_ref[rows, :] + w_pre * pre_o[rows, :]
        mixed = mixed + w_erl * jnp.where(on, erl_o[rows, :], 0.0)
        out_ref[rows, :] = (mixed / (w_own + w_pre + w_erl)).astype(bf16)
        return carry

    lax.fori_loop(0, 4, block, 0)


def norm_rows(hidden, gain, shift):
    mean = jnp.mean(hidden, axis=-1, keepdims=True)
    centred = hidden - mean
    var = jnp.mean(centred * centred, axis=-1, keepdims=True)
    return centred * lax.rsqrt(var + EPS) * gain + shift


def pack_kernel(at, up_ref, down_ref, out_ref, pack_ref, sem):
    x = at[0]
    up_rows = pl.ds(pl.multiple_of(x * 256, 256), 256)
    down_rows = pl.ds(pl.multiple_of(x * 128, 128), 128)
    out_rows = pl.ds(pl.multiple_of(x * 32, 32), 32)
    left, right = pl.ds(0, 512), pl.ds(512, 512)
    copies = (
        (up_ref.at[up_rows, :], 0, 256),
        (down_ref.at[down_rows, left], 256, 128),
        (down_ref.at[down_rows, right], 384, 128),
        (out_ref.at[out_rows, left], 512, 32),
        (out_ref.at[out_rows, right], 544, 32),
    )
    copies = [
        pltpu.make_async_copy(source, pack_ref.at[pl.ds(first, size), :], sem.at[i])
        for i, (source, first, size) in enumerate(copies)
    ]
    for copy in copies:
        copy.start()
    for copy in copies:
        copy.wait()


def tail_kernel(
    att_ref,
    tok_ref,
    ag_ref,
    as_ref,
    mg_ref,
    ms_ref,
    w_hbm,
    out_ref,
    acc,
    left,
    right,
    up,
    down,
    sem,
):
    first = []
    for x in range(4):
        for n, half in enumerate((left, right)):
            source = w_hbm.at[x, :, pl.ds(512 + 32 * n, 32), :]
            first.append(pltpu.make_async_copy(source, half.at[:, x], sem.at[16 + 2 * x + n]))

    def fetch(t):
        return (
            pltpu.make_async_copy(w_hbm.at[:, t, pl.ds(0, 256), :], up.at[t], sem.at[2 * t]),
            pltpu.make_async_copy(w_hbm.at[:, t, pl.ds(256, 256), :], down.at[t], sem.at[2 * t + 1]),
        )

    for copy in first:
        copy.start()
    for t in range(8):
        for copy in fetch(t):
            copy.start()
    att = jnp.concatenate([att_ref[i] for i in range(8)], axis=1)
    for copy in first:
        copy.wait()
    proj = [dot(att, half[...].reshape(1024, 512)) for half in (left, right)]
    hidden = tok_ref[...].astype(f32) + jnp.concatenate(proj, axis=1)
    normed = norm_rows(hidden, ag_ref[...], as_ref[...]).astype(bf16)
    acc[...] = normed.astype(f32)

    def block(t, carry):
        up_copy, down_copy = fetch(t)
        up_copy.wait()
        h = dot(normed, up[t].reshape(1024, 512))
        inner = (0.5 * h * (1.0 + lax.erf(h * 0.7071067811865476))).astype(bf16)
        down_copy.wait()
        for n in range(2):
            weight = down[t, :, 128 * n : 128 * n + 128, :].reshape(512, 512)
            acc[:, 512 * n : 512 * n + 512] += dot(inner, weight)
        return carry

    lax.fori_loop(0, 8, block, 0)
    done = norm_rows(acc[...], mg_ref[...], ms_ref[...]).astype(bf16)
    for i in range(8):
        out_ref[i] = done[:, 128 * i : 128 * i + 128]


def swap_all(value, axis):
    return lax.all_to_all(value, axis, split_axis=0, concat_axis=0, tiled=True)


def cost(flops, size, trans=0):
    return pl.CostEstimate(flops=flops, bytes_accessed=size, transcendentals=trans)


def local(
    tokens,
    qkv_weight,
    out_weight,
    attn_gain,
    attn_shift,
    up_weight,
    down_weight,
    mlp_gain,
    mlp_shift,
    prefix_cache,
    earlier_cache,
    suffix_len,
    prefix_id,
    earlier_slot,
):
    n_req = lax.axis_size(REQ)
    core = lax.axis_index("c")
    rank = lax.axis_index(TP)

    hbm = pl.BlockSpec(memory_space=pl.ANY)
    packed = pl.pallas_call(
        pack_kernel,
        in_specs=[SM] + [hbm] * 3,
        out_specs=hbm,
        out_shape=jax.ShapeDtypeStruct((576, 512), bf16),
        scratch_shapes=[pltpu.SemaphoreType.DMA((5,))],
        cost_estimate=cost(0, 1 << 20),
        name="pack_weights",
    )(lax.axis_index("x").reshape(1), up_weight, down_weight, out_weight)
    shards = lax.all_gather(packed, ("x", "y", "c"), axis=0, tiled=False)
    shards = shards.reshape(4, 8, 576, 512)

    own_half = swap_all(jnp.broadcast_to(tokens[None], (4, 512, 128)), "y")
    far_half = lax.ppermute(own_half, "c", [(0, 1), (1, 0)])

    core1 = core.reshape(1)
    w_qkv = qkv_weight.transpose(1, 0, 2)
    part = pl.pallas_call(
        part_kernel,
        in_specs=[SM, VM, VM],
        out_specs=VM,
        out_shape=jax.ShapeDtypeStruct((512, 384), f32),
        scratch_shapes=[pltpu.VMEM((512, 384), bf16)],
        compiler_params=SMALL,
        cost_estimate=cost(2 * 512 * 512 * 384, 2 << 20),
        name="qkv_own_half",
    )(core1, own_half, w_qkv)
    send, qkv = pl.pallas_call(
        place_kernel,
        in_specs=[SM] * 4 + [VM] * 3,
        out_specs=[VM, VM],
        out_shape=[
            jax.ShapeDtypeStruct((n_req, 32, 128), bf16),
            jax.ShapeDtypeStruct((512, 384), bf16),
        ],
        scratch_shapes=[pltpu.VMEM((512, 384), bf16)],
        compiler_params=SMALL,
        cost_estimate=cost(2 * 512 * 512 * 384, 3 << 20),
        name="qkv_place",
    )(core1, suffix_len, prefix_id, earlier_slot, part, far_half, w_qkv)

    got = swap_all(send, REQ)

    own_out, own_lse = pl.pallas_call(
        own_kernel,
        in_specs=[SM, VM],
        out_specs=[VM, VM],
        out_shape=[jax.ShapeDtypeStruct((512, 128), f32)] * 2,
        compiler_params=SMALL,
        cost_estimate=cost(2 * 512 * 128 * 128 * 4, 1 << 20, 2 * 512 * 128),
        name="own_attention",
    )(suffix_len, qkv)

    ret = pl.pallas_call(
        owner_kernel,
        in_specs=[VM] * 5,
        out_specs=VM,
        out_shape=jax.ShapeDtypeStruct((n_req, 32, 128), bf16),
        scratch_shapes=[
            pltpu.VMEM((n_req, 128), jnp.int32),
            pltpu.SMEM((n_req, 128), jnp.int32),
            pltpu.SemaphoreType.DMA,
        ],
        compiler_params=SMALL,
        cost_estimate=cost(2 * 1024 * 128 * 2048, 2 << 20, 2 * 1024 * 384),
        name="owner_attention",
    )(
        got,
        prefix_cache[:, :, 0],
        prefix_cache[:, :, 1],
        earlier_cache[:, :, 0].reshape(512, 128),
        earlier_cache[:, :, 1].reshape(512, 128),
    )

    back = swap_all(ret, REQ)

    attended = pl.pallas_call(
        merge_kernel,
        in_specs=[SM, SM, SM, VM, VM, VM],
        out_specs=VM,
        out_shape=jax.ShapeDtypeStruct((512, 128), bf16),
        scratch_shapes=[pltpu.VMEM((512, 128), f32)] * 5,
        cost_estimate=cost(2 * 512 * 128 * 256, 1 << 20, 3 * 512 * 128),
        compiler_params=SMALL,
        name="merge",
    )(suffix_len, prefix_id, earlier_slot, back, own_out, own_lse)

    att = swap_all(attended.reshape(8, 64, 128), TP)

    own_rows = lax.dynamic_slice_in_dim(own_half, rank * 64, 64, 1)
    far_rows = lax.dynamic_slice_in_dim(far_half, rank * 64, 64, 1)
    even = jnp.where(core == 0, own_rows, far_rows)
    odd = jnp.where(core == 0, far_rows, own_rows)
    tok_rows = jnp.stack([even, odd], axis=1).transpose(2, 0, 1, 3).reshape(64, 1024)

    encoded = pl.pallas_call(
        tail_kernel,
        in_specs=[VM] * 6 + [hbm],
        out_specs=VM,
        out_shape=jax.ShapeDtypeStruct((8, 64, 128), bf16),
        scratch_shapes=[
            pltpu.VMEM((64, 1024), f32),
            pltpu.VMEM((8, 4, 32, 512), bf16),
            pltpu.VMEM((8, 4, 32, 512), bf16),
            pltpu.VMEM((8, 4, 256, 512), bf16),
            pltpu.VMEM((8, 4, 256, 512), bf16),
            pltpu.SemaphoreType.DMA((24,)),
        ],
        compiler_params=pltpu.CompilerParams(vmem_limit_bytes=52 << 20),
        cost_estimate=cost(2 * 64 * 9 * 1024 * 1024, 19 << 20, 64 * 4096),
        name="project_norm_ffn",
    )(
        att,
        tok_rows,
        attn_gain.reshape(1, 1024),
        attn_shift.reshape(1, 1024),
        mlp_gain.reshape(1, 1024),
        mlp_shift.reshape(1, 1024),
        shards,
    )
    return swap_all(encoded, TP).reshape(512, 128)


def solution(mesh):
    split = Mesh(mesh.devices.reshape(16, 4, 4, 2), ("z", "x", "y", "c"))
    placed = (
        P(REQ, TP),
        P(None, None, TP),
        P(TP, None),
        P(),
        P(),
        P(None, TP),
        P(TP, None),
        P(),
        P(),
        P(REQ, None, None, TP),
        P(REQ, None, None, TP),
        P(REQ),
        P(REQ),
        P(REQ),
    )
    return jax.shard_map(
        local, mesh=split, in_specs=placed, out_specs=P(REQ, TP), check_vma=False
    )
```

```python
import jax
import jax.numpy as jnp
from jax import lax
from jax.experimental import pallas as pl
from jax.experimental.pallas import tpu as pltpu
from jax.sharding import Mesh, PartitionSpec as P

HD = 64
REQ = ("z", "x")
TP = ("y", "c")
SCALE = 0.125
NEG = -1e30
EPS = 1e-05
bf16 = jnp.bfloat16
f32 = jnp.float32

VM = pl.BlockSpec(memory_space=pltpu.VMEM)
SM = pl.BlockSpec(memory_space=pltpu.SMEM)
SMALL = pltpu.CompilerParams(vmem_limit_bytes=16 << 20)


def iota(shape, axis):
    return lax.broadcasted_iota(jnp.int32, shape, axis)


def head_mask(x, h):
    lane = iota(x.shape, len(x.shape) - 1)
    return jnp.where((lane >= HD) == (h == 1), x, jnp.zeros_like(x))


def dot_t(a, b):
    return lax.dot_general(a, b, (((1,), (1,)), ((), ())), preferred_element_type=f32)


def dot(a, b):
    return jnp.dot(a, b, preferred_element_type=f32)


def softmax_parts(scores, allowed):
    masked = scores if allowed is None else jnp.where(allowed, scores, NEG)
    top = jnp.max(masked, axis=-1, keepdims=True)
    weights = jnp.exp(masked - top)
    total = jnp.sum(weights, axis=-1, keepdims=True)
    return weights.astype(bf16), 1.0 / total, top + jnp.log(total)


def half_rows(half_ref, rows):
    return jnp.concatenate([half_ref[i, rows, :] for i in range(4)], axis=1)


def part_kernel(scal, half_ref, w_hbm, part_ref, far_ref, buf, sem):
    core = scal[3, 0]
    copies = []
    for side, target in ((core, buf), (1 - core, far_ref)):
        for y in range(4):
            rows = pl.ds(pl.multiple_of((2 * y + side) * 128, 128), 128)
            for n in range(3):
                place = target.at[pl.ds(128 * y, 128), pl.ds(128 * n, 128)]
                copies.append(
                    pltpu.make_async_copy(w_hbm.at[n, rows, :], place, sem.at[len(copies)])
                )
    for copy in copies:
        copy.start()
    for copy in copies:
        copy.wait()

    def block(b, carry):
        rows = pl.ds(pl.multiple_of(b * 256, 256), 256)
        part_ref[rows, :] = dot(half_rows(half_ref, rows), buf[...])
        return carry

    lax.fori_loop(0, 2, block, 0)


def pair_of(scal, g):
    first, later = scal[2, 2 * g], scal[2, 2 * g + 1]
    slot = jnp.maximum(first, later)
    return scal[1, 2 * g] // 2, slot // 32, slot % 32, later >= 0, scal[0, 2 * g]


def place_kernel(scal, part_ref, half_ref, w_ref, send_ref, qkv_ref):
    row = iota((16, 128), 0)
    lane = iota((16, 128), 1)
    send_ref[...] = jnp.zeros(send_ref.shape, bf16)

    def block(b, carry):
        rows = pl.ds(pl.multiple_of(b * 128, 128), 128)
        out = part_ref[rows, :] + dot(half_rows(half_ref, rows), w_ref[...])
        qkv_ref[rows, :] = out.astype(bf16)
        q = out[:, :128].astype(bf16)
        for p in range(8):
            g = b * 8 + p
            slot, slot_e, row_e, late, span = pair_of(scal, g)
            qp = q[16 * p : 16 * p + 16]
            send_ref[slot, 0:16, :] = qp
            pick = jnp.where(lane < span, scal[1, 2 * g] % 2, scal[1, 2 * g + 1] % 2)
            pick = jnp.where((row == 15) & (lane < 16), pick, 0).astype(f32)
            held = send_ref[slot, 16:32, :].astype(f32)
            send_ref[slot, 16:32, :] = (held + pick).astype(bf16)
            qf = qp.astype(f32)
            moved = jnp.where(late, pltpu.roll(qf, 15, 0), qf)
            held = send_ref[slot_e, 16:32, :].astype(f32)
            held = jnp.where(lane == 16, (row_e + 1).astype(f32), held)
            send_ref[slot_e, 16:32, :] = jnp.where(row == 15, held, moved).astype(bf16)
        return carry

    lax.fori_loop(0, 4, block, 0)


def own_kernel(scal, qkv_ref, out_ref, lse_ref):
    r = iota((128, 128), 0)
    c = iota((128, 128), 1)

    def block(b, carry):
        rows = pl.ds(pl.multiple_of(b * 128, 128), 128)
        q = qkv_ref[rows, 0:128]
        k = qkv_ref[rows, 128:256]
        v = qkv_ref[rows, 256:384]
        span = jnp.concatenate(
            [jnp.full((16, 128), scal[0, 2 * (b * 8 + p)], jnp.int32) for p in range(8)], axis=0
        )
        same = ((r // 16) == (c // 16)) & (c <= r) & (((r % 16) < span) == ((c % 16) < span))
        res = []
        for h in range(2):
            w, inv, lse = softmax_parts(dot_t(head_mask(q, h), k) * SCALE, same)
            res.append((dot(w, v) * inv, jnp.broadcast_to(lse, (128, 128))))
        out_ref[rows, :] = head_mask(res[0][0], 0) + head_mask(res[1][0], 1)
        lse_ref[rows, :] = head_mask(res[0][1], 0) + head_mask(res[1][1], 1)
        return carry

    lax.fori_loop(0, 4, block, 0)


def stack_heads(q):
    q = q * jnp.asarray(SCALE, q.dtype)
    return jnp.concatenate([head_mask(q, 0), head_mask(q, 1)], axis=0)


def join_heads(x):
    n = x.shape[0] // 2
    return head_mask(x[:n], 0) + head_mask(x[n:], 1)


def owner_kernel(got_ref, pk_ref, pv_ref, ek_ref, ev_ref, ret_ref, row_v, row_s, stat, sem):
    sub = iota((8, 16, 128), 1)
    lane = iota((8, 16, 128), 2)
    group = lane // 16
    r = iota((256, 128), 0)
    c = iota((256, 128), 1)
    near = ((r % 128) // 16) == (c // 16)

    for b in range(8):
        line = got_ref[8 * b : 8 * b + 8, 16:32, :].astype(f32)[:, 15:16, :].reshape(8, 128)
        stat[8 * b : 8 * b + 8, :] = line
        row_v[8 * b : 8 * b + 8, :] = jnp.maximum(line - 1.0, 0.0).astype(jnp.int32)
    copy = pltpu.make_async_copy(row_v, row_s, sem)
    copy.start()

    def stat_line(first, second):
        both = jnp.where(group % 2 == 0, first.reshape(8, 16, 1), second.reshape(8, 16, 1))
        line = jnp.sum(jnp.where(lane % 16 == sub, both, 0.0), axis=1)
        high = line.astype(bf16).astype(f32)
        return jnp.where((group[:, 0] // 2) % 2 == 1, line - high, high)

    def prefix_part(b, carry):
        slots = pl.ds(pl.multiple_of(b * 8, 8), 8)
        q = stack_heads(got_ref[slots, 0:16, :].reshape(128, 128))
        info = jnp.broadcast_to(stat[slots, :][:, None, :], (8, 16, 128))
        pick = jnp.sum(jnp.where(lane == sub, info, 0.0), axis=-1, keepdims=True)
        pick = pick.reshape(128, 1) > 0.5
        pick = jnp.broadcast_to(pick, (128, 256))
        pick = jnp.concatenate([pick, pick], axis=0)
        s = jnp.where(pick, dot_t(q, pk_ref[1]), dot_t(q, pk_ref[0]))
        w, inv, lse = softmax_parts(s, None)
        none = jnp.zeros_like(w)
        o = dot(jnp.where(pick, none, w), pv_ref[0]) + dot(jnp.where(pick, w, none), pv_ref[1])
        ret_ref[slots, 0:16, :] = join_heads(o * inv).astype(bf16).reshape(8, 16, 128)
        stat[slots, :] = stat_line(lse[:128], lse[128:])
        return carry

    lax.fori_loop(0, 8, prefix_part, 0, unroll=2)
    copy.wait()

    def earlier_part(b, carry):
        slots = pl.ds(pl.multiple_of(b * 8, 8), 8)
        q = stack_heads(got_ref[slots, 16:32, :].reshape(128, 128))
        at = [pl.ds(pl.multiple_of(row_s[b * 8 + i, 16] * 16, 16), 16) for i in range(8)]
        keys = jnp.concatenate([ek_ref[x, :] for x in at], axis=0)
        values = jnp.concatenate([ev_ref[x, :] for x in at], axis=0)
        w, inv, lse = softmax_parts(dot_t(q, keys), near)
        out = join_heads(dot(w, values) * inv).reshape(8, 16, 128)
        line = jnp.where(group[:, 0] < 4, stat[slots, :], stat_line(lse[:128], lse[128:]))
        line = jnp.broadcast_to(line[:, None, :], (8, 16, 128))
        ret_ref[slots, 16:32, :] = jnp.where(sub == 15, line, out).astype(bf16)
        return carry

    lax.fori_loop(0, 8, earlier_part, 0, unroll=2)


def merge_kernel(
    scal, ret_ref, own_ref, lse_ref, out_ref, pre_o, pre_s, erl_o, erl_s, erl_on
):
    row = iota((16, 128), 0)
    lane = iota((16, 128), 1)
    diag = (lane % 16) == row

    def block(b, carry):
        for p in range(8):
            g = b * 8 + p
            rows = pl.ds(pl.multiple_of(b * 128, 128) + 16 * p, 16)
            slot, slot_e, _, late, span = pair_of(scal, g)
            pre_o[rows, :] = ret_ref[slot, 0:16, :].astype(f32)
            line = jnp.broadcast_to(ret_ref[slot, 16:32, :].astype(f32)[15:16, :], (16, 128))
            pre_s[rows, :] = jnp.where(diag & (lane < 64), line, 0.0)
            part = ret_ref[slot_e, 16:32, :].astype(f32)
            line = jnp.broadcast_to(part[15:16, :], (16, 128))
            stat = jnp.where(diag & (lane >= 64), line, 0.0)
            erl_o[rows, :] = jnp.where(late, pltpu.roll(part, 1, 0), part)
            erl_s[rows, :] = jnp.where(late, pltpu.roll(stat, 1, 0), stat)
            turn = jnp.where(late, 1, 0)
            erl_on[rows, :] = jnp.where((row < span).astype(jnp.int32) + turn == 1, 1.0, 0.0)
        rows = pl.ds(pl.multiple_of(b * 128, 128), 128)
        a = iota((128, 128), 0)
        c = iota((128, 128), 1)
        pick = (((a // 16) % 2) == (c // 64)).astype(bf16)
        l_pre = dot(pre_s[rows, :].astype(bf16), pick)
        l_erl = dot(erl_s[rows, :].astype(bf16), pick)
        on = erl_on[rows, :] > 0.5
        l_erl = jnp.where(on, l_erl, NEG)
        l_own = lse_ref[rows, :]
        top = jnp.maximum(jnp.maximum(l_own, l_pre), l_erl)
        w_own = jnp.exp(l_own - top)
        w_pre = jnp.exp(l_pre - top)
        w_erl = jnp.exp(l_erl - top)
        mixed = w_own * own_ref[rows, :] + w_pre * pre_o[rows, :]
        mixed = mixed + w_erl * jnp.where(on, erl_o[rows, :], 0.0)
        out_ref[rows, :] = (mixed / (w_own + w_pre + w_erl)).astype(bf16)
        return carry

    lax.fori_loop(0, 4, block, 0)


def norm_rows(hidden, gain, shift):
    mean = jnp.mean(hidden, axis=-1, keepdims=True)
    centred = hidden - mean
    var = jnp.mean(centred * centred, axis=-1, keepdims=True)
    return centred * lax.rsqrt(var + EPS) * gain + shift


def pack_kernel(at, up_ref, down_ref, out_ref, pack_ref):
    pack_ref[0:256, :] = up_ref[...]
    pack_ref[256:384, :] = down_ref[:, 0:512]
    pack_ref[384:512, :] = down_ref[:, 512:1024]
    pack_ref[512:544, :] = out_ref[:, 0:512]
    pack_ref[544:576, :] = out_ref[:, 512:1024]


def row_kernel(scal, own_ref, far_ref, rows_ref):
    core = scal[3, 0]
    rows = pl.ds(pl.multiple_of(scal[3, 1] * 64, 64), 64)
    for y in range(4):
        own, far = own_ref[y, rows, :], far_ref[y, rows, :]
        at = 256 * y
        rows_ref[:, at : at + 128] = jnp.where(core == 0, own, far)
        rows_ref[:, at + 128 : at + 256] = jnp.where(core == 0, far, own)


def tail_kernel(
    att_ref,
    tok_ref,
    ag_ref,
    as_ref,
    mg_ref,
    ms_ref,
    w_hbm,
    out_ref,
    acc,
    left,
    right,
    up,
    down,
    sem,
):
    first = []
    for x in range(4):
        for n, half in enumerate((left, right)):
            source = w_hbm.at[x, :, pl.ds(512 + 32 * n, 32), :]
            first.append(pltpu.make_async_copy(source, half.at[:, x], sem.at[16 + 2 * x + n]))

    def fetch(t):
        return (
            pltpu.make_async_copy(w_hbm.at[:, t, pl.ds(0, 256), :], up.at[t], sem.at[2 * t]),
            pltpu.make_async_copy(w_hbm.at[:, t, pl.ds(256, 256), :], down.at[t], sem.at[2 * t + 1]),
        )

    for copy in first:
        copy.start()
    for t in range(8):
        for copy in fetch(t):
            copy.start()
    att = jnp.concatenate([att_ref[i] for i in range(8)], axis=1)
    for copy in first:
        copy.wait()
    proj = [dot(att, half[...].reshape(1024, 512)) for half in (left, right)]
    hidden = tok_ref[...].astype(f32) + jnp.concatenate(proj, axis=1)
    normed = norm_rows(hidden, ag_ref[...], as_ref[...]).astype(bf16)
    acc[...] = normed.astype(f32)

    def block(t, carry):
        up_copy, down_copy = fetch(t)
        up_copy.wait()
        h = dot(normed, up[t].reshape(1024, 512))
        inner = (0.5 * h * (1.0 + lax.erf(h * 0.7071067811865476))).astype(bf16)
        down_copy.wait()
        for n in range(2):
            weight = down[t, :, 128 * n : 128 * n + 128, :].reshape(512, 512)
            acc[:, 512 * n : 512 * n + 512] += dot(inner, weight)
        return carry

    lax.fori_loop(0, 8, block, 0)
    done = norm_rows(acc[...], mg_ref[...], ms_ref[...]).astype(bf16)
    for i in range(8):
        out_ref[i] = done[:, 128 * i : 128 * i + 128]


def swap_all(value, axis):
    return lax.all_to_all(value, axis, split_axis=0, concat_axis=0, tiled=True)


def cost(flops, size, trans=0):
    return pl.CostEstimate(flops=flops, bytes_accessed=size, transcendentals=trans)


def local(
    tokens,
    qkv_weight,
    out_weight,
    attn_gain,
    attn_shift,
    up_weight,
    down_weight,
    mlp_gain,
    mlp_shift,
    prefix_cache,
    earlier_cache,
    suffix_len,
    prefix_id,
    earlier_slot,
):
    n_req = lax.axis_size(REQ)
    core = lax.axis_index("c")
    rank = lax.axis_index(TP)

    hbm = pl.BlockSpec(memory_space=pl.ANY)
    packed = pl.pallas_call(
        pack_kernel,
        grid_spec=pltpu.PrefetchScalarGridSpec(
            num_scalar_prefetch=1,
            grid=(1,),
            in_specs=[
                pl.BlockSpec((256, 512), lambda i, at: (at[0], 0)),
                pl.BlockSpec((128, 1024), lambda i, at: (at[0], 0)),
                pl.BlockSpec((32, 1024), lambda i, at: (at[0], 0)),
            ],
            out_specs=pl.BlockSpec((576, 512), lambda i, at: (0, 0)),
        ),
        out_shape=jax.ShapeDtypeStruct((576, 512), bf16),
        cost_estimate=cost(0, 1 << 20),
        name="pack_weights",
    )(lax.axis_index("x").reshape(1), up_weight, down_weight, out_weight)
    shards = lax.all_gather(packed, ("x", "y", "c"), axis=0, tiled=False)
    shards = shards.reshape(4, 8, 576, 512)

    own_half = swap_all(jnp.broadcast_to(tokens[None], (4, 512, 128)), "y")
    far_half = lax.ppermute(own_half, "c", [(0, 1), (1, 0)])

    place = jnp.where(jnp.arange(64) % 2 == 0, core, rank)
    scal = jnp.stack([suffix_len, prefix_id, earlier_slot, place])
    part, w_far = pl.pallas_call(
        part_kernel,
        in_specs=[SM, VM, hbm],
        out_specs=[VM, VM],
        out_shape=[
            jax.ShapeDtypeStruct((512, 384), f32),
            jax.ShapeDtypeStruct((512, 384), bf16),
        ],
        scratch_shapes=[pltpu.VMEM((512, 384), bf16), pltpu.SemaphoreType.DMA((24,))],
        compiler_params=SMALL,
        cost_estimate=cost(2 * 512 * 512 * 384, 2 << 20),
        name="qkv_own_half",
    )(scal, own_half, qkv_weight.transpose(1, 0, 2))
    send, qkv = pl.pallas_call(
        place_kernel,
        in_specs=[SM] + [VM] * 3,
        out_specs=[VM, VM],
        out_shape=[
            jax.ShapeDtypeStruct((n_req, 32, 128), bf16),
            jax.ShapeDtypeStruct((512, 384), bf16),
        ],
        compiler_params=SMALL,
        cost_estimate=cost(2 * 512 * 512 * 384, 3 << 20),
        name="qkv_place",
    )(scal, part, far_half, w_far)

    got = swap_all(send, REQ)

    own_out, own_lse = pl.pallas_call(
        own_kernel,
        in_specs=[SM, VM],
        out_specs=[VM, VM],
        out_shape=[jax.ShapeDtypeStruct((512, 128), f32)] * 2,
        compiler_params=SMALL,
        cost_estimate=cost(2 * 512 * 128 * 128 * 4, 1 << 20, 2 * 512 * 128),
        name="own_attention",
    )(scal, qkv)

    ret = pl.pallas_call(
        owner_kernel,
        in_specs=[VM] * 5,
        out_specs=VM,
        out_shape=jax.ShapeDtypeStruct((n_req, 32, 128), bf16),
        scratch_shapes=[
            pltpu.VMEM((n_req, 128), jnp.int32),
            pltpu.SMEM((n_req, 128), jnp.int32),
            pltpu.VMEM((n_req, 128), f32),
            pltpu.SemaphoreType.DMA,
        ],
        compiler_params=SMALL,
        cost_estimate=cost(2 * 1024 * 128 * 2048, 2 << 20, 2 * 1024 * 384),
        name="owner_attention",
    )(
        got,
        prefix_cache[:, :, 0],
        prefix_cache[:, :, 1],
        earlier_cache[:, :, 0].reshape(512, 128),
        earlier_cache[:, :, 1].reshape(512, 128),
    )

    back = swap_all(ret, REQ)

    attended = pl.pallas_call(
        merge_kernel,
        in_specs=[SM, VM, VM, VM],
        out_specs=VM,
        out_shape=jax.ShapeDtypeStruct((512, 128), bf16),
        scratch_shapes=[pltpu.VMEM((512, 128), f32)] * 5,
        cost_estimate=cost(2 * 512 * 128 * 256, 1 << 20, 3 * 512 * 128),
        compiler_params=SMALL,
        name="merge",
    )(scal, back, own_out, own_lse)

    att = swap_all(attended.reshape(8, 64, 128), TP)

    tok_rows = pl.pallas_call(
        row_kernel,
        in_specs=[SM, VM, VM],
        out_specs=VM,
        out_shape=jax.ShapeDtypeStruct((64, 1024), bf16),
        compiler_params=SMALL,
        cost_estimate=cost(0, 60 << 20),
        name="token_rows",
    )(scal, own_half, far_half)

    encoded = pl.pallas_call(
        tail_kernel,
        in_specs=[VM] * 6 + [hbm],
        out_specs=VM,
        out_shape=jax.ShapeDtypeStruct((8, 64, 128), bf16),
        scratch_shapes=[
            pltpu.VMEM((64, 1024), f32),
            pltpu.VMEM((8, 4, 32, 512), bf16),
            pltpu.VMEM((8, 4, 32, 512), bf16),
            pltpu.VMEM((8, 4, 256, 512), bf16),
            pltpu.VMEM((8, 4, 256, 512), bf16),
            pltpu.SemaphoreType.DMA((24,)),
        ],
        compiler_params=pltpu.CompilerParams(vmem_limit_bytes=52 << 20),
        cost_estimate=cost(2 * 64 * 9 * 1024 * 1024, 19 << 20, 64 * 4096),
        name="project_norm_ffn",
    )(
        att,
        tok_rows,
        attn_gain.reshape(1, 1024),
        attn_shift.reshape(1, 1024),
        mlp_gain.reshape(1, 1024),
        mlp_shift.reshape(1, 1024),
        shards,
    )
    return swap_all(encoded, TP).reshape(512, 128)


def solution(mesh):
    split = Mesh(mesh.devices.reshape(16, 4, 4, 2), ("z", "x", "y", "c"))
    placed = (
        P(REQ, TP),
        P(None, None, TP),
        P(TP, None),
        P(),
        P(),
        P(None, TP),
        P(TP, None),
        P(),
        P(),
        P(REQ, None, None, TP),
        P(REQ, None, None, TP),
        P(REQ),
        P(REQ),
        P(REQ),
    )
    return jax.shard_map(
        local, mesh=split, in_specs=placed, out_specs=P(REQ, TP), check_vma=False
    )
```

```python
import jax
import jax.numpy as jnp
from jax import lax
from jax.experimental import pallas as pl
from jax.experimental.pallas import tpu as pltpu
from jax.sharding import Mesh, PartitionSpec as P

HD = 64
REQ = ("z", "x")
TP = ("y", "c")
SCALE = 0.125
NEG = -1e30
EPS = 1e-05
bf16 = jnp.bfloat16
f32 = jnp.float32

VM = pl.BlockSpec(memory_space=pltpu.VMEM)
SM = pl.BlockSpec(memory_space=pltpu.SMEM)
SMALL = pltpu.CompilerParams(vmem_limit_bytes=16 << 20)


def iota(shape, axis):
    return lax.broadcasted_iota(jnp.int32, shape, axis)


def head_mask(x, h):
    lane = iota(x.shape, len(x.shape) - 1)
    return jnp.where((lane >= HD) == (h == 1), x, jnp.zeros_like(x))


def dot_t(a, b):
    return lax.dot_general(a, b, (((1,), (1,)), ((), ())), preferred_element_type=f32)


def dot(a, b):
    return jnp.dot(a, b, preferred_element_type=f32)


def softmax_parts(scores, allowed):
    masked = scores if allowed is None else jnp.where(allowed, scores, NEG)
    top = jnp.max(masked, axis=-1, keepdims=True)
    weights = jnp.exp(masked - top)
    total = jnp.sum(weights, axis=-1, keepdims=True)
    return weights.astype(bf16), 1.0 / total, top + jnp.log(total)


def half_rows(half_ref, rows):
    return jnp.concatenate([half_ref[i, rows, :] for i in range(4)], axis=1)


def part_kernel(scal, half_ref, w_ref, part_ref, far_ref, buf):
    core = scal[3, 0]
    for side, target in ((core, buf), (1 - core, far_ref)):
        for y in range(4):
            rows = pl.ds(pl.multiple_of((2 * y + side) * 128, 128), 128)
            for n in range(3):
                target[128 * y : 128 * y + 128, 128 * n : 128 * n + 128] = w_ref[n, rows, :]
    for b in range(2):
        rows = pl.ds(256 * b, 256)
        part_ref[rows, :] = dot(half_rows(half_ref, rows), buf[...])


def pair_of(scal, g):
    first, later = scal[2, 2 * g], scal[2, 2 * g + 1]
    slot = jnp.maximum(first, later)
    return scal[1, 2 * g] // 2, slot // 32, slot % 32, later >= 0, scal[0, 2 * g]


def place_kernel(scal, part_ref, half_ref, w_ref, send_ref, qkv_ref):
    row = iota((16, 128), 0)
    lane = iota((16, 128), 1)
    send_ref[...] = jnp.zeros(send_ref.shape, bf16)

    def block(b, carry):
        rows = pl.ds(pl.multiple_of(b * 128, 128), 128)
        out = part_ref[rows, :] + dot(half_rows(half_ref, rows), w_ref[...])
        qkv_ref[rows, :] = out.astype(bf16)
        q = out[:, :128].astype(bf16)
        for p in range(8):
            g = b * 8 + p
            slot, slot_e, row_e, late, span = pair_of(scal, g)
            qp = q[16 * p : 16 * p + 16]
            send_ref[slot, 0:16, :] = qp
            pick = jnp.where(lane < span, scal[1, 2 * g] % 2, scal[1, 2 * g + 1] % 2)
            pick = jnp.where((row == 15) & (lane < 16), pick, 0).astype(f32)
            held = send_ref[slot, 16:32, :].astype(f32)
            send_ref[slot, 16:32, :] = (held + pick).astype(bf16)
            qf = qp.astype(f32)
            moved = jnp.where(late, pltpu.roll(qf, 15, 0), qf)
            held = send_ref[slot_e, 16:32, :].astype(f32)
            held = jnp.where(lane == 16, (row_e + 1).astype(f32), held)
            send_ref[slot_e, 16:32, :] = jnp.where(row == 15, held, moved).astype(bf16)
        return carry

    lax.fori_loop(0, 4, block, 0, unroll=4)


def own_kernel(scal, qkv_ref, out_ref, lse_ref):
    r = iota((128, 128), 0)
    c = iota((128, 128), 1)

    def block(b, carry):
        rows = pl.ds(pl.multiple_of(b * 128, 128), 128)
        q = qkv_ref[rows, 0:128]
        k = qkv_ref[rows, 128:256]
        v = qkv_ref[rows, 256:384]
        span = jnp.concatenate(
            [jnp.full((16, 128), scal[0, 2 * (b * 8 + p)], jnp.int32) for p in range(8)], axis=0
        )
        same = ((r // 16) == (c // 16)) & (c <= r) & (((r % 16) < span) == ((c % 16) < span))
        res = []
        for h in range(2):
            w, inv, lse = softmax_parts(dot_t(head_mask(q, h), k) * SCALE, same)
            res.append((dot(w, v) * inv, jnp.broadcast_to(lse, (128, 128))))
        out_ref[rows, :] = head_mask(res[0][0], 0) + head_mask(res[1][0], 1)
        lse_ref[rows, :] = head_mask(res[0][1], 0) + head_mask(res[1][1], 1)
        return carry

    lax.fori_loop(0, 4, block, 0)


def stack_heads(q):
    q = q * jnp.asarray(SCALE, q.dtype)
    return jnp.concatenate([head_mask(q, 0), head_mask(q, 1)], axis=0)


def join_heads(x):
    n = x.shape[0] // 2
    return head_mask(x[:n], 0) + head_mask(x[n:], 1)


def owner_kernel(got_ref, pk_ref, pv_ref, ek_ref, ev_ref, ret_ref, row_v, row_s, stat, sem):
    sub = iota((8, 16, 128), 1)
    lane = iota((8, 16, 128), 2)
    group = lane // 16
    r = iota((256, 128), 0)
    c = iota((256, 128), 1)
    near = ((r % 128) // 16) == (c // 16)

    for b in range(8):
        line = got_ref[8 * b : 8 * b + 8, 16:32, :].astype(f32)[:, 15:16, :].reshape(8, 128)
        stat[8 * b : 8 * b + 8, :] = line
        row_v[8 * b : 8 * b + 8, :] = jnp.maximum(line - 1.0, 0.0).astype(jnp.int32)
    copy = pltpu.make_async_copy(row_v, row_s, sem)
    copy.start()

    def stat_line(first, second):
        both = jnp.where(group % 2 == 0, first.reshape(8, 16, 1), second.reshape(8, 16, 1))
        line = jnp.sum(jnp.where(lane % 16 == sub, both, 0.0), axis=1)
        high = line.astype(bf16).astype(f32)
        return jnp.where((group[:, 0] // 2) % 2 == 1, line - high, high)

    def prefix_part(b, carry):
        slots = pl.ds(pl.multiple_of(b * 8, 8), 8)
        q = stack_heads(got_ref[slots, 0:16, :].reshape(128, 128))
        info = jnp.broadcast_to(stat[slots, :][:, None, :], (8, 16, 128))
        pick = jnp.sum(jnp.where(lane == sub, info, 0.0), axis=-1, keepdims=True)
        pick = pick.reshape(128, 1) > 0.5
        pick = jnp.broadcast_to(pick, (128, 256))
        pick = jnp.concatenate([pick, pick], axis=0)
        s = jnp.where(pick, dot_t(q, pk_ref[1]), dot_t(q, pk_ref[0]))
        w, inv, lse = softmax_parts(s, None)
        none = jnp.zeros_like(w)
        o = dot(jnp.where(pick, none, w), pv_ref[0]) + dot(jnp.where(pick, w, none), pv_ref[1])
        ret_ref[slots, 0:16, :] = join_heads(o * inv).astype(bf16).reshape(8, 16, 128)
        stat[slots, :] = stat_line(lse[:128], lse[128:])
        return carry

    lax.fori_loop(0, 8, prefix_part, 0, unroll=8)
    copy.wait()

    def earlier_part(b, carry):
        slots = pl.ds(pl.multiple_of(b * 8, 8), 8)
        q = stack_heads(got_ref[slots, 16:32, :].reshape(128, 128))
        at = [pl.ds(pl.multiple_of(row_s[b * 8 + i, 16] * 16, 16), 16) for i in range(8)]
        keys = jnp.concatenate([ek_ref[x, :] for x in at], axis=0)
        values = jnp.concatenate([ev_ref[x, :] for x in at], axis=0)
        w, inv, lse = softmax_parts(dot_t(q, keys), near)
        out = join_heads(dot(w, values) * inv).reshape(8, 16, 128)
        line = jnp.where(group[:, 0] < 4, stat[slots, :], stat_line(lse[:128], lse[128:]))
        line = jnp.broadcast_to(line[:, None, :], (8, 16, 128))
        ret_ref[slots, 16:32, :] = jnp.where(sub == 15, line, out).astype(bf16)
        return carry

    lax.fori_loop(0, 8, earlier_part, 0, unroll=8)


def merge_kernel(
    scal, ret_ref, own_ref, lse_ref, out_ref, pre_o, pre_s, erl_o, erl_s, erl_on
):
    row = iota((16, 128), 0)
    lane = iota((16, 128), 1)
    diag = (lane % 16) == row

    def block(b, carry):
        for p in range(8):
            g = b * 8 + p
            rows = pl.ds(pl.multiple_of(b * 128, 128) + 16 * p, 16)
            slot, slot_e, _, late, span = pair_of(scal, g)
            pre_o[rows, :] = ret_ref[slot, 0:16, :].astype(f32)
            line = jnp.broadcast_to(ret_ref[slot, 16:32, :].astype(f32)[15:16, :], (16, 128))
            pre_s[rows, :] = jnp.where(diag & (lane < 64), line, 0.0)
            part = ret_ref[slot_e, 16:32, :].astype(f32)
            line = jnp.broadcast_to(part[15:16, :], (16, 128))
            stat = jnp.where(diag & (lane >= 64), line, 0.0)
            erl_o[rows, :] = jnp.where(late, pltpu.roll(part, 1, 0), part)
            erl_s[rows, :] = jnp.where(late, pltpu.roll(stat, 1, 0), stat)
            turn = jnp.where(late, 1, 0)
            erl_on[rows, :] = jnp.where((row < span).astype(jnp.int32) + turn == 1, 1.0, 0.0)
        rows = pl.ds(pl.multiple_of(b * 128, 128), 128)
        a = iota((128, 128), 0)
        c = iota((128, 128), 1)
        pick = (((a // 16) % 2) == (c // 64)).astype(bf16)
        l_pre = dot(pre_s[rows, :].astype(bf16), pick)
        l_erl = dot(erl_s[rows, :].astype(bf16), pick)
        on = erl_on[rows, :] > 0.5
        l_erl = jnp.where(on, l_erl, NEG)
        l_own = lse_ref[rows, :]
        top = jnp.maximum(jnp.maximum(l_own, l_pre), l_erl)
        w_own = jnp.exp(l_own - top)
        w_pre = jnp.exp(l_pre - top)
        w_erl = jnp.exp(l_erl - top)
        mixed = w_own * own_ref[rows, :] + w_pre * pre_o[rows, :]
        mixed = mixed + w_erl * jnp.where(on, erl_o[rows, :], 0.0)
        out_ref[rows, :] = (mixed / (w_own + w_pre + w_erl)).astype(bf16)
        return carry

    lax.fori_loop(0, 4, block, 0, unroll=4)


def norm_rows(hidden, gain, shift):
    mean = jnp.mean(hidden, axis=-1, keepdims=True)
    centred = hidden - mean
    var = jnp.mean(centred * centred, axis=-1, keepdims=True)
    return centred * lax.rsqrt(var + EPS) * gain + shift


def pack_kernel(at, up_ref, down_ref, out_ref, pack_ref):
    pack_ref[0:256, :] = up_ref[...]
    pack_ref[256:384, :] = down_ref[:, 0:512]
    pack_ref[384:512, :] = down_ref[:, 512:1024]
    pack_ref[512:544, :] = out_ref[:, 0:512]
    pack_ref[544:576, :] = out_ref[:, 512:1024]


def row_kernel(scal, own_ref, far_ref, rows_ref):
    core = scal[3, 0]
    rows = pl.ds(pl.multiple_of(scal[3, 1] * 64, 64), 64)
    for y in range(4):
        own, far = own_ref[y, rows, :], far_ref[y, rows, :]
        at = 256 * y
        rows_ref[:, at : at + 128] = jnp.where(core == 0, own, far)
        rows_ref[:, at + 128 : at + 256] = jnp.where(core == 0, far, own)


def stage_kernel(w_hbm, left, right, sem):
    copies = []
    for x in range(4):
        for n, half in enumerate((left, right)):
            source = w_hbm.at[x, :, pl.ds(512 + 32 * n, 32), :]
            copies.append(pltpu.make_async_copy(source, half.at[:, x], sem.at[2 * x + n]))
    for copy in copies:
        copy.start()
    for copy in copies:
        copy.wait()


def tail_kernel(
    att_ref,
    tok_ref,
    ag_ref,
    as_ref,
    mg_ref,
    ms_ref,
    left,
    right,
    w_hbm,
    out_ref,
    acc,
    up,
    down,
    sem,
):
    def fetch(t):
        return (
            pltpu.make_async_copy(w_hbm.at[:, t, pl.ds(0, 256), :], up.at[t], sem.at[2 * t]),
            pltpu.make_async_copy(w_hbm.at[:, t, pl.ds(256, 256), :], down.at[t], sem.at[2 * t + 1]),
        )

    for t in range(8):
        for copy in fetch(t):
            copy.start()
    att = jnp.concatenate([att_ref[i] for i in range(8)], axis=1)
    proj = [dot(att, half[...].reshape(1024, 512)) for half in (left, right)]
    hidden = tok_ref[...].astype(f32) + jnp.concatenate(proj, axis=1)
    normed = norm_rows(hidden, ag_ref[...], as_ref[...]).astype(bf16)
    acc[...] = normed.astype(f32)

    def block(t, carry):
        up_copy, down_copy = fetch(t)
        up_copy.wait()
        h = dot(normed, up[t].reshape(1024, 512))
        inner = (0.5 * h * (1.0 + lax.erf(h * 0.7071067811865476))).astype(bf16)
        down_copy.wait()
        for n in range(2):
            weight = down[t, :, 128 * n : 128 * n + 128, :].reshape(512, 512)
            acc[:, 512 * n : 512 * n + 512] += dot(inner, weight)
        return carry

    lax.fori_loop(0, 8, block, 0, unroll=2)
    done = norm_rows(acc[...], mg_ref[...], ms_ref[...]).astype(bf16)
    for i in range(8):
        out_ref[i] = done[:, 128 * i : 128 * i + 128]


def swap_all(value, axis):
    return lax.all_to_all(value, axis, split_axis=0, concat_axis=0, tiled=True)


def cost(flops, size, trans=0):
    return pl.CostEstimate(flops=flops, bytes_accessed=size, transcendentals=trans)


def local(
    tokens,
    qkv_weight,
    out_weight,
    attn_gain,
    attn_shift,
    up_weight,
    down_weight,
    mlp_gain,
    mlp_shift,
    prefix_cache,
    earlier_cache,
    suffix_len,
    prefix_id,
    earlier_slot,
):
    n_req = lax.axis_size(REQ)
    core = lax.axis_index("c")
    rank = lax.axis_index(TP)

    hbm = pl.BlockSpec(memory_space=pl.ANY)
    packed = pl.pallas_call(
        pack_kernel,
        grid_spec=pltpu.PrefetchScalarGridSpec(
            num_scalar_prefetch=1,
            grid=(1,),
            in_specs=[
                pl.BlockSpec((256, 512), lambda i, at: (at[0], 0)),
                pl.BlockSpec((128, 1024), lambda i, at: (at[0], 0)),
                pl.BlockSpec((32, 1024), lambda i, at: (at[0], 0)),
            ],
            out_specs=pl.BlockSpec((576, 512), lambda i, at: (0, 0)),
        ),
        out_shape=jax.ShapeDtypeStruct((576, 512), bf16),
        cost_estimate=cost(0, 1 << 20),
        name="pack_weights",
    )(lax.axis_index("x").reshape(1), up_weight, down_weight, out_weight)
    shards = lax.all_gather(packed, ("x", "y", "c"), axis=0, tiled=False)
    shards = shards.reshape(4, 8, 576, 512)

    own_half = swap_all(jnp.broadcast_to(tokens[None], (4, 512, 128)), "y")
    far_half = lax.ppermute(own_half, "c", [(0, 1), (1, 0)])

    place = jnp.where(jnp.arange(64) % 2 == 0, core, rank)
    scal = jnp.stack([suffix_len, prefix_id, earlier_slot, place])
    part, w_far = pl.pallas_call(
        part_kernel,
        in_specs=[SM, VM, VM],
        out_specs=[VM, VM],
        out_shape=[
            jax.ShapeDtypeStruct((512, 384), f32),
            jax.ShapeDtypeStruct((512, 384), bf16),
        ],
        scratch_shapes=[pltpu.VMEM((512, 384), bf16)],
        compiler_params=SMALL,
        cost_estimate=cost(2 * 512 * 512 * 384, 2 << 20),
        name="qkv_own_half",
    )(scal, own_half, qkv_weight.transpose(1, 0, 2))
    send, qkv = pl.pallas_call(
        place_kernel,
        in_specs=[SM] + [VM] * 3,
        out_specs=[VM, VM],
        out_shape=[
            jax.ShapeDtypeStruct((n_req, 32, 128), bf16),
            jax.ShapeDtypeStruct((512, 384), bf16),
        ],
        compiler_params=SMALL,
        cost_estimate=cost(2 * 512 * 512 * 384, 3 << 20),
        name="qkv_place",
    )(scal, part, far_half, w_far)

    got = swap_all(send, REQ)

    own_out, own_lse = pl.pallas_call(
        own_kernel,
        in_specs=[SM, VM],
        out_specs=[VM, VM],
        out_shape=[jax.ShapeDtypeStruct((512, 128), f32)] * 2,
        compiler_params=SMALL,
        cost_estimate=cost(2 * 512 * 128 * 128 * 4, 1 << 20, 2 * 512 * 128),
        name="own_attention",
    )(scal, qkv)

    ret = pl.pallas_call(
        owner_kernel,
        in_specs=[VM] * 5,
        out_specs=VM,
        out_shape=jax.ShapeDtypeStruct((n_req, 32, 128), bf16),
        scratch_shapes=[
            pltpu.VMEM((n_req, 128), jnp.int32),
            pltpu.SMEM((n_req, 128), jnp.int32),
            pltpu.VMEM((n_req, 128), f32),
            pltpu.SemaphoreType.DMA,
        ],
        compiler_params=SMALL,
        cost_estimate=cost(2 * 1024 * 128 * 2048, 2 << 20, 2 * 1024 * 384),
        name="owner_attention",
    )(
        got,
        prefix_cache[:, :, 0],
        prefix_cache[:, :, 1],
        earlier_cache[:, :, 0].reshape(512, 128),
        earlier_cache[:, :, 1].reshape(512, 128),
    )

    back = swap_all(ret, REQ)

    attended = pl.pallas_call(
        merge_kernel,
        in_specs=[SM, VM, VM, VM],
        out_specs=VM,
        out_shape=jax.ShapeDtypeStruct((512, 128), bf16),
        scratch_shapes=[pltpu.VMEM((512, 128), f32)] * 5,
        cost_estimate=cost(2 * 512 * 128 * 256, 1 << 20, 3 * 512 * 128),
        compiler_params=SMALL,
        name="merge",
    )(scal, back, own_out, own_lse)

    att = swap_all(attended.reshape(8, 64, 128), TP)

    tok_rows = pl.pallas_call(
        row_kernel,
        in_specs=[SM, VM, VM],
        out_specs=VM,
        out_shape=jax.ShapeDtypeStruct((64, 1024), bf16),
        compiler_params=SMALL,
        cost_estimate=cost(0, 60 << 20),
        name="token_rows",
    )(scal, own_half, far_half)

    halves = pl.pallas_call(
        stage_kernel,
        in_specs=[hbm],
        out_specs=[VM] * 2,
        out_shape=[jax.ShapeDtypeStruct((8, 4, 32, 512), bf16)] * 2,
        scratch_shapes=[pltpu.SemaphoreType.DMA((8,))],
        compiler_params=pltpu.CompilerParams(vmem_limit_bytes=48 << 20),
        cost_estimate=cost(0, 4 << 20),
        name="stage_out_weight",
    )(shards)
    encoded = pl.pallas_call(
        tail_kernel,
        in_specs=[VM] * 8 + [hbm],
        out_specs=VM,
        out_shape=jax.ShapeDtypeStruct((8, 64, 128), bf16),
        scratch_shapes=[
            pltpu.VMEM((64, 1024), f32),
            pltpu.VMEM((8, 4, 256, 512), bf16),
            pltpu.VMEM((8, 4, 256, 512), bf16),
            pltpu.SemaphoreType.DMA((16,)),
        ],
        compiler_params=pltpu.CompilerParams(vmem_limit_bytes=52 << 20),
        cost_estimate=cost(2 * 64 * 9 * 1024 * 1024, 19 << 20, 64 * 4096),
        name="project_norm_ffn",
    )(
        att,
        tok_rows,
        attn_gain.reshape(1, 1024),
        attn_shift.reshape(1, 1024),
        mlp_gain.reshape(1, 1024),
        mlp_shift.reshape(1, 1024),
        *halves,
        shards,
    )
    return swap_all(encoded, TP).reshape(512, 128)


def solution(mesh):
    split = Mesh(mesh.devices.reshape(16, 4, 4, 2), ("z", "x", "y", "c"))
    placed = (
        P(REQ, TP),
        P(None, None, TP),
        P(TP, None),
        P(),
        P(),
        P(None, TP),
        P(TP, None),
        P(),
        P(),
        P(REQ, None, None, TP),
        P(REQ, None, None, TP),
        P(REQ),
        P(REQ),
        P(REQ),
    )
    return jax.shard_map(
        local, mesh=split, in_specs=placed, out_specs=P(REQ, TP), check_vma=False
    )
```

```python
import jax
import jax.numpy as jnp
from jax import lax
from jax.experimental import pallas as pl
from jax.experimental.pallas import tpu as pltpu
from jax.sharding import Mesh, PartitionSpec as P

HD = 64
REQ = ("z", "x")
TP = ("y", "c")
SCALE = 0.125
NEG = -1e30
EPS = 1e-05
bf16 = jnp.bfloat16
f32 = jnp.float32

VM = pl.BlockSpec(memory_space=pltpu.VMEM)
SM = pl.BlockSpec(memory_space=pltpu.SMEM)
SMALL = pltpu.CompilerParams(vmem_limit_bytes=16 << 20)


def iota(shape, axis):
    return lax.broadcasted_iota(jnp.int32, shape, axis)


def head_mask(x, h):
    lane = iota(x.shape, len(x.shape) - 1)
    return jnp.where((lane >= HD) == (h == 1), x, jnp.zeros_like(x))


def dot_t(a, b):
    return lax.dot_general(a, b, (((1,), (1,)), ((), ())), preferred_element_type=f32)


def dot(a, b):
    return jnp.dot(a, b, preferred_element_type=f32)


def softmax_parts(scores, allowed):
    masked = scores if allowed is None else jnp.where(allowed, scores, NEG)
    top = jnp.max(masked, axis=-1, keepdims=True)
    weights = jnp.exp(masked - top)
    total = jnp.sum(weights, axis=-1, keepdims=True)
    return weights.astype(bf16), 1.0 / total, top + jnp.log(total)


def half_rows(half_ref, rows):
    return jnp.concatenate([half_ref[i, rows, :] for i in range(4)], axis=1)


def order_kernel(scal, w_ref, own_ref, far_ref):
    core = scal[3, 0]
    for side, target in ((core, own_ref), (1 - core, far_ref)):
        for y in range(4):
            rows = pl.ds(pl.multiple_of((2 * y + side) * 128, 128), 128)
            for n in range(3):
                target[128 * y : 128 * y + 128, 128 * n : 128 * n + 128] = w_ref[n, rows, :]


def part_kernel(half_ref, w_ref, part_ref):
    for b in range(2):
        rows = pl.ds(256 * b, 256)
        part_ref[rows, :] = dot(half_rows(half_ref, rows), w_ref[...])


def pair_of(scal, g):
    first, later = scal[2, 2 * g], scal[2, 2 * g + 1]
    slot = jnp.maximum(first, later)
    return scal[1, 2 * g] // 2, slot // 32, slot % 32, later >= 0, scal[0, 2 * g]


def place_kernel(scal, part_ref, half_ref, w_ref, send_ref, qkv_ref):
    row = iota((16, 128), 0)
    lane = iota((16, 128), 1)
    send_ref[...] = jnp.zeros(send_ref.shape, bf16)

    def block(b, carry):
        rows = pl.ds(pl.multiple_of(b * 128, 128), 128)
        out = part_ref[rows, :] + dot(half_rows(half_ref, rows), w_ref[...])
        qkv_ref[rows, :] = out.astype(bf16)
        q = out[:, :128].astype(bf16)
        for p in range(8):
            g = b * 8 + p
            slot, slot_e, row_e, late, span = pair_of(scal, g)
            qp = q[16 * p : 16 * p + 16]
            send_ref[slot, 0:16, :] = qp
            pick = jnp.where(lane < span, scal[1, 2 * g] % 2, scal[1, 2 * g + 1] % 2)
            pick = jnp.where((row == 15) & (lane < 16), pick, 0).astype(f32)
            held = send_ref[slot, 16:32, :].astype(f32)
            send_ref[slot, 16:32, :] = (held + pick).astype(bf16)
            qf = qp.astype(f32)
            moved = jnp.where(late, pltpu.roll(qf, 15, 0), qf)
            held = send_ref[slot_e, 16:32, :].astype(f32)
            held = jnp.where(lane == 16, (row_e + 1).astype(f32), held)
            send_ref[slot_e, 16:32, :] = jnp.where(row == 15, held, moved).astype(bf16)
        return carry

    lax.fori_loop(0, 4, block, 0, unroll=4)


def own_kernel(scal, qkv_ref, out_ref, lse_ref):
    r = iota((128, 128), 0)
    c = iota((128, 128), 1)

    def block(b, carry):
        rows = pl.ds(pl.multiple_of(b * 128, 128), 128)
        q = qkv_ref[rows, 0:128]
        k = qkv_ref[rows, 128:256]
        v = qkv_ref[rows, 256:384]
        span = jnp.concatenate(
            [jnp.full((16, 128), scal[0, 2 * (b * 8 + p)], jnp.int32) for p in range(8)], axis=0
        )
        same = ((r // 16) == (c // 16)) & (c <= r) & (((r % 16) < span) == ((c % 16) < span))
        res = []
        for h in range(2):
            w, inv, lse = softmax_parts(dot_t(head_mask(q, h), k) * SCALE, same)
            res.append((dot(w, v) * inv, jnp.broadcast_to(lse, (128, 128))))
        out_ref[rows, :] = head_mask(res[0][0], 0) + head_mask(res[1][0], 1)
        lse_ref[rows, :] = head_mask(res[0][1], 0) + head_mask(res[1][1], 1)
        return carry

    lax.fori_loop(0, 4, block, 0)


def stack_heads(q):
    q = q * jnp.asarray(SCALE, q.dtype)
    return jnp.concatenate([head_mask(q, 0), head_mask(q, 1)], axis=0)


def join_heads(x):
    n = x.shape[0] // 2
    return head_mask(x[:n], 0) + head_mask(x[n:], 1)


def owner_kernel(got_ref, pk_ref, pv_ref, ek_ref, ev_ref, ret_ref, row_v, row_s, stat, sem):
    sub = iota((8, 16, 128), 1)
    lane = iota((8, 16, 128), 2)
    group = lane // 16
    r = iota((256, 128), 0)
    c = iota((256, 128), 1)
    near = ((r % 128) // 16) == (c // 16)

    for b in range(8):
        line = got_ref[8 * b : 8 * b + 8, 16:32, :].astype(f32)[:, 15:16, :].reshape(8, 128)
        stat[8 * b : 8 * b + 8, :] = line
        row_v[8 * b : 8 * b + 8, :] = jnp.maximum(line - 1.0, 0.0).astype(jnp.int32)
    copy = pltpu.make_async_copy(row_v, row_s, sem)
    copy.start()

    def stat_line(first, second):
        both = jnp.where(group % 2 == 0, first.reshape(8, 16, 1), second.reshape(8, 16, 1))
        line = jnp.sum(jnp.where(lane % 16 == sub, both, 0.0), axis=1)
        high = line.astype(bf16).astype(f32)
        return jnp.where((group[:, 0] // 2) % 2 == 1, line - high, high)

    def prefix_part(b, carry):
        slots = pl.ds(pl.multiple_of(b * 8, 8), 8)
        q = stack_heads(got_ref[slots, 0:16, :].reshape(128, 128))
        info = jnp.broadcast_to(stat[slots, :][:, None, :], (8, 16, 128))
        pick = jnp.sum(jnp.where(lane == sub, info, 0.0), axis=-1, keepdims=True)
        pick = pick.reshape(128, 1) > 0.5
        pick = jnp.broadcast_to(pick, (128, 256))
        pick = jnp.concatenate([pick, pick], axis=0)
        s = jnp.where(pick, dot_t(q, pk_ref[1]), dot_t(q, pk_ref[0]))
        w, inv, lse = softmax_parts(s, None)
        none = jnp.zeros_like(w)
        o = dot(jnp.where(pick, none, w), pv_ref[0]) + dot(jnp.where(pick, w, none), pv_ref[1])
        ret_ref[slots, 0:16, :] = join_heads(o * inv).astype(bf16).reshape(8, 16, 128)
        stat[slots, :] = stat_line(lse[:128], lse[128:])
        return carry

    lax.fori_loop(0, 8, prefix_part, 0, unroll=8)
    copy.wait()

    def earlier_part(b, carry):
        slots = pl.ds(pl.multiple_of(b * 8, 8), 8)
        q = stack_heads(got_ref[slots, 16:32, :].reshape(128, 128))
        at = [pl.ds(pl.multiple_of(row_s[b * 8 + i, 16] * 16, 16), 16) for i in range(8)]
        keys = jnp.concatenate([ek_ref[x, :] for x in at], axis=0)
        values = jnp.concatenate([ev_ref[x, :] for x in at], axis=0)
        w, inv, lse = softmax_parts(dot_t(q, keys), near)
        out = join_heads(dot(w, values) * inv).reshape(8, 16, 128)
        line = jnp.where(group[:, 0] < 4, stat[slots, :], stat_line(lse[:128], lse[128:]))
        line = jnp.broadcast_to(line[:, None, :], (8, 16, 128))
        ret_ref[slots, 16:32, :] = jnp.where(sub == 15, line, out).astype(bf16)
        return carry

    lax.fori_loop(0, 8, earlier_part, 0, unroll=8)


def merge_kernel(
    scal, ret_ref, own_ref, lse_ref, out_ref, pre_o, pre_s, erl_o, erl_s, erl_on
):
    row = iota((16, 128), 0)
    lane = iota((16, 128), 1)
    diag = (lane % 16) == row

    def block(b, carry):
        for p in range(8):
            g = b * 8 + p
            rows = pl.ds(pl.multiple_of(b * 128, 128) + 16 * p, 16)
            slot, slot_e, _, late, span = pair_of(scal, g)
            pre_o[rows, :] = ret_ref[slot, 0:16, :].astype(f32)
            line = jnp.broadcast_to(ret_ref[slot, 16:32, :].astype(f32)[15:16, :], (16, 128))
            pre_s[rows, :] = jnp.where(diag & (lane < 64), line, 0.0)
            part = ret_ref[slot_e, 16:32, :].astype(f32)
            line = jnp.broadcast_to(part[15:16, :], (16, 128))
            stat = jnp.where(diag & (lane >= 64), line, 0.0)
            erl_o[rows, :] = jnp.where(late, pltpu.roll(part, 1, 0), part)
            erl_s[rows, :] = jnp.where(late, pltpu.roll(stat, 1, 0), stat)
            turn = jnp.where(late, 1, 0)
            erl_on[rows, :] = jnp.where((row < span).astype(jnp.int32) + turn == 1, 1.0, 0.0)
        rows = pl.ds(pl.multiple_of(b * 128, 128), 128)
        a = iota((128, 128), 0)
        c = iota((128, 128), 1)
        pick = (((a // 16) % 2) == (c // 64)).astype(bf16)
        l_pre = dot(pre_s[rows, :].astype(bf16), pick)
        l_erl = dot(erl_s[rows, :].astype(bf16), pick)
        on = erl_on[rows, :] > 0.5
        l_erl = jnp.where(on, l_erl, NEG)
        l_own = lse_ref[rows, :]
        top = jnp.maximum(jnp.maximum(l_own, l_pre), l_erl)
        w_own = jnp.exp(l_own - top)
        w_pre = jnp.exp(l_pre - top)
        w_erl = jnp.exp(l_erl - top)
        mixed = w_own * own_ref[rows, :] + w_pre * pre_o[rows, :]
        mixed = mixed + w_erl * jnp.where(on, erl_o[rows, :], 0.0)
        out_ref[rows, :] = (mixed / (w_own + w_pre + w_erl)).astype(bf16)
        return carry

    lax.fori_loop(0, 4, block, 0, unroll=4)


def norm_rows(hidden, gain, shift):
    mean = jnp.mean(hidden, axis=-1, keepdims=True)
    centred = hidden - mean
    var = jnp.mean(centred * centred, axis=-1, keepdims=True)
    return centred * lax.rsqrt(var + EPS) * gain + shift


def pack_kernel(at, up_ref, down_ref, out_ref, pack_ref):
    pack_ref[0:256, :] = up_ref[...]
    pack_ref[256:384, :] = down_ref[:, 0:512]
    pack_ref[384:512, :] = down_ref[:, 512:1024]
    pack_ref[512:544, :] = out_ref[:, 0:512]
    pack_ref[544:576, :] = out_ref[:, 512:1024]


def row_kernel(scal, own_ref, far_ref, rows_ref):
    core = scal[3, 0]
    rows = pl.ds(pl.multiple_of(scal[3, 1] * 64, 64), 64)
    for y in range(4):
        own, far = own_ref[y, rows, :], far_ref[y, rows, :]
        at = 256 * y
        rows_ref[:, at : at + 128] = jnp.where(core == 0, own, far)
        rows_ref[:, at + 128 : at + 256] = jnp.where(core == 0, far, own)


def tail_kernel(
    att_ref,
    tok_ref,
    ag_ref,
    as_ref,
    mg_ref,
    ms_ref,
    w_hbm,
    out_ref,
    acc,
    left,
    right,
    up,
    down,
    sem,
):
    first = []
    for x in range(4):
        for n, half in enumerate((left, right)):
            source = w_hbm.at[x, :, pl.ds(512 + 32 * n, 32), :]
            first.append(pltpu.make_async_copy(source, half.at[:, x], sem.at[16 + 2 * x + n]))

    def fetch(t):
        return (
            pltpu.make_async_copy(w_hbm.at[:, t, pl.ds(0, 256), :], up.at[t], sem.at[2 * t]),
            pltpu.make_async_copy(w_hbm.at[:, t, pl.ds(256, 256), :], down.at[t], sem.at[2 * t + 1]),
        )

    for copy in first:
        copy.start()
    for t in range(8):
        for copy in fetch(t):
            copy.start()
    att = jnp.concatenate([att_ref[i] for i in range(8)], axis=1)
    for copy in first:
        copy.wait()
    proj = [dot(att, half[...].reshape(1024, 512)) for half in (left, right)]
    hidden = tok_ref[...].astype(f32) + jnp.concatenate(proj, axis=1)
    normed = norm_rows(hidden, ag_ref[...], as_ref[...]).astype(bf16)
    acc[...] = normed.astype(f32)

    def block(t, carry):
        up_copy, down_copy = fetch(t)
        up_copy.wait()
        h = dot(normed, up[t].reshape(1024, 512))
        inner = (0.5 * h * (1.0 + lax.erf(h * 0.7071067811865476))).astype(bf16)
        down_copy.wait()
        for n in range(2):
            weight = down[t, :, 128 * n : 128 * n + 128, :].reshape(512, 512)
            acc[:, 512 * n : 512 * n + 512] += dot(inner, weight)
        return carry

    lax.fori_loop(0, 8, block, 0, unroll=2)
    done = norm_rows(acc[...], mg_ref[...], ms_ref[...]).astype(bf16)
    for i in range(8):
        out_ref[i] = done[:, 128 * i : 128 * i + 128]


def swap_all(value, axis):
    return lax.all_to_all(value, axis, split_axis=0, concat_axis=0, tiled=True)


def cost(flops, size, trans=0):
    return pl.CostEstimate(flops=flops, bytes_accessed=size, transcendentals=trans)


def local(
    tokens,
    qkv_weight,
    out_weight,
    attn_gain,
    attn_shift,
    up_weight,
    down_weight,
    mlp_gain,
    mlp_shift,
    prefix_cache,
    earlier_cache,
    suffix_len,
    prefix_id,
    earlier_slot,
):
    n_req = lax.axis_size(REQ)
    core = lax.axis_index("c")
    rank = lax.axis_index(TP)

    place = jnp.where(jnp.arange(64) % 2 == 0, core, rank)
    scal = jnp.stack([suffix_len, prefix_id, earlier_slot, place])
    w_own, w_far = pl.pallas_call(
        order_kernel,
        in_specs=[SM, VM],
        out_specs=[VM, VM],
        out_shape=[jax.ShapeDtypeStruct((512, 384), bf16)] * 2,
        compiler_params=SMALL,
        cost_estimate=cost(0, 2 << 20),
        name="order_qkv_weight",
    )(scal, qkv_weight.transpose(1, 0, 2))

    hbm = pl.BlockSpec(memory_space=pl.ANY)
    packed = pl.pallas_call(
        pack_kernel,
        grid_spec=pltpu.PrefetchScalarGridSpec(
            num_scalar_prefetch=1,
            grid=(1,),
            in_specs=[
                pl.BlockSpec((256, 512), lambda i, at: (at[0], 0)),
                pl.BlockSpec((128, 1024), lambda i, at: (at[0], 0)),
                pl.BlockSpec((32, 1024), lambda i, at: (at[0], 0)),
            ],
            out_specs=pl.BlockSpec((576, 512), lambda i, at: (0, 0)),
        ),
        out_shape=jax.ShapeDtypeStruct((576, 512), bf16),
        compiler_params=SMALL,
        cost_estimate=cost(0, 1 << 20),
        name="pack_weights",
    )(lax.axis_index("x").reshape(1), up_weight, down_weight, out_weight)

    own_half = swap_all(jnp.broadcast_to(tokens[None], (4, 512, 128)), "y")
    own_half, scal, w_own, w_far, packed = lax.optimization_barrier(
        (own_half, scal, w_own, w_far, packed)
    )
    shards = lax.all_gather(packed, ("x", "y", "c"), axis=0, tiled=False)
    shards = shards.reshape(4, 8, 576, 512)

    far_half = lax.ppermute(own_half, "c", [(0, 1), (1, 0)])

    part = pl.pallas_call(
        part_kernel,
        in_specs=[VM, VM],
        out_specs=VM,
        out_shape=jax.ShapeDtypeStruct((512, 384), f32),
        compiler_params=SMALL,
        cost_estimate=cost(2 * 512 * 512 * 384, 2 << 20),
        name="qkv_own_half",
    )(own_half, w_own)
    send, qkv = pl.pallas_call(
        place_kernel,
        in_specs=[SM] + [VM] * 3,
        out_specs=[VM, VM],
        out_shape=[
            jax.ShapeDtypeStruct((n_req, 32, 128), bf16),
            jax.ShapeDtypeStruct((512, 384), bf16),
        ],
        compiler_params=SMALL,
        cost_estimate=cost(2 * 512 * 512 * 384, 3 << 20),
        name="qkv_place",
    )(scal, part, far_half, w_far)

    got = swap_all(send, REQ)

    own_out, own_lse = pl.pallas_call(
        own_kernel,
        in_specs=[SM, VM],
        out_specs=[VM, VM],
        out_shape=[jax.ShapeDtypeStruct((512, 128), f32)] * 2,
        compiler_params=SMALL,
        cost_estimate=cost(2 * 512 * 128 * 128 * 4, 1 << 20, 2 * 512 * 128),
        name="own_attention",
    )(scal, qkv)

    ret = pl.pallas_call(
        owner_kernel,
        in_specs=[VM] * 5,
        out_specs=VM,
        out_shape=jax.ShapeDtypeStruct((n_req, 32, 128), bf16),
        scratch_shapes=[
            pltpu.VMEM((n_req, 128), jnp.int32),
            pltpu.SMEM((n_req, 128), jnp.int32),
            pltpu.VMEM((n_req, 128), f32),
            pltpu.SemaphoreType.DMA,
        ],
        compiler_params=SMALL,
        cost_estimate=cost(2 * 1024 * 128 * 2048, 2 << 20, 2 * 1024 * 384),
        name="owner_attention",
    )(
        got,
        prefix_cache[:, :, 0],
        prefix_cache[:, :, 1],
        earlier_cache[:, :, 0].reshape(512, 128),
        earlier_cache[:, :, 1].reshape(512, 128),
    )

    back = swap_all(ret, REQ)

    attended = pl.pallas_call(
        merge_kernel,
        in_specs=[SM, VM, VM, VM],
        out_specs=VM,
        out_shape=jax.ShapeDtypeStruct((512, 128), bf16),
        scratch_shapes=[pltpu.VMEM((512, 128), f32)] * 5,
        cost_estimate=cost(2 * 512 * 128 * 256, 1 << 20, 3 * 512 * 128),
        compiler_params=SMALL,
        name="merge",
    )(scal, back, own_out, own_lse)

    att = swap_all(attended.reshape(8, 64, 128), TP)

    tok_rows = pl.pallas_call(
        row_kernel,
        in_specs=[SM, VM, VM],
        out_specs=VM,
        out_shape=jax.ShapeDtypeStruct((64, 1024), bf16),
        compiler_params=SMALL,
        cost_estimate=cost(0, 60 << 20),
        name="token_rows",
    )(scal, own_half, far_half)

    encoded = pl.pallas_call(
        tail_kernel,
        in_specs=[VM] * 6 + [hbm],
        out_specs=VM,
        out_shape=jax.ShapeDtypeStruct((8, 64, 128), bf16),
        scratch_shapes=[
            pltpu.VMEM((64, 1024), f32),
            pltpu.VMEM((8, 4, 32, 512), bf16),
            pltpu.VMEM((8, 4, 32, 512), bf16),
            pltpu.VMEM((8, 4, 256, 512), bf16),
            pltpu.VMEM((8, 4, 256, 512), bf16),
            pltpu.SemaphoreType.DMA((24,)),
        ],
        compiler_params=pltpu.CompilerParams(vmem_limit_bytes=52 << 20),
        cost_estimate=cost(2 * 64 * 9 * 1024 * 1024, 19 << 20, 64 * 4096),
        name="project_norm_ffn",
    )(
        att,
        tok_rows,
        attn_gain.reshape(1, 1024),
        attn_shift.reshape(1, 1024),
        mlp_gain.reshape(1, 1024),
        mlp_shift.reshape(1, 1024),
        shards,
    )
    return swap_all(encoded, TP).reshape(512, 128)


def solution(mesh):
    split = Mesh(mesh.devices.reshape(16, 4, 4, 2), ("z", "x", "y", "c"))
    placed = (
        P(REQ, TP),
        P(None, None, TP),
        P(TP, None),
        P(),
        P(),
        P(None, TP),
        P(TP, None),
        P(),
        P(),
        P(REQ, None, None, TP),
        P(REQ, None, None, TP),
        P(REQ),
        P(REQ),
        P(REQ),
    )
    return jax.shard_map(
        local, mesh=split, in_specs=placed, out_specs=P(REQ, TP), check_vma=False
    )
```

```python
import jax
import jax.numpy as jnp
from jax import lax
from jax.experimental import pallas as pl
from jax.experimental.pallas import tpu as pltpu
from jax.sharding import Mesh, PartitionSpec as P

HD = 64
REQ = ("z", "x")
TP = ("y", "c")
SCALE = 0.125
NEG = -1e30
EPS = 1e-05
bf16 = jnp.bfloat16
f32 = jnp.float32

VM = pl.BlockSpec(memory_space=pltpu.VMEM)
SM = pl.BlockSpec(memory_space=pltpu.SMEM)
SMALL = pltpu.CompilerParams(vmem_limit_bytes=16 << 20)


def iota(shape, axis):
    return lax.broadcasted_iota(jnp.int32, shape, axis)


def head_mask(x, h):
    lane = iota(x.shape, len(x.shape) - 1)
    return jnp.where((lane >= HD) == (h == 1), x, jnp.zeros_like(x))


def dot_t(a, b):
    return lax.dot_general(a, b, (((1,), (1,)), ((), ())), preferred_element_type=f32)


def dot(a, b):
    return jnp.dot(a, b, preferred_element_type=f32)


def softmax_parts(scores, allowed):
    masked = scores if allowed is None else jnp.where(allowed, scores, NEG)
    top = jnp.max(masked, axis=-1, keepdims=True)
    weights = jnp.exp(masked - top)
    total = jnp.sum(weights, axis=-1, keepdims=True)
    return weights.astype(bf16), 1.0 / total, top + jnp.log(total)


def half_rows(half_ref, rows):
    return jnp.concatenate([half_ref[i, rows, :] for i in range(4)], axis=1)


def order_kernel(scal, w_ref, own_ref, far_ref):
    core = scal[3, 0]
    for side, target in ((core, own_ref), (1 - core, far_ref)):
        for y in range(4):
            rows = pl.ds(pl.multiple_of((2 * y + side) * 128, 128), 128)
            for n in range(3):
                target[128 * y : 128 * y + 128, 128 * n : 128 * n + 128] = w_ref[n, rows, :]


def part_kernel(half_ref, w_ref, part_ref):
    for b in range(2):
        rows = pl.ds(256 * b, 256)
        part_ref[rows, :] = dot(half_rows(half_ref, rows), w_ref[...])


def pair_of(scal, g):
    first, later = scal[2, 2 * g], scal[2, 2 * g + 1]
    slot = jnp.maximum(first, later)
    return scal[1, 2 * g] // 2, slot // 32, slot % 32, later >= 0, scal[0, 2 * g]


def place_kernel(scal, part_ref, half_ref, w_ref, send_ref, qkv_ref):
    row = iota((16, 128), 0)
    lane = iota((16, 128), 1)
    send_ref[...] = jnp.zeros(send_ref.shape, bf16)

    def block(b, carry):
        rows = pl.ds(pl.multiple_of(b * 128, 128), 128)
        out = part_ref[rows, :] + dot(half_rows(half_ref, rows), w_ref[...])
        qkv_ref[rows, :] = out.astype(bf16)
        q = out[:, :128].astype(bf16)
        for p in range(8):
            g = b * 8 + p
            slot, slot_e, row_e, late, span = pair_of(scal, g)
            qp = q[16 * p : 16 * p + 16]
            send_ref[slot, 0:16, :] = qp
            pick = jnp.where(lane < span, scal[1, 2 * g] % 2, scal[1, 2 * g + 1] % 2)
            pick = jnp.where((row == 15) & (lane < 16), pick, 0).astype(f32)
            held = send_ref[slot, 16:32, :].astype(f32)
            send_ref[slot, 16:32, :] = (held + pick).astype(bf16)
            qf = qp.astype(f32)
            moved = jnp.where(late, pltpu.roll(qf, 15, 0), qf)
            held = send_ref[slot_e, 16:32, :].astype(f32)
            held = jnp.where(lane == 16, (row_e + 1).astype(f32), held)
            send_ref[slot_e, 16:32, :] = jnp.where(row == 15, held, moved).astype(bf16)
        return carry

    lax.fori_loop(0, 4, block, 0, unroll=4)


def own_kernel(scal, qkv_ref, out_ref, lse_ref):
    r = iota((128, 128), 0)
    c = iota((128, 128), 1)

    def block(b, carry):
        rows = pl.ds(pl.multiple_of(b * 128, 128), 128)
        q = qkv_ref[rows, 0:128]
        k = qkv_ref[rows, 128:256]
        v = qkv_ref[rows, 256:384]
        span = jnp.concatenate(
            [jnp.full((16, 128), scal[0, 2 * (b * 8 + p)], jnp.int32) for p in range(8)], axis=0
        )
        same = ((r // 16) == (c // 16)) & (c <= r) & (((r % 16) < span) == ((c % 16) < span))
        res = []
        for h in range(2):
            w, inv, lse = softmax_parts(dot_t(head_mask(q, h), k) * SCALE, same)
            res.append((dot(w, v) * inv, jnp.broadcast_to(lse, (128, 128))))
        out_ref[rows, :] = head_mask(res[0][0], 0) + head_mask(res[1][0], 1)
        lse_ref[rows, :] = head_mask(res[0][1], 0) + head_mask(res[1][1], 1)
        return carry

    lax.fori_loop(0, 4, block, 0)


def stack_heads(q):
    q = q * jnp.asarray(SCALE, q.dtype)
    return jnp.concatenate([head_mask(q, 0), head_mask(q, 1)], axis=0)


def join_heads(x):
    n = x.shape[0] // 2
    return head_mask(x[:n], 0) + head_mask(x[n:], 1)


def owner_kernel(got_ref, pk_ref, pv_ref, ek_ref, ev_ref, ret_ref, row_v, row_s, stat, sem):
    sub = iota((8, 16, 128), 1)
    lane = iota((8, 16, 128), 2)
    group = lane // 16
    r = iota((256, 128), 0)
    c = iota((256, 128), 1)
    near = ((r % 128) // 16) == (c // 16)

    for b in range(8):
        line = got_ref[8 * b : 8 * b + 8, 16:32, :].astype(f32)[:, 15:16, :].reshape(8, 128)
        stat[8 * b : 8 * b + 8, :] = line
        row_v[8 * b : 8 * b + 8, :] = jnp.maximum(line - 1.0, 0.0).astype(jnp.int32)
    copy = pltpu.make_async_copy(row_v, row_s, sem)
    copy.start()

    def stat_line(first, second):
        both = jnp.where(group % 2 == 0, first.reshape(8, 16, 1), second.reshape(8, 16, 1))
        line = jnp.sum(jnp.where(lane % 16 == sub, both, 0.0), axis=1)
        high = line.astype(bf16).astype(f32)
        return jnp.where((group[:, 0] // 2) % 2 == 1, line - high, high)

    def prefix_part(b, carry):
        slots = pl.ds(pl.multiple_of(b * 8, 8), 8)
        q = stack_heads(got_ref[slots, 0:16, :].reshape(128, 128))
        info = jnp.broadcast_to(stat[slots, :][:, None, :], (8, 16, 128))
        pick = jnp.sum(jnp.where(lane == sub, info, 0.0), axis=-1, keepdims=True)
        pick = pick.reshape(128, 1) > 0.5
        pick = jnp.broadcast_to(pick, (128, 256))
        pick = jnp.concatenate([pick, pick], axis=0)
        s = jnp.where(pick, dot_t(q, pk_ref[1]), dot_t(q, pk_ref[0]))
        w, inv, lse = softmax_parts(s, None)
        none = jnp.zeros_like(w)
        o = dot(jnp.where(pick, none, w), pv_ref[0]) + dot(jnp.where(pick, w, none), pv_ref[1])
        ret_ref[slots, 0:16, :] = join_heads(o * inv).astype(bf16).reshape(8, 16, 128)
        stat[slots, :] = stat_line(lse[:128], lse[128:])
        return carry

    lax.fori_loop(0, 8, prefix_part, 0, unroll=8)
    copy.wait()

    def earlier_part(b, carry):
        slots = pl.ds(pl.multiple_of(b * 8, 8), 8)
        q = stack_heads(got_ref[slots, 16:32, :].reshape(128, 128))
        at = [pl.ds(pl.multiple_of(row_s[b * 8 + i, 16] * 16, 16), 16) for i in range(8)]
        keys = jnp.concatenate([ek_ref[x, :] for x in at], axis=0)
        values = jnp.concatenate([ev_ref[x, :] for x in at], axis=0)
        w, inv, lse = softmax_parts(dot_t(q, keys), near)
        out = join_heads(dot(w, values) * inv).reshape(8, 16, 128)
        line = jnp.where(group[:, 0] < 4, stat[slots, :], stat_line(lse[:128], lse[128:]))
        line = jnp.broadcast_to(line[:, None, :], (8, 16, 128))
        ret_ref[slots, 16:32, :] = jnp.where(sub == 15, line, out).astype(bf16)
        return carry

    lax.fori_loop(0, 8, earlier_part, 0, unroll=8)


def merge_kernel(
    scal, ret_ref, own_ref, lse_ref, out_ref, pre_o, pre_s, erl_o, erl_s, erl_on
):
    row = iota((16, 128), 0)
    lane = iota((16, 128), 1)
    diag = (lane % 16) == row

    def block(b, carry):
        for p in range(8):
            g = b * 8 + p
            rows = pl.ds(pl.multiple_of(b * 128, 128) + 16 * p, 16)
            slot, slot_e, _, late, span = pair_of(scal, g)
            pre_o[rows, :] = ret_ref[slot, 0:16, :].astype(f32)
            line = jnp.broadcast_to(ret_ref[slot, 16:32, :].astype(f32)[15:16, :], (16, 128))
            pre_s[rows, :] = jnp.where(diag & (lane < 64), line, 0.0)
            part = ret_ref[slot_e, 16:32, :].astype(f32)
            line = jnp.broadcast_to(part[15:16, :], (16, 128))
            stat = jnp.where(diag & (lane >= 64), line, 0.0)
            erl_o[rows, :] = jnp.where(late, pltpu.roll(part, 1, 0), part)
            erl_s[rows, :] = jnp.where(late, pltpu.roll(stat, 1, 0), stat)
            turn = jnp.where(late, 1, 0)
            erl_on[rows, :] = jnp.where((row < span).astype(jnp.int32) + turn == 1, 1.0, 0.0)
        rows = pl.ds(pl.multiple_of(b * 128, 128), 128)
        a = iota((128, 128), 0)
        c = iota((128, 128), 1)
        pick = (((a // 16) % 2) == (c // 64)).astype(bf16)
        l_pre = dot(pre_s[rows, :].astype(bf16), pick)
        l_erl = dot(erl_s[rows, :].astype(bf16), pick)
        on = erl_on[rows, :] > 0.5
        l_erl = jnp.where(on, l_erl, NEG)
        l_own = lse_ref[rows, :]
        top = jnp.maximum(jnp.maximum(l_own, l_pre), l_erl)
        w_own = jnp.exp(l_own - top)
        w_pre = jnp.exp(l_pre - top)
        w_erl = jnp.exp(l_erl - top)
        mixed = w_own * own_ref[rows, :] + w_pre * pre_o[rows, :]
        mixed = mixed + w_erl * jnp.where(on, erl_o[rows, :], 0.0)
        out_ref[rows, :] = (mixed / (w_own + w_pre + w_erl)).astype(bf16)
        return carry

    lax.fori_loop(0, 4, block, 0, unroll=4)


def norm_rows(hidden, gain, shift):
    mean = jnp.mean(hidden, axis=-1, keepdims=True)
    centred = hidden - mean
    var = jnp.mean(centred * centred, axis=-1, keepdims=True)
    return centred * lax.rsqrt(var + EPS) * gain + shift


def pack_kernel(at, up_ref, down_ref, out_ref, pack_ref):
    pack_ref[0:256, :] = up_ref[...]
    pack_ref[256:384, :] = down_ref[:, 0:512]
    pack_ref[384:512, :] = down_ref[:, 512:1024]
    pack_ref[512:544, :] = out_ref[:, 0:512]
    pack_ref[544:576, :] = out_ref[:, 512:1024]


def row_kernel(scal, own_ref, far_ref, rows_ref):
    core = scal[3, 0]
    rows = pl.ds(pl.multiple_of(scal[3, 1] * 64, 64), 64)
    for y in range(4):
        own, far = own_ref[y, rows, :], far_ref[y, rows, :]
        at = 256 * y
        rows_ref[:, at : at + 128] = jnp.where(core == 0, own, far)
        rows_ref[:, at + 128 : at + 256] = jnp.where(core == 0, far, own)


def tail_kernel(
    att_ref,
    tok_ref,
    ag_ref,
    as_ref,
    mg_ref,
    ms_ref,
    w_hbm,
    out_ref,
    acc,
    left,
    right,
    up,
    down,
    sem,
):
    first = []
    for x in range(4):
        for n, half in enumerate((left, right)):
            source = w_hbm.at[x, :, pl.ds(512 + 32 * n, 32), :]
            first.append(pltpu.make_async_copy(source, half.at[:, x], sem.at[16 + 2 * x + n]))

    def fetch(t):
        return (
            pltpu.make_async_copy(w_hbm.at[:, t, pl.ds(0, 256), :], up.at[t], sem.at[2 * t]),
            pltpu.make_async_copy(w_hbm.at[:, t, pl.ds(256, 256), :], down.at[t], sem.at[2 * t + 1]),
        )

    for copy in first:
        copy.start()
    for t in range(8):
        for copy in fetch(t):
            copy.start()
    att = jnp.concatenate([att_ref[i] for i in range(8)], axis=1)
    for copy in first:
        copy.wait()
    proj = [dot(att, half[...].reshape(1024, 512)) for half in (left, right)]
    hidden = tok_ref[...].astype(f32) + jnp.concatenate(proj, axis=1)
    normed = norm_rows(hidden, ag_ref[...], as_ref[...]).astype(bf16)
    acc[...] = normed.astype(f32)

    def block(t, carry):
        up_copy, down_copy = fetch(t)
        up_copy.wait()
        h = dot(normed, up[t].reshape(1024, 512))
        inner = (0.5 * h * (1.0 + lax.erf(h * 0.7071067811865476))).astype(bf16)
        down_copy.wait()
        for n in range(2):
            weight = down[t, :, 128 * n : 128 * n + 128, :].reshape(512, 512)
            acc[:, 512 * n : 512 * n + 512] += dot(inner, weight)
        return carry

    lax.fori_loop(0, 8, block, 0, unroll=2)
    done = norm_rows(acc[...], mg_ref[...], ms_ref[...]).astype(bf16)
    for i in range(8):
        out_ref[i] = done[:, 128 * i : 128 * i + 128]


def swap_all(value, axis):
    return lax.all_to_all(value, axis, split_axis=0, concat_axis=0, tiled=True)


def cost(flops, size, trans=0):
    return pl.CostEstimate(flops=flops, bytes_accessed=size, transcendentals=trans)


def local(
    tokens,
    qkv_weight,
    out_weight,
    attn_gain,
    attn_shift,
    up_weight,
    down_weight,
    mlp_gain,
    mlp_shift,
    prefix_cache,
    earlier_cache,
    suffix_len,
    prefix_id,
    earlier_slot,
):
    n_req = lax.axis_size(REQ)
    core = lax.axis_index("c")
    rank = lax.axis_index(TP)

    place = jnp.where(jnp.arange(64) % 2 == 0, core, rank)
    scal = jnp.stack([suffix_len, prefix_id, earlier_slot, place])
    hbm = pl.BlockSpec(memory_space=pl.ANY)
    packed = pl.pallas_call(
        pack_kernel,
        grid_spec=pltpu.PrefetchScalarGridSpec(
            num_scalar_prefetch=1,
            grid=(1,),
            in_specs=[
                pl.BlockSpec((256, 512), lambda i, at: (at[0], 0)),
                pl.BlockSpec((128, 1024), lambda i, at: (at[0], 0)),
                pl.BlockSpec((32, 1024), lambda i, at: (at[0], 0)),
            ],
            out_specs=pl.BlockSpec((576, 512), lambda i, at: (0, 0)),
        ),
        out_shape=jax.ShapeDtypeStruct((576, 512), bf16),
        compiler_params=pltpu.CompilerParams(vmem_limit_bytes=61 << 20),
        cost_estimate=cost(0, 1 << 20),
        name="pack_weights",
    )(lax.axis_index("x").reshape(1), up_weight, down_weight, out_weight)
    scal, packed = lax.optimization_barrier((scal, packed))
    w_own, w_far = pl.pallas_call(
        order_kernel,
        in_specs=[SM, VM],
        out_specs=[VM, VM],
        out_shape=[jax.ShapeDtypeStruct((512, 384), bf16)] * 2,
        compiler_params=SMALL,
        cost_estimate=cost(0, 2 << 20),
        name="order_qkv_weight",
    )(scal, qkv_weight.transpose(1, 0, 2))

    own_half = swap_all(jnp.broadcast_to(tokens[None], (4, 512, 128)), "y")
    own_half, scal, w_own, w_far, packed = lax.optimization_barrier(
        (own_half, scal, w_own, w_far, packed)
    )
    shards = lax.all_gather(packed, ("x", "y", "c"), axis=0, tiled=False)
    shards = shards.reshape(4, 8, 576, 512)

    far_half = lax.ppermute(own_half, "c", [(0, 1), (1, 0)])

    part = pl.pallas_call(
        part_kernel,
        in_specs=[VM, VM],
        out_specs=VM,
        out_shape=jax.ShapeDtypeStruct((512, 384), f32),
        compiler_params=SMALL,
        cost_estimate=cost(2 * 512 * 512 * 384, 2 << 20),
        name="qkv_own_half",
    )(own_half, w_own)
    send, qkv = pl.pallas_call(
        place_kernel,
        in_specs=[SM] + [VM] * 3,
        out_specs=[VM, VM],
        out_shape=[
            jax.ShapeDtypeStruct((n_req, 32, 128), bf16),
            jax.ShapeDtypeStruct((512, 384), bf16),
        ],
        compiler_params=SMALL,
        cost_estimate=cost(2 * 512 * 512 * 384, 3 << 20),
        name="qkv_place",
    )(scal, part, far_half, w_far)

    got = swap_all(send, REQ)

    own_out, own_lse = pl.pallas_call(
        own_kernel,
        in_specs=[SM, VM],
        out_specs=[VM, VM],
        out_shape=[jax.ShapeDtypeStruct((512, 128), f32)] * 2,
        compiler_params=SMALL,
        cost_estimate=cost(2 * 512 * 128 * 128 * 4, 1 << 20, 2 * 512 * 128),
        name="own_attention",
    )(scal, qkv)

    ret = pl.pallas_call(
        owner_kernel,
        in_specs=[VM] * 5,
        out_specs=VM,
        out_shape=jax.ShapeDtypeStruct((n_req, 32, 128), bf16),
        scratch_shapes=[
            pltpu.VMEM((n_req, 128), jnp.int32),
            pltpu.SMEM((n_req, 128), jnp.int32),
            pltpu.VMEM((n_req, 128), f32),
            pltpu.SemaphoreType.DMA,
        ],
        compiler_params=SMALL,
        cost_estimate=cost(2 * 1024 * 128 * 2048, 2 << 20, 2 * 1024 * 384),
        name="owner_attention",
    )(
        got,
        prefix_cache[:, :, 0],
        prefix_cache[:, :, 1],
        earlier_cache[:, :, 0].reshape(512, 128),
        earlier_cache[:, :, 1].reshape(512, 128),
    )

    back = swap_all(ret, REQ)

    attended = pl.pallas_call(
        merge_kernel,
        in_specs=[SM, VM, VM, VM],
        out_specs=VM,
        out_shape=jax.ShapeDtypeStruct((512, 128), bf16),
        scratch_shapes=[pltpu.VMEM((512, 128), f32)] * 5,
        cost_estimate=cost(2 * 512 * 128 * 256, 1 << 20, 3 * 512 * 128),
        compiler_params=SMALL,
        name="merge",
    )(scal, back, own_out, own_lse)

    att = swap_all(attended.reshape(8, 64, 128), TP)

    tok_rows = pl.pallas_call(
        row_kernel,
        in_specs=[SM, VM, VM],
        out_specs=VM,
        out_shape=jax.ShapeDtypeStruct((64, 1024), bf16),
        compiler_params=SMALL,
        cost_estimate=cost(0, 60 << 20),
        name="token_rows",
    )(scal, own_half, far_half)

    encoded = pl.pallas_call(
        tail_kernel,
        in_specs=[VM] * 6 + [hbm],
        out_specs=VM,
        out_shape=jax.ShapeDtypeStruct((8, 64, 128), bf16),
        scratch_shapes=[
            pltpu.VMEM((64, 1024), f32),
            pltpu.VMEM((8, 4, 32, 512), bf16),
            pltpu.VMEM((8, 4, 32, 512), bf16),
            pltpu.VMEM((8, 4, 256, 512), bf16),
            pltpu.VMEM((8, 4, 256, 512), bf16),
            pltpu.SemaphoreType.DMA((24,)),
        ],
        compiler_params=pltpu.CompilerParams(vmem_limit_bytes=52 << 20),
        cost_estimate=cost(2 * 64 * 9 * 1024 * 1024, 19 << 20, 64 * 4096),
        name="project_norm_ffn",
    )(
        att,
        tok_rows,
        attn_gain.reshape(1, 1024),
        attn_shift.reshape(1, 1024),
        mlp_gain.reshape(1, 1024),
        mlp_shift.reshape(1, 1024),
        shards,
    )
    return swap_all(encoded, TP).reshape(512, 128)


def solution(mesh):
    split = Mesh(mesh.devices.reshape(16, 4, 4, 2), ("z", "x", "y", "c"))
    placed = (
        P(REQ, TP),
        P(None, None, TP),
        P(TP, None),
        P(),
        P(),
        P(None, TP),
        P(TP, None),
        P(),
        P(),
        P(REQ, None, None, TP),
        P(REQ, None, None, TP),
        P(REQ),
        P(REQ),
        P(REQ),
    )
    return jax.shard_map(
        local, mesh=split, in_specs=placed, out_specs=P(REQ, TP), check_vma=False
    )
```

```python
import jax
import jax.numpy as jnp
from jax import lax
from jax.experimental import pallas as pl
from jax.experimental.pallas import tpu as pltpu
from jax.sharding import Mesh, PartitionSpec as P

HD = 64
REQ = ("z", "x")
TP = ("y", "c")
SCALE = 0.125
NEG = -1e30
EPS = 1e-05
bf16 = jnp.bfloat16
f32 = jnp.float32

VM = pl.BlockSpec(memory_space=pltpu.VMEM)
SM = pl.BlockSpec(memory_space=pltpu.SMEM)
SMALL = pltpu.CompilerParams(vmem_limit_bytes=16 << 20)


def iota(shape, axis):
    return lax.broadcasted_iota(jnp.int32, shape, axis)


def head_mask(x, h):
    lane = iota(x.shape, len(x.shape) - 1)
    return jnp.where((lane >= HD) == (h == 1), x, jnp.zeros_like(x))


def dot_t(a, b):
    return lax.dot_general(a, b, (((1,), (1,)), ((), ())), preferred_element_type=f32)


def dot(a, b):
    return jnp.dot(a, b, preferred_element_type=f32)


def softmax_parts(scores, allowed):
    masked = scores if allowed is None else jnp.where(allowed, scores, NEG)
    top = jnp.max(masked, axis=-1, keepdims=True)
    weights = jnp.exp(masked - top)
    total = jnp.sum(weights, axis=-1, keepdims=True)
    return weights.astype(bf16), 1.0 / total, top + jnp.log(total)


def half_rows(half_ref, rows):
    return jnp.concatenate([half_ref[i, rows, :] for i in range(4)], axis=1)


def order_kernel(scal, w_ref, own_ref, far_ref):
    core = scal[3, 0]
    for side, target in ((core, own_ref), (1 - core, far_ref)):
        for y in range(4):
            rows = pl.ds(pl.multiple_of((2 * y + side) * 128, 128), 128)
            for n in range(3):
                target[128 * y : 128 * y + 128, 128 * n : 128 * n + 128] = w_ref[n, rows, :]


def part_kernel(half_ref, w_ref, part_ref):
    for b in range(2):
        rows = pl.ds(256 * b, 256)
        part_ref[rows, :] = dot(half_rows(half_ref, rows), w_ref[...])


def pair_of(scal, g):
    first, later = scal[2, 2 * g], scal[2, 2 * g + 1]
    slot = jnp.maximum(first, later)
    return scal[1, 2 * g] // 2, slot // 32, slot % 32, later >= 0, scal[0, 2 * g]


def place_kernel(scal, part_ref, half_ref, w_ref, send_ref, qkv_ref):
    row = iota((16, 128), 0)
    lane = iota((16, 128), 1)
    send_ref[...] = jnp.zeros(send_ref.shape, bf16)

    def block(b, carry):
        rows = pl.ds(pl.multiple_of(b * 128, 128), 128)
        out = part_ref[rows, :] + dot(half_rows(half_ref, rows), w_ref[...])
        qkv_ref[rows, :] = out.astype(bf16)
        q = out[:, :128].astype(bf16)
        for p in range(8):
            g = b * 8 + p
            slot, slot_e, row_e, late, span = pair_of(scal, g)
            qp = q[16 * p : 16 * p + 16]
            send_ref[slot, 0:16, :] = qp
            pick = jnp.where(lane < span, scal[1, 2 * g] % 2, scal[1, 2 * g + 1] % 2)
            pick = jnp.where((row == 15) & (lane < 16), pick, 0).astype(f32)
            held = send_ref[slot, 16:32, :].astype(f32)
            send_ref[slot, 16:32, :] = (held + pick).astype(bf16)
            qf = qp.astype(f32)
            moved = jnp.where(late, pltpu.roll(qf, 15, 0), qf)
            held = send_ref[slot_e, 16:32, :].astype(f32)
            held = jnp.where(lane == 16, (row_e + 1).astype(f32), held)
            send_ref[slot_e, 16:32, :] = jnp.where(row == 15, held, moved).astype(bf16)
        return carry

    lax.fori_loop(0, 4, block, 0, unroll=4)


def own_kernel(scal, qkv_ref, out_ref, lse_ref):
    r = iota((128, 128), 0)
    c = iota((128, 128), 1)

    def block(b, carry):
        rows = pl.ds(pl.multiple_of(b * 128, 128), 128)
        q = qkv_ref[rows, 0:128]
        k = qkv_ref[rows, 128:256]
        v = qkv_ref[rows, 256:384]
        span = jnp.concatenate(
            [jnp.full((16, 128), scal[0, 2 * (b * 8 + p)], jnp.int32) for p in range(8)], axis=0
        )
        same = ((r // 16) == (c // 16)) & (c <= r) & (((r % 16) < span) == ((c % 16) < span))
        res = []
        for h in range(2):
            w, inv, lse = softmax_parts(dot_t(head_mask(q, h), k) * SCALE, same)
            res.append((dot(w, v) * inv, jnp.broadcast_to(lse, (128, 128))))
        out_ref[rows, :] = head_mask(res[0][0], 0) + head_mask(res[1][0], 1)
        lse_ref[rows, :] = head_mask(res[0][1], 0) + head_mask(res[1][1], 1)
        return carry

    lax.fori_loop(0, 4, block, 0)


def stack_heads(q):
    q = q * jnp.asarray(SCALE, q.dtype)
    return jnp.concatenate([head_mask(q, 0), head_mask(q, 1)], axis=0)


def with_ones(v, h):
    lane = iota(v.shape, 1)
    return jnp.where((lane >= HD) == (h == 1), v, jnp.ones_like(v))


def finish_heads(top, first, second):
    n = first.shape[0]
    low = iota((n, 128), 1) < HD
    total = pltpu.roll(jnp.where(low, second, first), HD, 1)
    lse = jnp.where(low, top[:n], top[n:]) + jnp.log(total)
    return jnp.where(low, first, second) / total, lse


def owner_kernel(got_ref, pk_ref, pv_ref, ek_ref, ev_ref, ret_ref, row_v, row_s, stat, sem):
    sub = iota((8, 16, 128), 1)
    lane = iota((8, 16, 128), 2)
    group = lane // 16
    r = iota((256, 128), 0)
    c = iota((256, 128), 1)
    near = ((r % 128) // 16) == (c // 16)

    for b in range(8):
        line = got_ref[8 * b : 8 * b + 8, 16:32, :].astype(f32)[:, 15:16, :].reshape(8, 128)
        stat[8 * b : 8 * b + 8, :] = line
        row_v[8 * b : 8 * b + 8, :] = jnp.maximum(line - 1.0, 0.0).astype(jnp.int32)
    copy = pltpu.make_async_copy(row_v, row_s, sem)
    copy.start()

    def stat_line(lse):
        line = jnp.sum(jnp.where(lane % 16 == sub, lse.reshape(8, 16, 128), 0.0), axis=1)
        high = line.astype(bf16).astype(f32)
        return jnp.where(group[:, 0] % 2 == 1, line - high, high)

    values = [[with_ones(pv_ref[p], h) for h in range(2)] for p in range(2)]

    def prefix_part(b, carry):
        slots = pl.ds(pl.multiple_of(b * 8, 8), 8)
        q = stack_heads(got_ref[slots, 0:16, :].reshape(128, 128))
        info = jnp.broadcast_to(stat[slots, :][:, None, :], (8, 16, 128))
        pick = jnp.sum(jnp.where(lane == sub, info, 0.0), axis=-1, keepdims=True)
        pick = pick.reshape(128, 1) > 0.5
        pick = jnp.broadcast_to(pick, (128, 256))
        pick = jnp.concatenate([pick, pick], axis=0)
        s = jnp.where(pick, dot_t(q, pk_ref[1]), dot_t(q, pk_ref[0]))
        top = jnp.max(s, axis=-1, keepdims=True)
        w = jnp.exp(s - top).astype(bf16)
        none = jnp.zeros_like(w)
        w0, w1 = jnp.where(pick, none, w), jnp.where(pick, w, none)
        parts = [
            dot(w0[n : n + 128], values[0][h]) + dot(w1[n : n + 128], values[1][h])
            for h, n in enumerate((0, 128))
        ]
        out, lse = finish_heads(top, *parts)
        ret_ref[slots, 0:16, :] = out.astype(bf16).reshape(8, 16, 128)
        stat[slots, :] = stat_line(lse)
        return carry

    lax.fori_loop(0, 8, prefix_part, 0, unroll=8)
    copy.wait()

    def earlier_part(b, carry):
        slots = pl.ds(pl.multiple_of(b * 8, 8), 8)
        q = stack_heads(got_ref[slots, 16:32, :].reshape(128, 128))
        at = [pl.ds(pl.multiple_of(row_s[b * 8 + i, 16] * 16, 16), 16) for i in range(8)]
        keys = jnp.concatenate([ek_ref[x, :] for x in at], axis=0)
        rows = jnp.concatenate([ev_ref[x, :] for x in at], axis=0)
        s = jnp.where(near, dot_t(q, keys), NEG)
        top = jnp.max(s, axis=-1, keepdims=True)
        w = jnp.exp(s - top).astype(bf16)
        parts = [dot(w[n : n + 128], with_ones(rows, h)) for h, n in enumerate((0, 128))]
        out, lse = finish_heads(top, *parts)
        out = out.reshape(8, 16, 128)
        line = jnp.where(group[:, 0] % 4 < 2, stat[slots, :], stat_line(lse))
        line = jnp.broadcast_to(line[:, None, :], (8, 16, 128))
        ret_ref[slots, 16:32, :] = jnp.where(sub == 15, line, out).astype(bf16)
        return carry

    lax.fori_loop(0, 8, earlier_part, 0, unroll=8)


def merge_kernel(
    scal, ret_ref, own_ref, lse_ref, out_ref, pre_o, pre_s, erl_o, erl_s, erl_on
):
    row = iota((16, 128), 0)
    lane = iota((16, 128), 1)
    diag = (lane % 16) == row

    def block(b, carry):
        for p in range(8):
            g = b * 8 + p
            rows = pl.ds(pl.multiple_of(b * 128, 128) + 16 * p, 16)
            slot, slot_e, _, late, span = pair_of(scal, g)
            pre_o[rows, :] = ret_ref[slot, 0:16, :].astype(f32)
            line = jnp.broadcast_to(ret_ref[slot, 16:32, :].astype(f32)[15:16, :], (16, 128))
            pre_s[rows, :] = jnp.where(diag & ((lane // 32) % 2 == 0), line, 0.0)
            part = ret_ref[slot_e, 16:32, :].astype(f32)
            line = jnp.broadcast_to(part[15:16, :], (16, 128))
            stat = jnp.where(diag & ((lane // 32) % 2 == 1), line, 0.0)
            erl_o[rows, :] = jnp.where(late, pltpu.roll(part, 1, 0), part)
            erl_s[rows, :] = jnp.where(late, pltpu.roll(stat, 1, 0), stat)
            turn = jnp.where(late, 1, 0)
            erl_on[rows, :] = jnp.where((row < span).astype(jnp.int32) + turn == 1, 1.0, 0.0)
        rows = pl.ds(pl.multiple_of(b * 128, 128), 128)
        a = iota((128, 128), 0)
        c = iota((128, 128), 1)
        pick = ((a // 64) == (c // 64)).astype(bf16)
        l_pre = dot(pre_s[rows, :].astype(bf16), pick)
        l_erl = dot(erl_s[rows, :].astype(bf16), pick)
        on = erl_on[rows, :] > 0.5
        l_erl = jnp.where(on, l_erl, NEG)
        l_own = lse_ref[rows, :]
        top = jnp.maximum(jnp.maximum(l_own, l_pre), l_erl)
        w_own = jnp.exp(l_own - top)
        w_pre = jnp.exp(l_pre - top)
        w_erl = jnp.exp(l_erl - top)
        mixed = w_own * own_ref[rows, :] + w_pre * pre_o[rows, :]
        mixed = mixed + w_erl * jnp.where(on, erl_o[rows, :], 0.0)
        out_ref[rows, :] = (mixed / (w_own + w_pre + w_erl)).astype(bf16)
        return carry

    lax.fori_loop(0, 4, block, 0, unroll=4)


def norm_rows(hidden, gain, shift):
    mean = jnp.mean(hidden, axis=-1, keepdims=True)
    centred = hidden - mean
    var = jnp.mean(centred * centred, axis=-1, keepdims=True)
    return centred * lax.rsqrt(var + EPS) * gain + shift


def pack_kernel(at, up_ref, down_ref, out_ref, pack_ref):
    pack_ref[0:256, :] = up_ref[...]
    pack_ref[256:384, :] = down_ref[:, 0:512]
    pack_ref[384:512, :] = down_ref[:, 512:1024]
    pack_ref[512:544, :] = out_ref[:, 0:512]
    pack_ref[544:576, :] = out_ref[:, 512:1024]


def row_kernel(scal, own_ref, far_ref, rows_ref):
    core = scal[3, 0]
    rows = pl.ds(pl.multiple_of(scal[3, 1] * 64, 64), 64)
    for y in range(4):
        own, far = own_ref[y, rows, :], far_ref[y, rows, :]
        at = 256 * y
        rows_ref[:, at : at + 128] = jnp.where(core == 0, own, far)
        rows_ref[:, at + 128 : at + 256] = jnp.where(core == 0, far, own)


def tail_kernel(
    att_ref,
    tok_ref,
    ag_ref,
    as_ref,
    mg_ref,
    ms_ref,
    w_hbm,
    out_ref,
    acc,
    left,
    right,
    up,
    down,
    sem,
):
    first = []
    for x in range(4):
        for n, half in enumerate((left, right)):
            source = w_hbm.at[x, :, pl.ds(512 + 32 * n, 32), :]
            first.append(pltpu.make_async_copy(source, half.at[:, x], sem.at[16 + 2 * x + n]))

    def fetch(t):
        return (
            pltpu.make_async_copy(w_hbm.at[:, t, pl.ds(0, 256), :], up.at[t], sem.at[2 * t]),
            pltpu.make_async_copy(w_hbm.at[:, t, pl.ds(256, 256), :], down.at[t], sem.at[2 * t + 1]),
        )

    for copy in first:
        copy.start()
    for t in range(8):
        for copy in fetch(t):
            copy.start()
    att = jnp.concatenate([att_ref[i] for i in range(8)], axis=1)
    for copy in first:
        copy.wait()
    proj = [dot(att, half[...].reshape(1024, 512)) for half in (left, right)]
    hidden = tok_ref[...].astype(f32) + jnp.concatenate(proj, axis=1)
    normed = norm_rows(hidden, ag_ref[...], as_ref[...]).astype(bf16)
    acc[...] = normed.astype(f32)

    def block(t, carry):
        up_copy, down_copy = fetch(t)
        up_copy.wait()
        h = dot(normed, up[t].reshape(1024, 512))
        inner = (0.5 * h * (1.0 + lax.erf(h * 0.7071067811865476))).astype(bf16)
        down_copy.wait()
        for n in range(2):
            weight = down[t, :, 128 * n : 128 * n + 128, :].reshape(512, 512)
            acc[:, 512 * n : 512 * n + 512] += dot(inner, weight)
        return carry

    lax.fori_loop(0, 8, block, 0, unroll=2)
    done = norm_rows(acc[...], mg_ref[...], ms_ref[...]).astype(bf16)
    for i in range(8):
        out_ref[i] = done[:, 128 * i : 128 * i + 128]


def swap_all(value, axis):
    return lax.all_to_all(value, axis, split_axis=0, concat_axis=0, tiled=True)


def cost(flops, size, trans=0):
    return pl.CostEstimate(flops=flops, bytes_accessed=size, transcendentals=trans)


def local(
    tokens,
    qkv_weight,
    out_weight,
    attn_gain,
    attn_shift,
    up_weight,
    down_weight,
    mlp_gain,
    mlp_shift,
    prefix_cache,
    earlier_cache,
    suffix_len,
    prefix_id,
    earlier_slot,
):
    n_req = lax.axis_size(REQ)
    core = lax.axis_index("c")
    rank = lax.axis_index(TP)

    place = jnp.where(jnp.arange(64) % 2 == 0, core, rank)
    scal = jnp.stack([suffix_len, prefix_id, earlier_slot, place])
    hbm = pl.BlockSpec(memory_space=pl.ANY)
    packed = pl.pallas_call(
        pack_kernel,
        grid_spec=pltpu.PrefetchScalarGridSpec(
            num_scalar_prefetch=1,
            grid=(1,),
            in_specs=[
                pl.BlockSpec((256, 512), lambda i, at: (at[0], 0)),
                pl.BlockSpec((128, 1024), lambda i, at: (at[0], 0)),
                pl.BlockSpec((32, 1024), lambda i, at: (at[0], 0)),
            ],
            out_specs=pl.BlockSpec((576, 512), lambda i, at: (0, 0)),
        ),
        out_shape=jax.ShapeDtypeStruct((576, 512), bf16),
        compiler_params=pltpu.CompilerParams(vmem_limit_bytes=61 << 20),
        cost_estimate=cost(0, 1 << 20),
        name="pack_weights",
    )(lax.axis_index("x").reshape(1), up_weight, down_weight, out_weight)
    scal, packed = lax.optimization_barrier((scal, packed))
    w_own, w_far = pl.pallas_call(
        order_kernel,
        in_specs=[SM, VM],
        out_specs=[VM, VM],
        out_shape=[jax.ShapeDtypeStruct((512, 384), bf16)] * 2,
        compiler_params=SMALL,
        cost_estimate=cost(0, 2 << 20),
        name="order_qkv_weight",
    )(scal, qkv_weight.transpose(1, 0, 2))

    own_half = swap_all(jnp.broadcast_to(tokens[None], (4, 512, 128)), "y")
    own_half, scal, w_own, w_far, packed = lax.optimization_barrier(
        (own_half, scal, w_own, w_far, packed)
    )
    shards = lax.all_gather(packed, ("x", "y", "c"), axis=0, tiled=False)
    shards = shards.reshape(4, 8, 576, 512)

    far_half = lax.ppermute(own_half, "c", [(0, 1), (1, 0)])

    part = pl.pallas_call(
        part_kernel,
        in_specs=[VM, VM],
        out_specs=VM,
        out_shape=jax.ShapeDtypeStruct((512, 384), f32),
        compiler_params=SMALL,
        cost_estimate=cost(2 * 512 * 512 * 384, 2 << 20),
        name="qkv_own_half",
    )(own_half, w_own)
    send, qkv = pl.pallas_call(
        place_kernel,
        in_specs=[SM] + [VM] * 3,
        out_specs=[VM, VM],
        out_shape=[
            jax.ShapeDtypeStruct((n_req, 32, 128), bf16),
            jax.ShapeDtypeStruct((512, 384), bf16),
        ],
        compiler_params=SMALL,
        cost_estimate=cost(2 * 512 * 512 * 384, 3 << 20),
        name="qkv_place",
    )(scal, part, far_half, w_far)

    got = swap_all(send, REQ)

    own_out, own_lse = pl.pallas_call(
        own_kernel,
        in_specs=[SM, VM],
        out_specs=[VM, VM],
        out_shape=[jax.ShapeDtypeStruct((512, 128), f32)] * 2,
        compiler_params=SMALL,
        cost_estimate=cost(2 * 512 * 128 * 128 * 4, 1 << 20, 2 * 512 * 128),
        name="own_attention",
    )(scal, qkv)

    ret = pl.pallas_call(
        owner_kernel,
        in_specs=[VM] * 5,
        out_specs=VM,
        out_shape=jax.ShapeDtypeStruct((n_req, 32, 128), bf16),
        scratch_shapes=[
            pltpu.VMEM((n_req, 128), jnp.int32),
            pltpu.SMEM((n_req, 128), jnp.int32),
            pltpu.VMEM((n_req, 128), f32),
            pltpu.SemaphoreType.DMA,
        ],
        compiler_params=SMALL,
        cost_estimate=cost(2 * 1024 * 128 * 2048, 2 << 20, 2 * 1024 * 384),
        name="owner_attention",
    )(
        got,
        prefix_cache[:, :, 0],
        prefix_cache[:, :, 1],
        earlier_cache[:, :, 0].reshape(512, 128),
        earlier_cache[:, :, 1].reshape(512, 128),
    )

    back = swap_all(ret, REQ)

    attended = pl.pallas_call(
        merge_kernel,
        in_specs=[SM, VM, VM, VM],
        out_specs=VM,
        out_shape=jax.ShapeDtypeStruct((512, 128), bf16),
        scratch_shapes=[pltpu.VMEM((512, 128), f32)] * 5,
        cost_estimate=cost(2 * 512 * 128 * 256, 1 << 20, 3 * 512 * 128),
        compiler_params=SMALL,
        name="merge",
    )(scal, back, own_out, own_lse)

    att = swap_all(attended.reshape(8, 64, 128), TP)

    tok_rows = pl.pallas_call(
        row_kernel,
        in_specs=[SM, VM, VM],
        out_specs=VM,
        out_shape=jax.ShapeDtypeStruct((64, 1024), bf16),
        compiler_params=SMALL,
        cost_estimate=cost(0, 60 << 20),
        name="token_rows",
    )(scal, own_half, far_half)

    encoded = pl.pallas_call(
        tail_kernel,
        in_specs=[VM] * 6 + [hbm],
        out_specs=VM,
        out_shape=jax.ShapeDtypeStruct((8, 64, 128), bf16),
        scratch_shapes=[
            pltpu.VMEM((64, 1024), f32),
            pltpu.VMEM((8, 4, 32, 512), bf16),
            pltpu.VMEM((8, 4, 32, 512), bf16),
            pltpu.VMEM((8, 4, 256, 512), bf16),
            pltpu.VMEM((8, 4, 256, 512), bf16),
            pltpu.SemaphoreType.DMA((24,)),
        ],
        compiler_params=pltpu.CompilerParams(vmem_limit_bytes=52 << 20),
        cost_estimate=cost(2 * 64 * 9 * 1024 * 1024, 19 << 20, 64 * 4096),
        name="project_norm_ffn",
    )(
        att,
        tok_rows,
        attn_gain.reshape(1, 1024),
        attn_shift.reshape(1, 1024),
        mlp_gain.reshape(1, 1024),
        mlp_shift.reshape(1, 1024),
        shards,
    )
    return swap_all(encoded, TP).reshape(512, 128)


def solution(mesh):
    split = Mesh(mesh.devices.reshape(16, 4, 4, 2), ("z", "x", "y", "c"))
    placed = (
        P(REQ, TP),
        P(None, None, TP),
        P(TP, None),
        P(),
        P(),
        P(None, TP),
        P(TP, None),
        P(),
        P(),
        P(REQ, None, None, TP),
        P(REQ, None, None, TP),
        P(REQ),
        P(REQ),
        P(REQ),
    )
    return jax.shard_map(
        local, mesh=split, in_specs=placed, out_specs=P(REQ, TP), check_vma=False
    )
```

```python
import jax
import jax.numpy as jnp
from jax import lax
from jax.experimental import pallas as pl
from jax.experimental.pallas import tpu as pltpu
from jax.sharding import Mesh, PartitionSpec as P

HD = 64
REQ = ("z", "x")
TP = ("y", "c")
SCALE = 0.125
NEG = -1e30
EPS = 1e-05
bf16 = jnp.bfloat16
f32 = jnp.float32

VM = pl.BlockSpec(memory_space=pltpu.VMEM)
SM = pl.BlockSpec(memory_space=pltpu.SMEM)
SMALL = pltpu.CompilerParams(vmem_limit_bytes=16 << 20)


def iota(shape, axis):
    return lax.broadcasted_iota(jnp.int32, shape, axis)


def head_mask(x, h):
    lane = iota(x.shape, len(x.shape) - 1)
    return jnp.where((lane >= HD) == (h == 1), x, jnp.zeros_like(x))


def dot_t(a, b):
    return lax.dot_general(a, b, (((1,), (1,)), ((), ())), preferred_element_type=f32)


def dot(a, b):
    return jnp.dot(a, b, preferred_element_type=f32)


def softmax_parts(scores, allowed):
    masked = scores if allowed is None else jnp.where(allowed, scores, NEG)
    top = jnp.max(masked, axis=-1, keepdims=True)
    weights = jnp.exp(masked - top)
    total = jnp.sum(weights, axis=-1, keepdims=True)
    return weights.astype(bf16), 1.0 / total, top + jnp.log(total)


def half_rows(half_ref, rows):
    return jnp.concatenate([half_ref[i, rows, :] for i in range(4)], axis=1)


def order_kernel(scal, w_ref, own_ref, far_ref):
    core = scal[3, 0]
    for side, target in ((core, own_ref), (1 - core, far_ref)):
        for y in range(4):
            rows = pl.ds(pl.multiple_of((2 * y + side) * 128, 128), 128)
            for n in range(3):
                target[128 * y : 128 * y + 128, 128 * n : 128 * n + 128] = w_ref[n, rows, :]


def part_kernel(half_ref, w_ref, part_ref):
    for b in range(2):
        rows = pl.ds(256 * b, 256)
        part_ref[rows, :] = dot(half_rows(half_ref, rows), w_ref[...])


def pair_of(scal, g):
    first, later = scal[2, 2 * g], scal[2, 2 * g + 1]
    slot = jnp.maximum(first, later)
    return scal[1, 2 * g] // 2, slot // 32, slot % 32, later >= 0, scal[0, 2 * g]


def place_kernel(scal, part_ref, half_ref, w_ref, send_ref, q_ref):
    row = iota((16, 128), 0)
    lane = iota((16, 128), 1)
    send_ref[...] = jnp.zeros(send_ref.shape, bf16)

    def block(b, carry):
        rows = pl.ds(pl.multiple_of(b * 128, 128), 128)
        out = part_ref[rows, 0:128] + dot(half_rows(half_ref, rows), w_ref[:, 0:128])
        q = out.astype(bf16)
        q_ref[rows, :] = q
        for p in range(8):
            g = b * 8 + p
            slot, slot_e, row_e, late, span = pair_of(scal, g)
            qp = q[16 * p : 16 * p + 16]
            send_ref[slot, 0:16, :] = qp
            pick = jnp.where(lane < span, scal[1, 2 * g] % 2, scal[1, 2 * g + 1] % 2)
            pick = jnp.where((row == 15) & (lane < 16), pick, 0).astype(f32)
            held = send_ref[slot, 16:32, :].astype(f32)
            send_ref[slot, 16:32, :] = (held + pick).astype(bf16)
            qf = qp.astype(f32)
            moved = jnp.where(late, pltpu.roll(qf, 15, 0), qf)
            held = send_ref[slot_e, 16:32, :].astype(f32)
            held = jnp.where(lane == 16, (row_e + 1).astype(f32), held)
            send_ref[slot_e, 16:32, :] = jnp.where(row == 15, held, moved).astype(bf16)
        return carry

    lax.fori_loop(0, 4, block, 0, unroll=4)


def own_kernel(scal, q_ref, part_ref, half_ref, w_ref, out_ref, lse_ref):
    r = iota((128, 128), 0)
    c = iota((128, 128), 1)

    def block(b, carry):
        rows = pl.ds(pl.multiple_of(b * 128, 128), 128)
        q = q_ref[rows, :]
        kv = part_ref[rows, 128:384] + dot(half_rows(half_ref, rows), w_ref[:, 128:384])
        k = kv[:, 0:128].astype(bf16)
        v = kv[:, 128:256].astype(bf16)
        span = jnp.concatenate(
            [jnp.full((16, 128), scal[0, 2 * (b * 8 + p)], jnp.int32) for p in range(8)], axis=0
        )
        same = ((r // 16) == (c // 16)) & (c <= r) & (((r % 16) < span) == ((c % 16) < span))
        res = []
        for h in range(2):
            w, inv, lse = softmax_parts(dot_t(head_mask(q, h), k) * SCALE, same)
            res.append((dot(w, v) * inv, jnp.broadcast_to(lse, (128, 128))))
        out_ref[rows, :] = head_mask(res[0][0], 0) + head_mask(res[1][0], 1)
        lse_ref[rows, :] = head_mask(res[0][1], 0) + head_mask(res[1][1], 1)
        return carry

    lax.fori_loop(0, 4, block, 0)


def stack_heads(q):
    q = q * jnp.asarray(SCALE, q.dtype)
    return jnp.concatenate([head_mask(q, 0), head_mask(q, 1)], axis=0)


def with_ones(v, h):
    lane = iota(v.shape, 1)
    return jnp.where((lane >= HD) == (h == 1), v, jnp.ones_like(v))


def finish_heads(top, first, second):
    n = first.shape[0]
    low = iota((n, 128), 1) < HD
    total = pltpu.roll(jnp.where(low, second, first), HD, 1)
    lse = jnp.where(low, top[:n], top[n:]) + jnp.log(total)
    return jnp.where(low, first, second) / total, lse


def owner_kernel(got_ref, pk_ref, pv_ref, ek_ref, ev_ref, ret_ref, row_v, row_s, stat, sem):
    sub = iota((8, 16, 128), 1)
    lane = iota((8, 16, 128), 2)
    group = lane // 16
    r = iota((256, 128), 0)
    c = iota((256, 128), 1)
    near = ((r % 128) // 16) == (c // 16)

    for b in range(8):
        line = got_ref[8 * b : 8 * b + 8, 16:32, :].astype(f32)[:, 15:16, :].reshape(8, 128)
        stat[8 * b : 8 * b + 8, :] = line
        row_v[8 * b : 8 * b + 8, :] = jnp.maximum(line - 1.0, 0.0).astype(jnp.int32)
    copy = pltpu.make_async_copy(row_v, row_s, sem)
    copy.start()

    def stat_line(lse):
        line = jnp.sum(jnp.where(lane % 16 == sub, lse.reshape(8, 16, 128), 0.0), axis=1)
        high = line.astype(bf16).astype(f32)
        return jnp.where(group[:, 0] % 2 == 1, line - high, high)

    values = [[with_ones(pv_ref[p], h) for h in range(2)] for p in range(2)]

    def prefix_part(b, carry):
        slots = pl.ds(pl.multiple_of(b * 8, 8), 8)
        q = stack_heads(got_ref[slots, 0:16, :].reshape(128, 128))
        info = jnp.broadcast_to(stat[slots, :][:, None, :], (8, 16, 128))
        pick = jnp.sum(jnp.where(lane == sub, info, 0.0), axis=-1, keepdims=True)
        pick = pick.reshape(128, 1) > 0.5
        pick = jnp.broadcast_to(pick, (128, 256))
        pick = jnp.concatenate([pick, pick], axis=0)
        s = jnp.where(pick, dot_t(q, pk_ref[1]), dot_t(q, pk_ref[0]))
        top = jnp.max(s, axis=-1, keepdims=True)
        w = jnp.exp(s - top).astype(bf16)
        none = jnp.zeros_like(w)
        w0, w1 = jnp.where(pick, none, w), jnp.where(pick, w, none)
        parts = [
            dot(w0[n : n + 128], values[0][h]) + dot(w1[n : n + 128], values[1][h])
            for h, n in enumerate((0, 128))
        ]
        out, lse = finish_heads(top, *parts)
        ret_ref[slots, 0:16, :] = out.astype(bf16).reshape(8, 16, 128)
        stat[slots, :] = stat_line(lse)
        return carry

    lax.fori_loop(0, 8, prefix_part, 0, unroll=8)
    copy.wait()

    def earlier_part(b, carry):
        slots = pl.ds(pl.multiple_of(b * 8, 8), 8)
        q = stack_heads(got_ref[slots, 16:32, :].reshape(128, 128))
        at = [pl.ds(pl.multiple_of(row_s[b * 8 + i, 16] * 16, 16), 16) for i in range(8)]
        keys = jnp.concatenate([ek_ref[x, :] for x in at], axis=0)
        rows = jnp.concatenate([ev_ref[x, :] for x in at], axis=0)
        s = jnp.where(near, dot_t(q, keys), NEG)
        top = jnp.max(s, axis=-1, keepdims=True)
        w = jnp.exp(s - top).astype(bf16)
        parts = [dot(w[n : n + 128], with_ones(rows, h)) for h, n in enumerate((0, 128))]
        out, lse = finish_heads(top, *parts)
        out = out.reshape(8, 16, 128)
        line = jnp.where(group[:, 0] % 4 < 2, stat[slots, :], stat_line(lse))
        line = jnp.broadcast_to(line[:, None, :], (8, 16, 128))
        ret_ref[slots, 16:32, :] = jnp.where(sub == 15, line, out).astype(bf16)
        return carry

    lax.fori_loop(0, 8, earlier_part, 0, unroll=8)


def merge_kernel(
    scal, ret_ref, own_ref, lse_ref, out_ref, pre_o, pre_s, erl_o, erl_s, erl_on
):
    row = iota((16, 128), 0)
    lane = iota((16, 128), 1)
    diag = (lane % 16) == row

    def block(b, carry):
        for p in range(8):
            g = b * 8 + p
            rows = pl.ds(pl.multiple_of(b * 128, 128) + 16 * p, 16)
            slot, slot_e, _, late, span = pair_of(scal, g)
            pre_o[rows, :] = ret_ref[slot, 0:16, :].astype(f32)
            line = jnp.broadcast_to(ret_ref[slot, 16:32, :].astype(f32)[15:16, :], (16, 128))
            pre_s[rows, :] = jnp.where(diag & ((lane // 32) % 2 == 0), line, 0.0)
            part = ret_ref[slot_e, 16:32, :].astype(f32)
            line = jnp.broadcast_to(part[15:16, :], (16, 128))
            stat = jnp.where(diag & ((lane // 32) % 2 == 1), line, 0.0)
            erl_o[rows, :] = jnp.where(late, pltpu.roll(part, 1, 0), part)
            erl_s[rows, :] = jnp.where(late, pltpu.roll(stat, 1, 0), stat)
            turn = jnp.where(late, 1, 0)
            erl_on[rows, :] = jnp.where((row < span).astype(jnp.int32) + turn == 1, 1.0, 0.0)
        rows = pl.ds(pl.multiple_of(b * 128, 128), 128)
        a = iota((128, 128), 0)
        c = iota((128, 128), 1)
        pick = ((a // 64) == (c // 64)).astype(bf16)
        l_pre = dot(pre_s[rows, :].astype(bf16), pick)
        l_erl = dot(erl_s[rows, :].astype(bf16), pick)
        on = erl_on[rows, :] > 0.5
        l_erl = jnp.where(on, l_erl, NEG)
        l_own = lse_ref[rows, :]
        top = jnp.maximum(jnp.maximum(l_own, l_pre), l_erl)
        w_own = jnp.exp(l_own - top)
        w_pre = jnp.exp(l_pre - top)
        w_erl = jnp.exp(l_erl - top)
        mixed = w_own * own_ref[rows, :] + w_pre * pre_o[rows, :]
        mixed = mixed + w_erl * jnp.where(on, erl_o[rows, :], 0.0)
        out_ref[rows, :] = (mixed / (w_own + w_pre + w_erl)).astype(bf16)
        return carry

    lax.fori_loop(0, 4, block, 0, unroll=4)


def norm_rows(hidden, gain, shift):
    mean = jnp.mean(hidden, axis=-1, keepdims=True)
    centred = hidden - mean
    var = jnp.mean(centred * centred, axis=-1, keepdims=True)
    return centred * lax.rsqrt(var + EPS) * gain + shift


def pack_kernel(at, up_ref, down_ref, out_ref, pack_ref):
    pack_ref[0:256, :] = up_ref[...]
    pack_ref[256:384, :] = down_ref[:, 0:512]
    pack_ref[384:512, :] = down_ref[:, 512:1024]
    pack_ref[512:544, :] = out_ref[:, 0:512]
    pack_ref[544:576, :] = out_ref[:, 512:1024]


def row_kernel(scal, own_ref, far_ref, rows_ref):
    core = scal[3, 0]
    rows = pl.ds(pl.multiple_of(scal[3, 1] * 64, 64), 64)
    for y in range(4):
        own, far = own_ref[y, rows, :], far_ref[y, rows, :]
        at = 256 * y
        rows_ref[:, at : at + 128] = jnp.where(core == 0, own, far)
        rows_ref[:, at + 128 : at + 256] = jnp.where(core == 0, far, own)


def tail_kernel(
    att_ref,
    tok_ref,
    ag_ref,
    as_ref,
    mg_ref,
    ms_ref,
    w_hbm,
    out_ref,
    acc,
    left,
    right,
    up,
    down,
    sem,
):
    first = []
    for x in range(4):
        for n, half in enumerate((left, right)):
            source = w_hbm.at[x, :, pl.ds(512 + 32 * n, 32), :]
            first.append(pltpu.make_async_copy(source, half.at[:, x], sem.at[16 + 2 * x + n]))

    def fetch(t):
        return (
            pltpu.make_async_copy(w_hbm.at[:, t, pl.ds(0, 256), :], up.at[t], sem.at[2 * t]),
            pltpu.make_async_copy(w_hbm.at[:, t, pl.ds(256, 256), :], down.at[t], sem.at[2 * t + 1]),
        )

    for copy in first:
        copy.start()
    for t in range(8):
        for copy in fetch(t):
            copy.start()
    att = jnp.concatenate([att_ref[i] for i in range(8)], axis=1)
    for copy in first:
        copy.wait()
    proj = [dot(att, half[...].reshape(1024, 512)) for half in (left, right)]
    hidden = tok_ref[...].astype(f32) + jnp.concatenate(proj, axis=1)
    normed = norm_rows(hidden, ag_ref[...], as_ref[...]).astype(bf16)
    acc[...] = normed.astype(f32)

    def block(t, carry):
        up_copy, down_copy = fetch(t)
        up_copy.wait()
        h = dot(normed, up[t].reshape(1024, 512))
        inner = (0.5 * h * (1.0 + lax.erf(h * 0.7071067811865476))).astype(bf16)
        down_copy.wait()
        for n in range(2):
            weight = down[t, :, 128 * n : 128 * n + 128, :].reshape(512, 512)
            acc[:, 512 * n : 512 * n + 512] += dot(inner, weight)
        return carry

    lax.fori_loop(0, 8, block, 0, unroll=2)
    done = norm_rows(acc[...], mg_ref[...], ms_ref[...]).astype(bf16)
    for i in range(8):
        out_ref[i] = done[:, 128 * i : 128 * i + 128]


def swap_all(value, axis):
    return lax.all_to_all(value, axis, split_axis=0, concat_axis=0, tiled=True)


def cost(flops, size, trans=0):
    return pl.CostEstimate(flops=flops, bytes_accessed=size, transcendentals=trans)


def local(
    tokens,
    qkv_weight,
    out_weight,
    attn_gain,
    attn_shift,
    up_weight,
    down_weight,
    mlp_gain,
    mlp_shift,
    prefix_cache,
    earlier_cache,
    suffix_len,
    prefix_id,
    earlier_slot,
):
    n_req = lax.axis_size(REQ)
    core = lax.axis_index("c")
    rank = lax.axis_index(TP)

    place = jnp.where(jnp.arange(64) % 2 == 0, core, rank)
    scal = jnp.stack([suffix_len, prefix_id, earlier_slot, place])
    hbm = pl.BlockSpec(memory_space=pl.ANY)
    packed = pl.pallas_call(
        pack_kernel,
        grid_spec=pltpu.PrefetchScalarGridSpec(
            num_scalar_prefetch=1,
            grid=(1,),
            in_specs=[
                pl.BlockSpec((256, 512), lambda i, at: (at[0], 0)),
                pl.BlockSpec((128, 1024), lambda i, at: (at[0], 0)),
                pl.BlockSpec((32, 1024), lambda i, at: (at[0], 0)),
            ],
            out_specs=pl.BlockSpec((576, 512), lambda i, at: (0, 0)),
        ),
        out_shape=jax.ShapeDtypeStruct((576, 512), bf16),
        compiler_params=pltpu.CompilerParams(vmem_limit_bytes=61 << 20),
        cost_estimate=cost(0, 1 << 20),
        name="pack_weights",
    )(lax.axis_index("x").reshape(1), up_weight, down_weight, out_weight)
    scal, packed = lax.optimization_barrier((scal, packed))
    w_own, w_far = pl.pallas_call(
        order_kernel,
        in_specs=[SM, VM],
        out_specs=[VM, VM],
        out_shape=[jax.ShapeDtypeStruct((512, 384), bf16)] * 2,
        compiler_params=SMALL,
        cost_estimate=cost(0, 2 << 20),
        name="order_qkv_weight",
    )(scal, qkv_weight.transpose(1, 0, 2))

    own_half = swap_all(jnp.broadcast_to(tokens[None], (4, 512, 128)), "y")
    own_half, scal, w_own, w_far, packed = lax.optimization_barrier(
        (own_half, scal, w_own, w_far, packed)
    )
    shards = lax.all_gather(packed, ("x", "y", "c"), axis=0, tiled=False)
    shards = shards.reshape(4, 8, 576, 512)

    far_half = lax.ppermute(own_half, "c", [(0, 1), (1, 0)])

    part = pl.pallas_call(
        part_kernel,
        in_specs=[VM, VM],
        out_specs=VM,
        out_shape=jax.ShapeDtypeStruct((512, 384), f32),
        compiler_params=SMALL,
        cost_estimate=cost(2 * 512 * 512 * 384, 2 << 20),
        name="qkv_own_half",
    )(own_half, w_own)
    send, q = pl.pallas_call(
        place_kernel,
        in_specs=[SM] + [VM] * 3,
        out_specs=[VM, VM],
        out_shape=[
            jax.ShapeDtypeStruct((n_req, 32, 128), bf16),
            jax.ShapeDtypeStruct((512, 128), bf16),
        ],
        compiler_params=SMALL,
        cost_estimate=cost(2 * 512 * 512 * 384, 3 << 20),
        name="qkv_place",
    )(scal, part, far_half, w_far)

    got = swap_all(send, REQ)

    own_out, own_lse = pl.pallas_call(
        own_kernel,
        in_specs=[SM, VM, VM, VM, VM],
        out_specs=[VM, VM],
        out_shape=[jax.ShapeDtypeStruct((512, 128), f32)] * 2,
        compiler_params=SMALL,
        cost_estimate=cost(2 * 512 * 128 * 128 * 4, 1 << 20, 2 * 512 * 128),
        name="own_attention",
    )(scal, q, part, far_half, w_far)

    ret = pl.pallas_call(
        owner_kernel,
        in_specs=[VM] * 5,
        out_specs=VM,
        out_shape=jax.ShapeDtypeStruct((n_req, 32, 128), bf16),
        scratch_shapes=[
            pltpu.VMEM((n_req, 128), jnp.int32),
            pltpu.SMEM((n_req, 128), jnp.int32),
            pltpu.VMEM((n_req, 128), f32),
            pltpu.SemaphoreType.DMA,
        ],
        compiler_params=SMALL,
        cost_estimate=cost(2 * 1024 * 128 * 2048, 2 << 20, 2 * 1024 * 384),
        name="owner_attention",
    )(
        got,
        prefix_cache[:, :, 0],
        prefix_cache[:, :, 1],
        earlier_cache[:, :, 0].reshape(512, 128),
        earlier_cache[:, :, 1].reshape(512, 128),
    )

    back = swap_all(ret, REQ)

    attended = pl.pallas_call(
        merge_kernel,
        in_specs=[SM, VM, VM, VM],
        out_specs=VM,
        out_shape=jax.ShapeDtypeStruct((512, 128), bf16),
        scratch_shapes=[pltpu.VMEM((512, 128), f32)] * 5,
        cost_estimate=cost(2 * 512 * 128 * 256, 1 << 20, 3 * 512 * 128),
        compiler_params=SMALL,
        name="merge",
    )(scal, back, own_out, own_lse)

    att = swap_all(attended.reshape(8, 64, 128), TP)

    tok_rows = pl.pallas_call(
        row_kernel,
        in_specs=[SM, VM, VM],
        out_specs=VM,
        out_shape=jax.ShapeDtypeStruct((64, 1024), bf16),
        compiler_params=SMALL,
        cost_estimate=cost(0, 60 << 20),
        name="token_rows",
    )(scal, own_half, far_half)

    encoded = pl.pallas_call(
        tail_kernel,
        in_specs=[VM] * 6 + [hbm],
        out_specs=VM,
        out_shape=jax.ShapeDtypeStruct((8, 64, 128), bf16),
        scratch_shapes=[
            pltpu.VMEM((64, 1024), f32),
            pltpu.VMEM((8, 4, 32, 512), bf16),
            pltpu.VMEM((8, 4, 32, 512), bf16),
            pltpu.VMEM((8, 4, 256, 512), bf16),
            pltpu.VMEM((8, 4, 256, 512), bf16),
            pltpu.SemaphoreType.DMA((24,)),
        ],
        compiler_params=pltpu.CompilerParams(vmem_limit_bytes=52 << 20),
        cost_estimate=cost(2 * 64 * 9 * 1024 * 1024, 19 << 20, 64 * 4096),
        name="project_norm_ffn",
    )(
        att,
        tok_rows,
        attn_gain.reshape(1, 1024),
        attn_shift.reshape(1, 1024),
        mlp_gain.reshape(1, 1024),
        mlp_shift.reshape(1, 1024),
        shards,
    )
    return swap_all(encoded, TP).reshape(512, 128)


def solution(mesh):
    split = Mesh(mesh.devices.reshape(16, 4, 4, 2), ("z", "x", "y", "c"))
    placed = (
        P(REQ, TP),
        P(None, None, TP),
        P(TP, None),
        P(),
        P(),
        P(None, TP),
        P(TP, None),
        P(),
        P(),
        P(REQ, None, None, TP),
        P(REQ, None, None, TP),
        P(REQ),
        P(REQ),
        P(REQ),
    )
    return jax.shard_map(
        local, mesh=split, in_specs=placed, out_specs=P(REQ, TP), check_vma=False
    )
```
